256 devices in a mesh: dp: 8 (over y, core), cls: 32 (over z, x).
Axes of the slice: x: 4, y: 4, z: 8, core: 2. Of those that a mesh axis runs over, the one named last changes fastest.
Arguments:
- embeddings: bfloat16 [262144, 512], P(('dp', 'cls'))
- proxies: bfloat16 [98304, 512], P('cls')
- hard_tiles: int32 [2048, 8], P(('dp', 'cls')), may hold values from 0 to 767, as said below
- tile_count: int32 [2048], P(('dp', 'cls')), may hold values from 5 to 8
- labels: int32 [262144], P(('dp', 'cls')), may hold values from 0 to 98303, as said below
Outputs:
- row_loss: float32 [262144], P(('dp', 'cls'))
- embed_grad: bfloat16 [262144, 512], P(('dp', 'cls'))
- proxy_grad: float32 [98304, 512], P('cls', 'dp')
The draws below stay inside these ranges and needn't reach their ends.
Inputs may be any that keep to these rules, and one draw needn't show every extreme that they name: `hard_tiles`: tile t is stored on class shard t // 24. Among the 8 x 8 list entries of one device's blocks (all entries, used or not), every one of the class shards is named exactly 2 times; the entries of one block name different tiles. Only the first tile_count entries of a block's list are used. `labels`: A row's positive class lies in the first tile of its block's list.
All inputs are finite; a program needn't handle non-finite values.
Results may differ from the reference program's by a relative error of at most 0.0098.
Values may be sent and summed in bfloat16 or wider, within the bound.
A program may use at most 128 MiB of HBM per device.

```python
import jax
import jax.numpy as jnp
import numpy as np
from jax import lax

D = 512
TILE = 128
BR = 128
K = 8
K_MIN = 5
BLK_DEV = 8
TILE_DEV = 24
CAP = 2
BLOCKS = 2048
ROWS = 262144
CLASSES = 98304
N_CLS = 32


def request_plan(key):
    devices_all = BLOCKS // BLK_DEV
    pair_count = BLK_DEV * K
    subkeys = jax.random.split(jax.random.fold_in(key, 101), 4)
    counter = jnp.arange(pair_count, dtype=jnp.int32)
    owner_of = counter // CAP
    noise_bits = jax.random.randint(subkeys[0], (devices_all, pair_count), 0, 1 << 20)
    chosen = jax.random.randint(subkeys[1], (devices_all, 1), 0, N_CLS)
    scores = noise_bits * pair_count + counter[None, :]
    scores = jnp.where(owner_of[None, :] == chosen, scores - (1 << 30), scores)
    ranking = jnp.argsort(scores, axis=1, stable=True).astype(jnp.int32)
    static_index = np.arange(pair_count)
    position_key = np.where(static_index % K < K_MIN, 0, 1) * pair_count + static_index
    positions = np.argsort(position_key, kind='stable')
    placed = jnp.zeros((devices_all, pair_count), jnp.int32).at[:, positions].set(ranking)
    owner_at = placed // CAP
    copy_at = placed % CAP
    base_tile = jax.random.randint(subkeys[2], (devices_all, BLK_DEV * N_CLS), 0, TILE_DEV)
    block_at = counter // K
    base_at = jnp.take_along_axis(base_tile, block_at[None, :] * N_CLS + owner_at, axis=1)
    tile_ids = owner_at * TILE_DEV + (base_at + copy_at) % TILE_DEV
    hard_list = tile_ids.reshape(BLOCKS, K).astype(jnp.int32)
    offsets = jax.random.randint(subkeys[3], (BLOCKS, BR), 0, TILE)
    labels = (hard_list[:, 0:1] * TILE + offsets).reshape(ROWS).astype(jnp.int32)
    return (hard_list, labels)


def proxy_table(key):
    proxy_rows = jax.random.normal(jax.random.fold_in(key, 202), (CLASSES, D), jnp.float32) * 0.5
    return proxy_rows


def draw_hard_tiles(key, part):
    hard_list, labels = request_plan(key)
    return hard_list


def draw_labels(key, part):
    hard_list, labels = request_plan(key)
    return labels


def draw_proxies(key, part):
    return proxy_table(key).astype(jnp.bfloat16)


def draw_embeddings(key, part):
    noise_rows = jax.random.normal(jax.random.fold_in(key, 204), (ROWS, D), jnp.float32)
    result = noise_rows
    return result.astype(jnp.bfloat16)


def set_ends(values, key, smallest, largest):
    place = [jax.random.randint(jax.random.fold_in(key, axis), (), 0, length) for axis, length in enumerate(values.shape)]
    main_axis = values.shape.index(max(values.shape))
    beside = place[:main_axis] + [(place[main_axis] + 1) % values.shape[main_axis]] + place[main_axis + 1:]
    return values.at[tuple(place)].set(smallest).at[tuple(beside)].set(largest)


def setup_inputs(seed: int = 0) -> dict:
    seeds = jax.random.split(jax.random.key(seed), 6)
    return {
        "embeddings": draw_embeddings(jax.random.fold_in(seeds[5], 71), 0),
        "proxies": draw_proxies(jax.random.fold_in(seeds[5], 71), 0),
        "hard_tiles": draw_hard_tiles(jax.random.fold_in(seeds[5], 71), 0),
        "tile_count": set_ends(jax.random.randint(seeds[3], (BLOCKS,), K_MIN, K + 1), jax.random.fold_in(seeds[3], 1), K_MIN, K).astype(jnp.int32),
        "labels": draw_labels(jax.random.fold_in(seeds[5], 71), 0),
    }


logit_scale = 4.0
epsilon = 1e-06

def reference(embeddings, proxies, hard_tiles, tile_count, labels):
    emb_exact = embeddings.astype(jnp.float32)
    inverse_norm = lax.rsqrt(lax.optimization_barrier(jnp.sum(emb_exact * emb_exact, axis=1, keepdims=True)) + epsilon)
    unit_exact = emb_exact * inverse_norm
    unit_rows = unit_exact.astype(jnp.bfloat16)
    tile_table = proxies.reshape(-1, TILE, D)
    columns = jnp.arange(TILE, dtype=jnp.int32)
    entries = jnp.arange(K, dtype=jnp.int32)

    def per_block(accumulated, inputs):
        unit_block, exact_block, norm_block, tile_list, count_one, label_block = inputs
        candidates = tile_table[tile_list].astype(jnp.float32)
        unit_wide = unit_block.astype(jnp.float32)
        logits = logit_scale * jnp.einsum('rd,kcd->rkc', unit_wide, candidates)
        valid_entry = (entries < count_one)[None, :, None]
        masked = jnp.where(valid_entry, logits, -1e+30)
        peak_row = lax.optimization_barrier(jnp.max(masked, axis=(1, 2)))
        total_row = lax.optimization_barrier(jnp.sum(jnp.exp(masked - peak_row[:, None, None]), axis=(1, 2)))
        log_total = peak_row + jnp.log(total_row)
        position = label_block - tile_list[0] * TILE
        positive_hit = ((entries == 0)[None, :, None] & (columns[None, None, :] == position[:, None, None])).astype(jnp.float32)
        positive = lax.optimization_barrier(jnp.sum(logits * positive_hit, axis=(1, 2)))
        probabilities = jnp.exp(masked - log_total[:, None, None])
        dscore = (logit_scale * (probabilities - positive_hit)).astype(jnp.bfloat16)
        dscore = lax.optimization_barrier(dscore)
        score_wide = dscore.astype(jnp.float32)
        tile_terms = jnp.einsum('rkc,kcd->rkd', score_wide, candidates).astype(jnp.bfloat16)
        tile_terms = lax.optimization_barrier(tile_terms)
        grad_unit = lax.optimization_barrier(jnp.sum(tile_terms.astype(jnp.float32), axis=1))
        radial = lax.optimization_barrier(jnp.sum(exact_block * grad_unit, axis=1, keepdims=True))
        grad_rows = ((grad_unit - exact_block * radial) * norm_block).astype(jnp.bfloat16)
        tile_grads = jnp.einsum('rkc,rd->kcd', score_wide, unit_wide)
        accumulated = accumulated.at[tile_list].add(tile_grads)
        return (accumulated, (log_total - positive, grad_rows))
    zero_grads = jnp.zeros((tile_table.shape[0], TILE, D), jnp.float32)
    inputs = (unit_rows.reshape(-1, BR, D), unit_exact.reshape(-1, BR, D), inverse_norm.reshape(-1, BR, 1), hard_tiles, tile_count, labels.reshape(-1, BR))
    accumulated, outputs = lax.scan(per_block, zero_grads, inputs)
    losses, row_grads = outputs
    return (losses.reshape(-1), row_grads.reshape(-1, D), accumulated.reshape(-1, D))
```

```python
import jax
import jax.numpy as jnp
from jax import lax
from jax.sharding import PartitionSpec as P

D = 512
TILE = 128
BR = 128
K = 8


logit_scale = 4.0
epsilon = 1e-06


def per_device(embeddings, proxies, hard_tiles, tile_count, labels):
    blocks = hard_tiles.shape[0]
    pair_count = blocks * K
    groups = lax.axis_size("cls")
    capacity = pair_count // groups
    tile_dev = proxies.shape[0] // TILE
    flat_tiles = hard_tiles.reshape(pair_count)
    owners = flat_tiles // tile_dev
    local_ids = flat_tiles % tile_dev
    counter = jnp.arange(pair_count, dtype=jnp.int32)
    same_owner = owners[:, None] == owners[None, :]
    earlier = counter[None, :] < counter[:, None]
    rank_order = jnp.sum(jnp.where(same_owner & earlier, 1, 0), axis=1).astype(jnp.int32)
    slot_of = owners * capacity + rank_order
    holder = jnp.sum(jnp.where(slot_of[None, :] == counter[:, None], counter[None, :], 0), axis=1)
    request_ids = local_ids[holder].reshape(groups, capacity)
    emb_exact = embeddings.astype(jnp.float32)
    inverse_norm = lax.rsqrt(jnp.sum(emb_exact * emb_exact, axis=1, keepdims=True) + epsilon)
    unit_exact = emb_exact * inverse_norm
    unit_rows = unit_exact.astype(jnp.bfloat16)
    unit_blocks = unit_rows.reshape(blocks, BR, D)
    entries = jnp.arange(K, dtype=jnp.int32)
    columns = jnp.arange(TILE, dtype=jnp.int32)
    valid_entry = entries[None, :] < tile_count[:, None]
    pos_cols = labels.reshape(blocks, BR) - hard_tiles[:, 0:1] * TILE
    tile_table = proxies.reshape(tile_dev, TILE, D)
    wanted = lax.all_to_all(request_ids, "cls", split_axis=0, concat_axis=0, tiled=True)
    outgoing = tile_table[wanted]
    fetched = lax.all_to_all(outgoing, "cls", split_axis=0, concat_axis=0, tiled=True)
    candidates = fetched.reshape(pair_count, TILE, D)[slot_of].reshape(blocks, K, TILE, D)
    logits = logit_scale * jnp.einsum(
        "brd,bkcd->brkc", unit_blocks, candidates, preferred_element_type=jnp.float32
    )
    masked = jnp.where(valid_entry[:, None, :, None], logits, -1e30)
    peak_row = jnp.max(masked, axis=(2, 3))
    total_row = jnp.sum(jnp.exp(masked - peak_row[:, :, None, None]), axis=(2, 3))
    log_total = peak_row + jnp.log(total_row)
    positive_hit = (
        (entries == 0)[None, None, :, None]
        & (columns[None, None, None, :] == pos_cols[:, :, None, None])
    ).astype(jnp.float32)
    positive = jnp.sum(logits * positive_hit, axis=(2, 3))
    probabilities = jnp.exp(masked - log_total[:, :, None, None])
    dscore = (logit_scale * (probabilities - positive_hit)).astype(jnp.bfloat16)
    tile_terms = jnp.einsum(
        "brkc,bkcd->brkd", dscore, candidates, preferred_element_type=jnp.float32
    ).astype(jnp.bfloat16)
    tile_terms = lax.optimization_barrier(tile_terms)
    grad_unit = jnp.sum(tile_terms.astype(jnp.float32), axis=2)
    pair_grads = jnp.einsum(
        "brkc,brd->bkcd", dscore, unit_blocks, preferred_element_type=jnp.float32
    ).astype(jnp.bfloat16)
    pair_grads = pair_grads.reshape(pair_count, TILE, D)[holder].reshape(groups, capacity, TILE, D)
    returned = lax.all_to_all(pair_grads, "cls", split_axis=0, concat_axis=0, tiled=True)
    got_ids = wanted.reshape(pair_count)
    got_terms = returned.reshape(pair_count, TILE * D)
    row_loss = (log_total - positive).reshape(-1)
    grad_flat = grad_unit.reshape(-1, D)
    radial = jnp.sum(unit_exact * grad_flat, axis=1, keepdims=True)
    embed_grad = ((grad_flat - unit_exact * radial) * inverse_norm).astype(jnp.bfloat16)
    select_rows = (jnp.arange(tile_dev, dtype=jnp.int32)[:, None] == got_ids[None, :]).astype(
        jnp.bfloat16
    )
    owned = jnp.dot(select_rows, got_terms, preferred_element_type=jnp.float32)
    owned = owned.reshape(tile_dev * TILE, D)
    proxy_share = lax.psum_scatter(owned, "dp", scatter_dimension=1, tiled=True)
    return (row_loss, embed_grad, proxy_share)


def solution(mesh):
    placed = (
        P(("dp", "cls"), None),
        P("cls", None),
        P(("dp", "cls"), None),
        P(("dp", "cls")),
        P(("dp", "cls")),
    )
    return jax.shard_map(
        per_device,
        mesh=mesh,
        in_specs=placed,
        out_specs=(P(("dp", "cls")), P(("dp", "cls"), None), P("cls", "dp")),
        check_vma=False,
    )
```

```python
import functools

import jax
import jax.numpy as jnp
from jax import lax
from jax.experimental import pallas as pl
from jax.experimental.pallas import tpu as pltpu
from jax.sharding import PartitionSpec as P

D = 512
TILE = 128
BR = 128
K = 8


MESH = pl.DeviceIdType.MESH


def _a2a_kernel(n, src_ref, out_ref, send_sem, recv_sem, local_sem):
    me = lax.axis_index("cls")
    row = lax.axis_index("dp")
    barrier = pltpu.get_barrier_semaphore()

    def greet(j, carry):
        peer = lax.rem(me + j, n)
        pl.semaphore_signal(barrier, inc=1, device_id=(row, peer), device_id_type=MESH)
        return carry

    lax.fori_loop(1, n, greet, 0)
    pl.semaphore_wait(barrier, n - 1)
    local = pltpu.make_async_copy(src_ref.at[me], out_ref.at[me], local_sem)
    local.start()

    def remote(j):
        peer = lax.rem(me + j, n)
        return pltpu.make_async_remote_copy(
            src_ref=src_ref.at[peer],
            dst_ref=out_ref.at[me],
            send_sem=send_sem.at[j],
            recv_sem=recv_sem.at[j],
            device_id=(row, peer),
            device_id_type=MESH,
        )

    def launch(j, carry):
        remote(j).start()
        return carry

    def finish(j, carry):
        remote(j).wait()
        return carry

    lax.fori_loop(1, n, launch, 0)
    lax.fori_loop(1, n, finish, 0)
    local.wait()


def cls_all_to_all(x, cid):
    n = x.shape[0]
    return pl.pallas_call(
        functools.partial(_a2a_kernel, n),
        out_shape=jax.ShapeDtypeStruct(x.shape, x.dtype),
        in_specs=[pl.BlockSpec(memory_space=pl.ANY)],
        out_specs=pl.BlockSpec(memory_space=pl.ANY),
        scratch_shapes=[
            pltpu.SemaphoreType.DMA((n,)),
            pltpu.SemaphoreType.DMA((n,)),
            pltpu.SemaphoreType.DMA,
        ],
        compiler_params=pltpu.CompilerParams(collective_id=cid, has_side_effects=True),
    )(x)


logit_scale = 4.0
epsilon = 1e-06


def per_device(embeddings, proxies, hard_tiles, tile_count, labels):
    blocks = hard_tiles.shape[0]
    pair_count = blocks * K
    groups = lax.axis_size("cls")
    capacity = pair_count // groups
    tile_dev = proxies.shape[0] // TILE
    flat_tiles = hard_tiles.reshape(pair_count)
    owners = flat_tiles // tile_dev
    local_ids = flat_tiles % tile_dev
    counter = jnp.arange(pair_count, dtype=jnp.int32)
    same_owner = owners[:, None] == owners[None, :]
    earlier = counter[None, :] < counter[:, None]
    rank_order = jnp.sum(jnp.where(same_owner & earlier, 1, 0), axis=1).astype(jnp.int32)
    slot_of = owners * capacity + rank_order
    holder = jnp.sum(jnp.where(slot_of[None, :] == counter[:, None], counter[None, :], 0), axis=1)
    request_ids = local_ids[holder].reshape(groups, capacity)
    emb_exact = embeddings.astype(jnp.float32)
    inverse_norm = lax.rsqrt(jnp.sum(emb_exact * emb_exact, axis=1, keepdims=True) + epsilon)
    unit_exact = emb_exact * inverse_norm
    unit_rows = unit_exact.astype(jnp.bfloat16)
    unit_blocks = unit_rows.reshape(blocks, BR, D)
    entries = jnp.arange(K, dtype=jnp.int32)
    columns = jnp.arange(TILE, dtype=jnp.int32)
    valid_entry = entries[None, :] < tile_count[:, None]
    pos_cols = labels.reshape(blocks, BR) - hard_tiles[:, 0:1] * TILE
    tile_table = proxies.reshape(tile_dev, TILE, D)
    wanted = cls_all_to_all(request_ids, 0)
    outgoing = tile_table[wanted]
    fetched = cls_all_to_all(outgoing, 1)
    candidates = fetched.reshape(pair_count, TILE, D)[slot_of].reshape(blocks, K, TILE, D)
    logits = logit_scale * jnp.einsum(
        "brd,bkcd->brkc", unit_blocks, candidates, preferred_element_type=jnp.float32
    )
    masked = jnp.where(valid_entry[:, None, :, None], logits, -1e30)
    peak_row = jnp.max(masked, axis=(2, 3))
    total_row = jnp.sum(jnp.exp(masked - peak_row[:, :, None, None]), axis=(2, 3))
    log_total = peak_row + jnp.log(total_row)
    positive_hit = (
        (entries == 0)[None, None, :, None]
        & (columns[None, None, None, :] == pos_cols[:, :, None, None])
    ).astype(jnp.float32)
    positive = jnp.sum(logits * positive_hit, axis=(2, 3))
    probabilities = jnp.exp(masked - log_total[:, :, None, None])
    dscore = (logit_scale * (probabilities - positive_hit)).astype(jnp.bfloat16)
    tile_terms = jnp.einsum(
        "brkc,bkcd->brkd", dscore, candidates, preferred_element_type=jnp.float32
    ).astype(jnp.bfloat16)
    tile_terms = lax.optimization_barrier(tile_terms)
    grad_unit = jnp.sum(tile_terms.astype(jnp.float32), axis=2)
    pair_grads = jnp.einsum(
        "brkc,brd->bkcd", dscore, unit_blocks, preferred_element_type=jnp.float32
    ).astype(jnp.bfloat16)
    pair_grads = pair_grads.reshape(pair_count, TILE, D)[holder].reshape(groups, capacity, TILE, D)
    returned = cls_all_to_all(pair_grads, 2)
    got_ids = wanted.reshape(pair_count)
    got_terms = returned.reshape(pair_count, TILE * D)
    row_loss = (log_total - positive).reshape(-1)
    grad_flat = grad_unit.reshape(-1, D)
    radial = jnp.sum(unit_exact * grad_flat, axis=1, keepdims=True)
    embed_grad = ((grad_flat - unit_exact * radial) * inverse_norm).astype(jnp.bfloat16)
    select_rows = (jnp.arange(tile_dev, dtype=jnp.int32)[:, None] == got_ids[None, :]).astype(
        jnp.bfloat16
    )
    owned = jnp.dot(select_rows, got_terms, preferred_element_type=jnp.float32)
    owned = owned.reshape(tile_dev * TILE, D)
    proxy_share = lax.psum_scatter(owned, "dp", scatter_dimension=1, tiled=True)
    return (row_loss, embed_grad, proxy_share)


def solution(mesh):
    placed = (
        P(("dp", "cls"), None),
        P("cls", None),
        P(("dp", "cls"), None),
        P(("dp", "cls")),
        P(("dp", "cls")),
    )
    return jax.shard_map(
        per_device,
        mesh=mesh,
        in_specs=placed,
        out_specs=(P(("dp", "cls")), P(("dp", "cls"), None), P("cls", "dp")),
        check_vma=False,
    )
```

```python
import functools

import jax
import jax.numpy as jnp
from jax import lax
from jax.experimental import pallas as pl
from jax.experimental.pallas import tpu as pltpu
from jax.sharding import PartitionSpec as P

D = 512
TILE = 128
BR = 128
K = 8


MESH = pl.DeviceIdType.MESH


def _a2a_kernel(n, src_ref, out_ref, send_sem, recv_sem, local_sem):
    me = lax.axis_index("cls")
    row = lax.axis_index("dp")
    barrier = pltpu.get_barrier_semaphore()

    def greet(j, carry):
        peer = lax.rem(me + j, n)
        pl.semaphore_signal(barrier, inc=1, device_id=(row, peer), device_id_type=MESH)
        return carry

    lax.fori_loop(1, n, greet, 0)
    pl.semaphore_wait(barrier, n - 1)
    local = pltpu.make_async_copy(src_ref.at[me], out_ref.at[me], local_sem)
    local.start()

    def remote(j):
        peer = lax.rem(me + j, n)
        return pltpu.make_async_remote_copy(
            src_ref=src_ref.at[peer],
            dst_ref=out_ref.at[me],
            send_sem=send_sem.at[j],
            recv_sem=recv_sem.at[j],
            device_id=(row, peer),
            device_id_type=MESH,
        )

    def launch(j, carry):
        remote(j).start()
        return carry

    def finish(j, carry):
        remote(j).wait()
        return carry

    lax.fori_loop(1, n, launch, 0)
    lax.fori_loop(1, n, finish, 0)
    local.wait()


def cls_all_to_all(x, cid):
    n = x.shape[0]
    return pl.pallas_call(
        functools.partial(_a2a_kernel, n),
        out_shape=jax.ShapeDtypeStruct(x.shape, x.dtype),
        in_specs=[pl.BlockSpec(memory_space=pl.ANY)],
        out_specs=pl.BlockSpec(memory_space=pl.ANY),
        scratch_shapes=[
            pltpu.SemaphoreType.DMA((n,)),
            pltpu.SemaphoreType.DMA((n,)),
            pltpu.SemaphoreType.DMA,
        ],
        compiler_params=pltpu.CompilerParams(collective_id=cid, has_side_effects=True),
    )(x)


logit_scale = 4.0
epsilon = 1e-06


def _block_kernel(slot_ref, count_ref, emb_ref, pos_ref, *rest):
    tiles = rest[:K]
    loss_ref, grad_ref, pair_hbm, pair_buf, pair_sem = rest[K:]
    b = pl.program_id(0)
    emb = emb_ref[0].astype(jnp.float32)
    inverse_norm = lax.rsqrt(jnp.sum(emb * emb, axis=1, keepdims=True) + epsilon)
    unit_exact = emb * inverse_norm
    unit_rows = unit_exact.astype(jnp.bfloat16)
    count = count_ref[b]
    columns = lax.broadcasted_iota(jnp.int32, (BR, TILE), 1)
    hit = columns == pos_ref[0]
    logits = []
    for k in range(K):
        cand = tiles[k][0]
        lg = logit_scale * lax.dot_general(
            unit_rows, cand, (((1,), (1,)), ((), ())), preferred_element_type=jnp.float32
        )
        logits.append(lg)
    masked = [jnp.where(k < count, logits[k], -1e30) for k in range(K)]
    peak = masked[0].max(axis=1, keepdims=True)
    for k in range(1, K):
        peak = jnp.maximum(peak, masked[k].max(axis=1, keepdims=True))
    total = jnp.zeros_like(peak)
    for k in range(K):
        total = total + jnp.sum(jnp.exp(masked[k] - peak), axis=1, keepdims=True)
    log_total = peak + jnp.log(total)
    positive = jnp.sum(jnp.where(hit, logits[0], 0.0), axis=1, keepdims=True)
    loss_ref[0] = log_total - positive
    grad_unit = jnp.zeros((BR, D), jnp.float32)
    for k in range(K):
        probabilities = jnp.exp(masked[k] - log_total)
        if k == 0:
            probabilities = probabilities - jnp.where(hit, 1.0, 0.0)
        dscore = (logit_scale * probabilities).astype(jnp.bfloat16)
        cand = tiles[k][0]
        terms = jnp.dot(dscore, cand, preferred_element_type=jnp.float32)
        grad_unit = grad_unit + terms.astype(jnp.bfloat16).astype(jnp.float32)
        pair_buf[k] = lax.dot_general(
            dscore, unit_rows, (((0,), (0,)), ((), ())), preferred_element_type=jnp.float32
        ).astype(jnp.bfloat16)
    copies = []
    for k in range(K):
        cp = pltpu.make_async_copy(pair_buf.at[k], pair_hbm.at[slot_ref[b * K + k]], pair_sem.at[k])
        cp.start()
        copies.append(cp)
    radial = jnp.sum(unit_exact * grad_unit, axis=1, keepdims=True)
    grad_ref[0] = ((grad_unit - unit_exact * radial) * inverse_norm).astype(grad_ref.dtype)
    for cp in copies:
        cp.wait()


def block_step(slot_of, tile_count, emb_blocks, pos_cols, fetched):
    blocks = emb_blocks.shape[0]
    pairs = fetched.shape[0]

    def tile_spec(k):
        return pl.BlockSpec((1, TILE, D), lambda b, slot, cnt: (slot[b * K + k], 0, 0))

    grid_spec = pltpu.PrefetchScalarGridSpec(
        num_scalar_prefetch=2,
        grid=(blocks,),
        in_specs=[
            pl.BlockSpec((1, BR, D), lambda b, slot, cnt: (b, 0, 0)),
            pl.BlockSpec((1, BR, 1), lambda b, slot, cnt: (b, 0, 0)),
        ]
        + [tile_spec(k) for k in range(K)],
        out_specs=[
            pl.BlockSpec((1, BR, 1), lambda b, slot, cnt: (b, 0, 0)),
            pl.BlockSpec((1, BR, D), lambda b, slot, cnt: (b, 0, 0)),
            pl.BlockSpec(memory_space=pl.ANY),
        ],
        scratch_shapes=[
            pltpu.VMEM((K, TILE, D), jnp.bfloat16),
            pltpu.SemaphoreType.DMA((K,)),
        ],
    )
    return pl.pallas_call(
        _block_kernel,
        grid_spec=grid_spec,
        out_shape=[
            jax.ShapeDtypeStruct((blocks, BR, 1), jnp.float32),
            jax.ShapeDtypeStruct((blocks, BR, D), jnp.bfloat16),
            jax.ShapeDtypeStruct((pairs, TILE, D), jnp.bfloat16),
        ],
        compiler_params=pltpu.CompilerParams(vmem_limit_bytes=48 * 1024 * 1024),
    )(slot_of, tile_count, emb_blocks, pos_cols, *([fetched] * K))


def per_device(embeddings, proxies, hard_tiles, tile_count, labels):
    blocks = hard_tiles.shape[0]
    pair_count = blocks * K
    groups = lax.axis_size("cls")
    capacity = pair_count // groups
    tile_dev = proxies.shape[0] // TILE
    flat_tiles = hard_tiles.reshape(pair_count)
    owners = flat_tiles // tile_dev
    local_ids = flat_tiles % tile_dev
    counter = jnp.arange(pair_count, dtype=jnp.int32)
    same_owner = owners[:, None] == owners[None, :]
    earlier = counter[None, :] < counter[:, None]
    rank_order = jnp.sum(jnp.where(same_owner & earlier, 1, 0), axis=1).astype(jnp.int32)
    slot_of = owners * capacity + rank_order
    holder = jnp.sum(jnp.where(slot_of[None, :] == counter[:, None], counter[None, :], 0), axis=1)
    request_ids = local_ids[holder].reshape(groups, capacity)
    tile_table = proxies.reshape(tile_dev, TILE, D)
    wanted = cls_all_to_all(request_ids, 0)
    outgoing = tile_table[wanted]
    fetched = lax.all_to_all(outgoing, "cls", split_axis=0, concat_axis=0, tiled=True)
    fetched = fetched.reshape(pair_count, TILE, D)
    pos_cols = labels.reshape(blocks, BR, 1) - hard_tiles[:, 0:1, None] * TILE
    loss, embed_grad, pair_grads = block_step(
        slot_of, tile_count, embeddings.reshape(blocks, BR, D), pos_cols, fetched
    )
    pair_grads = pair_grads.reshape(groups, capacity, TILE, D)
    returned = lax.all_to_all(pair_grads, "cls", split_axis=0, concat_axis=0, tiled=True)
    got_ids = wanted.reshape(pair_count)
    got_terms = returned.reshape(pair_count, TILE * D)
    select_rows = (jnp.arange(tile_dev, dtype=jnp.int32)[:, None] == got_ids[None, :]).astype(
        jnp.bfloat16
    )
    owned = jnp.dot(select_rows, got_terms, preferred_element_type=jnp.float32)
    owned = owned.reshape(tile_dev * TILE, D)
    proxy_share = lax.psum_scatter(owned, "dp", scatter_dimension=1, tiled=True)
    return (loss.reshape(-1), embed_grad.reshape(-1, D), proxy_share)


def solution(mesh):
    placed = (
        P(("dp", "cls"), None),
        P("cls", None),
        P(("dp", "cls"), None),
        P(("dp", "cls")),
        P(("dp", "cls")),
    )
    return jax.shard_map(
        per_device,
        mesh=mesh,
        in_specs=placed,
        out_specs=(P(("dp", "cls")), P(("dp", "cls"), None), P("cls", "dp")),
        check_vma=False,
    )
```

```python
import functools

import jax
import jax.numpy as jnp
from jax import lax
from jax.experimental import pallas as pl
from jax.experimental.pallas import tpu as pltpu
from jax.sharding import PartitionSpec as P

D = 512
TILE = 128
BR = 128
K = 8


MESH = pl.DeviceIdType.MESH


def _a2a_kernel(n, src_ref, out_ref, send_sem, recv_sem, local_sem):
    me = lax.axis_index("cls")
    row = lax.axis_index("dp")
    barrier = pltpu.get_barrier_semaphore()

    def greet(j, carry):
        peer = lax.rem(me + j, n)
        pl.semaphore_signal(barrier, inc=1, device_id=(row, peer), device_id_type=MESH)
        return carry

    lax.fori_loop(1, n, greet, 0)
    pl.semaphore_wait(barrier, n - 1)
    local = pltpu.make_async_copy(src_ref.at[me], out_ref.at[me], local_sem)
    local.start()

    def remote(j):
        peer = lax.rem(me + j, n)
        return pltpu.make_async_remote_copy(
            src_ref=src_ref.at[peer],
            dst_ref=out_ref.at[me],
            send_sem=send_sem.at[j],
            recv_sem=recv_sem.at[j],
            device_id=(row, peer),
            device_id_type=MESH,
        )

    def launch(j, carry):
        remote(j).start()
        return carry

    def finish(j, carry):
        remote(j).wait()
        return carry

    lax.fori_loop(1, n, launch, 0)
    lax.fori_loop(1, n, finish, 0)
    local.wait()


def cls_all_to_all(x, cid):
    n = x.shape[0]
    return pl.pallas_call(
        functools.partial(_a2a_kernel, n),
        out_shape=jax.ShapeDtypeStruct(x.shape, x.dtype),
        in_specs=[pl.BlockSpec(memory_space=pl.ANY)],
        out_specs=pl.BlockSpec(memory_space=pl.ANY),
        scratch_shapes=[
            pltpu.SemaphoreType.DMA((n,)),
            pltpu.SemaphoreType.DMA((n,)),
            pltpu.SemaphoreType.DMA,
        ],
        compiler_params=pltpu.CompilerParams(collective_id=cid, has_side_effects=True),
    )(x)


logit_scale = 4.0
epsilon = 1e-06


def _block_kernel(slot_ref, count_ref, emb_ref, pos_ref, *rest):
    tiles = rest[:K]
    loss_ref, grad_ref, pair_hbm, pair_buf, pair_sem = rest[K:]
    b = pl.program_id(0)
    emb = emb_ref[0].astype(jnp.float32)
    inverse_norm = lax.rsqrt(jnp.sum(emb * emb, axis=1, keepdims=True) + epsilon)
    unit_exact = emb * inverse_norm
    unit_rows = unit_exact.astype(jnp.bfloat16)
    count = count_ref[b]
    columns = lax.broadcasted_iota(jnp.int32, (BR, TILE), 1)
    hit = columns == pos_ref[0]
    logits = []
    for k in range(K):
        cand = tiles[k][0]
        lg = logit_scale * lax.dot_general(
            unit_rows, cand, (((1,), (1,)), ((), ())), preferred_element_type=jnp.float32
        )
        logits.append(lg)
    masked = [jnp.where(k < count, logits[k], -1e30) for k in range(K)]
    peak = masked[0].max(axis=1, keepdims=True)
    for k in range(1, K):
        peak = jnp.maximum(peak, masked[k].max(axis=1, keepdims=True))
    total = jnp.zeros_like(peak)
    for k in range(K):
        total = total + jnp.sum(jnp.exp(masked[k] - peak), axis=1, keepdims=True)
    log_total = peak + jnp.log(total)
    positive = jnp.sum(jnp.where(hit, logits[0], 0.0), axis=1, keepdims=True)
    loss_ref[0] = log_total - positive
    grad_unit = jnp.zeros((BR, D), jnp.float32)
    for k in range(K):
        probabilities = jnp.exp(masked[k] - log_total)
        if k == 0:
            probabilities = probabilities - jnp.where(hit, 1.0, 0.0)
        dscore = (logit_scale * probabilities).astype(jnp.bfloat16)
        cand = tiles[k][0]
        terms = jnp.dot(dscore, cand, preferred_element_type=jnp.float32)
        grad_unit = grad_unit + terms.astype(jnp.bfloat16).astype(jnp.float32)
        pair_buf[k] = lax.dot_general(
            dscore, unit_rows, (((0,), (0,)), ((), ())), preferred_element_type=jnp.float32
        ).astype(jnp.bfloat16)
    copies = []
    for k in range(K):
        cp = pltpu.make_async_copy(pair_buf.at[k], pair_hbm.at[slot_ref[b * K + k]], pair_sem.at[k])
        cp.start()
        copies.append(cp)
    radial = jnp.sum(unit_exact * grad_unit, axis=1, keepdims=True)
    grad_ref[0] = ((grad_unit - unit_exact * radial) * inverse_norm).astype(grad_ref.dtype)
    for cp in copies:
        cp.wait()


def block_step(slot_of, tile_count, emb_blocks, pos_cols, fetched):
    blocks = emb_blocks.shape[0]
    pairs = fetched.shape[0]

    def tile_spec(k):
        return pl.BlockSpec((1, TILE, D), lambda b, slot, cnt: (slot[b * K + k], 0, 0))

    grid_spec = pltpu.PrefetchScalarGridSpec(
        num_scalar_prefetch=2,
        grid=(blocks,),
        in_specs=[
            pl.BlockSpec((1, BR, D), lambda b, slot, cnt: (b, 0, 0)),
            pl.BlockSpec((1, BR, 1), lambda b, slot, cnt: (b, 0, 0)),
        ]
        + [tile_spec(k) for k in range(K)],
        out_specs=[
            pl.BlockSpec((1, BR, 1), lambda b, slot, cnt: (b, 0, 0)),
            pl.BlockSpec((1, BR, D), lambda b, slot, cnt: (b, 0, 0)),
            pl.BlockSpec(memory_space=pl.ANY),
        ],
        scratch_shapes=[
            pltpu.VMEM((K, TILE, D), jnp.bfloat16),
            pltpu.SemaphoreType.DMA((K,)),
        ],
    )
    return pl.pallas_call(
        _block_kernel,
        grid_spec=grid_spec,
        out_shape=[
            jax.ShapeDtypeStruct((blocks, BR, 1), jnp.float32),
            jax.ShapeDtypeStruct((blocks, BR, D), jnp.bfloat16),
            jax.ShapeDtypeStruct((pairs, TILE, D), jnp.bfloat16),
        ],
        compiler_params=pltpu.CompilerParams(vmem_limit_bytes=48 * 1024 * 1024),
    )(slot_of, tile_count, emb_blocks, pos_cols, *([fetched] * K))


def _owned_kernel(ids_ref, grad_ref, out_ref):
    s = pl.program_id(0)

    @pl.when(s == 0)
    def _():
        out_ref[...] = jnp.zeros_like(out_ref)

    start = pl.multiple_of(ids_ref[s] * TILE, TILE)
    columns = pl.ds(start, TILE)
    out_ref[:, columns] += grad_ref[0].astype(jnp.float32).T


def owned_columns(got_ids, returned, tile_dev):
    pairs = returned.shape[0]
    grid_spec = pltpu.PrefetchScalarGridSpec(
        num_scalar_prefetch=1,
        grid=(pairs,),
        in_specs=[pl.BlockSpec((1, TILE, D), lambda s, ids: (s, 0, 0))],
        out_specs=pl.BlockSpec((D, tile_dev * TILE), lambda s, ids: (0, 0)),
    )
    return pl.pallas_call(
        _owned_kernel,
        grid_spec=grid_spec,
        out_shape=jax.ShapeDtypeStruct((D, tile_dev * TILE), jnp.float32),
        compiler_params=pltpu.CompilerParams(vmem_limit_bytes=48 * 1024 * 1024),
    )(got_ids, returned)


def per_device(embeddings, proxies, hard_tiles, tile_count, labels):
    blocks = hard_tiles.shape[0]
    pair_count = blocks * K
    groups = lax.axis_size("cls")
    capacity = pair_count // groups
    tile_dev = proxies.shape[0] // TILE
    flat_tiles = hard_tiles.reshape(pair_count)
    owners = flat_tiles // tile_dev
    local_ids = flat_tiles % tile_dev
    counter = jnp.arange(pair_count, dtype=jnp.int32)
    same_owner = owners[:, None] == owners[None, :]
    earlier = counter[None, :] < counter[:, None]
    rank_order = jnp.sum(jnp.where(same_owner & earlier, 1, 0), axis=1).astype(jnp.int32)
    slot_of = owners * capacity + rank_order
    holder = jnp.sum(jnp.where(slot_of[None, :] == counter[:, None], counter[None, :], 0), axis=1)
    request_ids = local_ids[holder].reshape(groups, capacity)
    tile_table = proxies.reshape(tile_dev, TILE, D)
    wanted = cls_all_to_all(request_ids, 0)
    outgoing = tile_table[wanted]
    fetched = lax.all_to_all(outgoing, "cls", split_axis=0, concat_axis=0, tiled=True)
    fetched = fetched.reshape(pair_count, TILE, D)
    pos_cols = labels.reshape(blocks, BR, 1) - hard_tiles[:, 0:1, None] * TILE
    loss, embed_grad, pair_grads = block_step(
        slot_of, tile_count, embeddings.reshape(blocks, BR, D), pos_cols, fetched
    )
    pair_grads = pair_grads.reshape(groups, capacity, TILE, D)
    returned = lax.all_to_all(pair_grads, "cls", split_axis=0, concat_axis=0, tiled=True)
    got_ids = wanted.reshape(pair_count)
    owned_t = owned_columns(got_ids, returned.reshape(pair_count, TILE, D), tile_dev)
    proxy_share = lax.psum_scatter(owned_t, "dp", scatter_dimension=0, tiled=True).T
    return (loss.reshape(-1), embed_grad.reshape(-1, D), proxy_share)


def solution(mesh):
    placed = (
        P(("dp", "cls"), None),
        P("cls", None),
        P(("dp", "cls"), None),
        P(("dp", "cls")),
        P(("dp", "cls")),
    )
    return jax.shard_map(
        per_device,
        mesh=mesh,
        in_specs=placed,
        out_specs=(P(("dp", "cls")), P(("dp", "cls"), None), P("cls", "dp")),
        check_vma=False,
    )
```

```python
import functools

import jax
import jax.numpy as jnp
from jax import lax
from jax.experimental import pallas as pl
from jax.experimental.pallas import tpu as pltpu
from jax.sharding import PartitionSpec as P

D = 512
TILE = 128
BR = 128
K = 8


MESH = pl.DeviceIdType.MESH


def _a2a_kernel(n, src_ref, out_ref, send_sem, recv_sem, local_sem):
    me = lax.axis_index("cls")
    row = lax.axis_index("dp")
    barrier = pltpu.get_barrier_semaphore()

    def greet(j, carry):
        peer = lax.rem(me + j, n)
        pl.semaphore_signal(barrier, inc=1, device_id=(row, peer), device_id_type=MESH)
        return carry

    lax.fori_loop(1, n, greet, 0)
    pl.semaphore_wait(barrier, n - 1)
    local = pltpu.make_async_copy(src_ref.at[me], out_ref.at[me], local_sem)
    local.start()

    def remote(j):
        peer = lax.rem(me + j, n)
        return pltpu.make_async_remote_copy(
            src_ref=src_ref.at[peer],
            dst_ref=out_ref.at[me],
            send_sem=send_sem.at[j],
            recv_sem=recv_sem.at[j],
            device_id=(row, peer),
            device_id_type=MESH,
        )

    def launch(j, carry):
        remote(j).start()
        return carry

    def finish(j, carry):
        remote(j).wait()
        return carry

    lax.fori_loop(1, n, launch, 0)
    lax.fori_loop(1, n, finish, 0)
    local.wait()


def cls_all_to_all(x, cid):
    n = x.shape[0]
    return pl.pallas_call(
        functools.partial(_a2a_kernel, n),
        out_shape=jax.ShapeDtypeStruct(x.shape, x.dtype),
        in_specs=[pl.BlockSpec(memory_space=pl.ANY)],
        out_specs=pl.BlockSpec(memory_space=pl.ANY),
        scratch_shapes=[
            pltpu.SemaphoreType.DMA((n,)),
            pltpu.SemaphoreType.DMA((n,)),
            pltpu.SemaphoreType.DMA,
        ],
        compiler_params=pltpu.CompilerParams(collective_id=cid, has_side_effects=True),
    )(x)


logit_scale = 4.0
epsilon = 1e-06


def _block_kernel(slot_ref, count_ref, emb_ref, pos_ref, *rest):
    tiles = rest[:K]
    loss_ref, grad_ref, pair_lo, pair_hi, pair_buf, pair_sem = rest[K:]
    b = pl.program_id(0)
    emb = emb_ref[0].astype(jnp.float32)
    inverse_norm = lax.rsqrt(jnp.sum(emb * emb, axis=1, keepdims=True) + epsilon)
    unit_exact = emb * inverse_norm
    unit_rows = unit_exact.astype(jnp.bfloat16)
    count = count_ref[b]
    columns = lax.broadcasted_iota(jnp.int32, (BR, TILE), 1)
    hit = columns == pos_ref[0]
    logits = []
    for k in range(K):
        cand = tiles[k][0]
        lg = logit_scale * lax.dot_general(
            unit_rows, cand, (((1,), (1,)), ((), ())), preferred_element_type=jnp.float32
        )
        logits.append(lg)
    masked = [jnp.where(k < count, logits[k], -1e30) for k in range(K)]
    peak = masked[0].max(axis=1, keepdims=True)
    for k in range(1, K):
        peak = jnp.maximum(peak, masked[k].max(axis=1, keepdims=True))
    total = jnp.zeros_like(peak)
    for k in range(K):
        total = total + jnp.sum(jnp.exp(masked[k] - peak), axis=1, keepdims=True)
    log_total = peak + jnp.log(total)
    positive = jnp.sum(jnp.where(hit, logits[0], 0.0), axis=1, keepdims=True)
    loss_ref[0] = log_total - positive
    grad_unit = jnp.zeros((BR, D), jnp.float32)
    for k in range(K):
        probabilities = jnp.exp(masked[k] - log_total)
        if k == 0:
            probabilities = probabilities - jnp.where(hit, 1.0, 0.0)
        dscore = (logit_scale * probabilities).astype(jnp.bfloat16)
        cand = tiles[k][0]
        terms = jnp.dot(dscore, cand, preferred_element_type=jnp.float32)
        grad_unit = grad_unit + terms.astype(jnp.bfloat16).astype(jnp.float32)
        pair_buf[k] = lax.dot_general(
            dscore, unit_rows, (((0,), (0,)), ((), ())), preferred_element_type=jnp.float32
        ).astype(jnp.bfloat16)
    copies = []
    half = TILE // 2
    for k in range(K):
        slot = slot_ref[b * K + k]
        for h, dst in enumerate((pair_lo, pair_hi)):
            cp = pltpu.make_async_copy(
                pair_buf.at[k, pl.ds(h * half, half)], dst.at[slot], pair_sem.at[k, h]
            )
            cp.start()
            copies.append(cp)
    radial = jnp.sum(unit_exact * grad_unit, axis=1, keepdims=True)
    grad_ref[0] = ((grad_unit - unit_exact * radial) * inverse_norm).astype(grad_ref.dtype)
    for cp in copies:
        cp.wait()


def block_step(slot_of, tile_count, emb_blocks, pos_cols, fetched):
    blocks = emb_blocks.shape[0]
    pairs = fetched.shape[0]

    def tile_spec(k):
        return pl.BlockSpec((1, TILE, D), lambda b, slot, cnt: (slot[b * K + k], 0, 0))

    grid_spec = pltpu.PrefetchScalarGridSpec(
        num_scalar_prefetch=2,
        grid=(blocks,),
        in_specs=[
            pl.BlockSpec((1, BR, D), lambda b, slot, cnt: (b, 0, 0)),
            pl.BlockSpec((1, BR, 1), lambda b, slot, cnt: (b, 0, 0)),
        ]
        + [tile_spec(k) for k in range(K)],
        out_specs=[
            pl.BlockSpec((1, BR, 1), lambda b, slot, cnt: (b, 0, 0)),
            pl.BlockSpec((1, BR, D), lambda b, slot, cnt: (b, 0, 0)),
            pl.BlockSpec(memory_space=pl.ANY),
            pl.BlockSpec(memory_space=pl.ANY),
        ],
        scratch_shapes=[
            pltpu.VMEM((K, TILE, D), jnp.bfloat16),
            pltpu.SemaphoreType.DMA((K, 2)),
        ],
    )
    return pl.pallas_call(
        _block_kernel,
        grid_spec=grid_spec,
        out_shape=[
            jax.ShapeDtypeStruct((blocks, BR, 1), jnp.float32),
            jax.ShapeDtypeStruct((blocks, BR, D), jnp.bfloat16),
            jax.ShapeDtypeStruct((pairs, TILE // 2, D), jnp.bfloat16),
            jax.ShapeDtypeStruct((pairs, TILE // 2, D), jnp.bfloat16),
        ],
        compiler_params=pltpu.CompilerParams(vmem_limit_bytes=48 * 1024 * 1024),
    )(slot_of, tile_count, emb_blocks, pos_cols, *([fetched] * K))


def _owned_kernel(ids_ref, grad_ref, out_ref):
    s = pl.program_id(0)

    @pl.when(s == 0)
    def _():
        out_ref[...] = jnp.zeros_like(out_ref)

    rows = grad_ref.shape[1]
    start = pl.multiple_of(ids_ref[s] * rows, rows)
    out_ref[pl.ds(start, rows), :] += grad_ref[0].astype(jnp.float32)


def owned_rows(got_ids, returned, tile_dev):
    pairs, rows, _ = returned.shape
    grid_spec = pltpu.PrefetchScalarGridSpec(
        num_scalar_prefetch=1,
        grid=(pairs,),
        in_specs=[pl.BlockSpec((1, rows, D), lambda s, ids: (s, 0, 0))],
        out_specs=pl.BlockSpec((tile_dev * rows, D), lambda s, ids: (0, 0)),
    )
    return pl.pallas_call(
        _owned_kernel,
        grid_spec=grid_spec,
        out_shape=jax.ShapeDtypeStruct((tile_dev * rows, D), jnp.float32),
        compiler_params=pltpu.CompilerParams(vmem_limit_bytes=48 * 1024 * 1024),
    )(got_ids, returned)


def per_device(embeddings, proxies, hard_tiles, tile_count, labels):
    blocks = hard_tiles.shape[0]
    pair_count = blocks * K
    groups = lax.axis_size("cls")
    capacity = pair_count // groups
    tile_dev = proxies.shape[0] // TILE
    flat_tiles = hard_tiles.reshape(pair_count)
    owners = flat_tiles // tile_dev
    local_ids = flat_tiles % tile_dev
    counter = jnp.arange(pair_count, dtype=jnp.int32)
    same_owner = owners[:, None] == owners[None, :]
    earlier = counter[None, :] < counter[:, None]
    rank_order = jnp.sum(jnp.where(same_owner & earlier, 1, 0), axis=1).astype(jnp.int32)
    slot_of = owners * capacity + rank_order
    holder = jnp.sum(jnp.where(slot_of[None, :] == counter[:, None], counter[None, :], 0), axis=1)
    request_ids = local_ids[holder].reshape(groups, capacity)
    tile_table = proxies.reshape(tile_dev, TILE, D)
    wanted = cls_all_to_all(request_ids, 0)
    outgoing = tile_table[wanted]
    fetched = lax.all_to_all(outgoing, "cls", split_axis=0, concat_axis=0, tiled=True)
    fetched = fetched.reshape(pair_count, TILE, D)
    pos_cols = labels.reshape(blocks, BR, 1) - hard_tiles[:, 0:1, None] * TILE
    loss, embed_grad, pair_lo, pair_hi = block_step(
        slot_of, tile_count, embeddings.reshape(blocks, BR, D), pos_cols, fetched
    )
    got_ids = wanted.reshape(pair_count)
    shares = []
    for part in (pair_lo, pair_hi):
        part = part.reshape(groups, capacity, TILE // 2, D)
        returned = lax.all_to_all(part, "cls", split_axis=0, concat_axis=0, tiled=True)
        owned = owned_rows(got_ids, returned.reshape(pair_count, TILE // 2, D), tile_dev)
        share = lax.psum_scatter(owned, "dp", scatter_dimension=1, tiled=True)
        shares.append(share.reshape(tile_dev, 1, TILE // 2, -1))
    proxy_share = jnp.concatenate(shares, axis=1).reshape(tile_dev * TILE, -1)
    return (loss.reshape(-1), embed_grad.reshape(-1, D), proxy_share)


def solution(mesh):
    placed = (
        P(("dp", "cls"), None),
        P("cls", None),
        P(("dp", "cls"), None),
        P(("dp", "cls")),
        P(("dp", "cls")),
    )
    return jax.shard_map(
        per_device,
        mesh=mesh,
        in_specs=placed,
        out_specs=(P(("dp", "cls")), P(("dp", "cls"), None), P("cls", "dp")),
        check_vma=False,
    )
```

```python
import functools

import jax
import jax.numpy as jnp
from jax import lax
from jax.experimental import pallas as pl
from jax.experimental.pallas import tpu as pltpu
from jax.sharding import PartitionSpec as P

D = 512
TILE = 128
BR = 128
K = 8


MESH = pl.DeviceIdType.MESH


def _a2a_kernel(n, src_ref, out_ref, send_sem, recv_sem, local_sem):
    me = lax.axis_index("cls")
    row = lax.axis_index("dp")
    barrier = pltpu.get_barrier_semaphore()

    def greet(j, carry):
        peer = lax.rem(me + j, n)
        pl.semaphore_signal(barrier, inc=1, device_id=(row, peer), device_id_type=MESH)
        return carry

    lax.fori_loop(1, n, greet, 0)
    pl.semaphore_wait(barrier, n - 1)
    local = pltpu.make_async_copy(src_ref.at[me], out_ref.at[me], local_sem)
    local.start()

    def remote(j):
        peer = lax.rem(me + j, n)
        return pltpu.make_async_remote_copy(
            src_ref=src_ref.at[peer],
            dst_ref=out_ref.at[me],
            send_sem=send_sem.at[j],
            recv_sem=recv_sem.at[j],
            device_id=(row, peer),
            device_id_type=MESH,
        )

    def launch(j, carry):
        remote(j).start()
        return carry

    def finish(j, carry):
        remote(j).wait()
        return carry

    lax.fori_loop(1, n, launch, 0)
    lax.fori_loop(1, n, finish, 0)
    local.wait()


def cls_all_to_all(x, cid):
    n = x.shape[0]
    return pl.pallas_call(
        functools.partial(_a2a_kernel, n),
        out_shape=jax.ShapeDtypeStruct(x.shape, x.dtype),
        in_specs=[pl.BlockSpec(memory_space=pl.ANY)],
        out_specs=pl.BlockSpec(memory_space=pl.ANY),
        scratch_shapes=[
            pltpu.SemaphoreType.DMA((n,)),
            pltpu.SemaphoreType.DMA((n,)),
            pltpu.SemaphoreType.DMA,
        ],
        compiler_params=pltpu.CompilerParams(collective_id=cid, has_side_effects=True),
    )(x)


logit_scale = 4.0
epsilon = 1e-06


def _block_kernel(slot_ref, count_ref, emb_ref, pos_ref, *rest):
    tiles = rest[:K]
    loss_ref, grad_ref, pair_hbm, pair_buf, pair_sem = rest[K:]
    b = pl.program_id(0)
    emb = emb_ref[0].astype(jnp.float32)
    inverse_norm = lax.rsqrt(jnp.sum(emb * emb, axis=1, keepdims=True) + epsilon)
    unit_exact = emb * inverse_norm
    unit_rows = unit_exact.astype(jnp.bfloat16)
    count = count_ref[b]
    columns = lax.broadcasted_iota(jnp.int32, (BR, TILE), 1)
    hit = columns == pos_ref[0]
    logits = []
    for k in range(K):
        cand = tiles[k][0]
        lg = logit_scale * lax.dot_general(
            unit_rows, cand, (((1,), (1,)), ((), ())), preferred_element_type=jnp.float32
        )
        logits.append(lg)
    masked = [jnp.where(k < count, logits[k], -1e30) for k in range(K)]
    peak = masked[0].max(axis=1, keepdims=True)
    for k in range(1, K):
        peak = jnp.maximum(peak, masked[k].max(axis=1, keepdims=True))
    total = jnp.zeros_like(peak)
    for k in range(K):
        total = total + jnp.sum(jnp.exp(masked[k] - peak), axis=1, keepdims=True)
    log_total = peak + jnp.log(total)
    positive = jnp.sum(jnp.where(hit, logits[0], 0.0), axis=1, keepdims=True)
    loss_ref[0] = log_total - positive
    grad_unit = jnp.zeros((BR, D), jnp.float32)
    for k in range(K):
        probabilities = jnp.exp(masked[k] - log_total)
        if k == 0:
            probabilities = probabilities - jnp.where(hit, 1.0, 0.0)
        dscore = (logit_scale * probabilities).astype(jnp.bfloat16)
        cand = tiles[k][0]
        terms = jnp.dot(dscore, cand, preferred_element_type=jnp.float32)
        grad_unit = grad_unit + terms.astype(jnp.bfloat16).astype(jnp.float32)
        pair_buf[k] = lax.dot_general(
            dscore, unit_rows, (((0,), (0,)), ((), ())), preferred_element_type=jnp.float32
        ).astype(jnp.bfloat16)
    copies = []
    for k in range(K):
        cp = pltpu.make_async_copy(pair_buf.at[k], pair_hbm.at[slot_ref[b * K + k]], pair_sem.at[k])
        cp.start()
        copies.append(cp)
    radial = jnp.sum(unit_exact * grad_unit, axis=1, keepdims=True)
    grad_ref[0] = ((grad_unit - unit_exact * radial) * inverse_norm).astype(grad_ref.dtype)
    for cp in copies:
        cp.wait()


def block_step(slot_of, tile_count, emb_blocks, pos_cols, fetched):
    blocks = emb_blocks.shape[0]
    pairs = fetched.shape[0]

    def tile_spec(k):
        return pl.BlockSpec((1, TILE, D), lambda b, slot, cnt: (slot[b * K + k], 0, 0))

    grid_spec = pltpu.PrefetchScalarGridSpec(
        num_scalar_prefetch=2,
        grid=(blocks,),
        in_specs=[
            pl.BlockSpec((1, BR, D), lambda b, slot, cnt: (b, 0, 0)),
            pl.BlockSpec((1, BR, 1), lambda b, slot, cnt: (b, 0, 0)),
        ]
        + [tile_spec(k) for k in range(K)],
        out_specs=[
            pl.BlockSpec((1, BR, 1), lambda b, slot, cnt: (b, 0, 0)),
            pl.BlockSpec((1, BR, D), lambda b, slot, cnt: (b, 0, 0)),
            pl.BlockSpec(memory_space=pl.ANY),
        ],
        scratch_shapes=[
            pltpu.VMEM((K, TILE, D), jnp.bfloat16),
            pltpu.SemaphoreType.DMA((K,)),
        ],
    )
    return pl.pallas_call(
        _block_kernel,
        grid_spec=grid_spec,
        out_shape=[
            jax.ShapeDtypeStruct((blocks, BR, 1), jnp.float32),
            jax.ShapeDtypeStruct((blocks, BR, D), jnp.bfloat16),
            jax.ShapeDtypeStruct((pairs, TILE, D), jnp.bfloat16),
        ],
        compiler_params=pltpu.CompilerParams(vmem_limit_bytes=48 * 1024 * 1024),
    )(slot_of, tile_count, emb_blocks, pos_cols, *([fetched] * K))


def per_device(embeddings, proxies, hard_tiles, tile_count, labels):
    blocks = hard_tiles.shape[0]
    pair_count = blocks * K
    groups = lax.axis_size("cls")
    capacity = pair_count // groups
    tile_dev = proxies.shape[0] // TILE
    flat_tiles = hard_tiles.reshape(pair_count)
    owners = flat_tiles // tile_dev
    local_ids = flat_tiles % tile_dev
    counter = jnp.arange(pair_count, dtype=jnp.int32)
    same_owner = owners[:, None] == owners[None, :]
    earlier = counter[None, :] < counter[:, None]
    rank_order = jnp.sum(jnp.where(same_owner & earlier, 1, 0), axis=1).astype(jnp.int32)
    slot_of = owners * capacity + rank_order
    holder = jnp.sum(jnp.where(slot_of[None, :] == counter[:, None], counter[None, :], 0), axis=1)
    request_ids = local_ids[holder].reshape(groups, capacity)
    tile_table = proxies.reshape(tile_dev, TILE, D)
    wanted = cls_all_to_all(request_ids, 0)
    outgoing = tile_table[wanted]
    fetched = lax.all_to_all(outgoing, "cls", split_axis=0, concat_axis=0, tiled=True)
    fetched = fetched.reshape(pair_count, TILE, D)
    pos_cols = labels.reshape(blocks, BR, 1) - hard_tiles[:, 0:1, None] * TILE
    loss, embed_grad, pair_grads = block_step(
        slot_of, tile_count, embeddings.reshape(blocks, BR, D), pos_cols, fetched
    )
    pair_grads = pair_grads.reshape(groups, capacity, TILE, D)
    returned = lax.all_to_all(pair_grads, "cls", split_axis=0, concat_axis=0, tiled=True)
    got_ids = wanted.reshape(pair_count)
    got_terms = returned.reshape(pair_count, TILE * D)
    select_rows = (jnp.arange(tile_dev, dtype=jnp.int32)[:, None] == got_ids[None, :]).astype(
        jnp.bfloat16
    )
    owned = jnp.dot(select_rows, got_terms, preferred_element_type=jnp.float32)
    owned = owned.astype(jnp.bfloat16).reshape(tile_dev * TILE, D)
    proxy_share = lax.psum_scatter(owned, "dp", scatter_dimension=1, tiled=True)
    proxy_share = proxy_share.astype(jnp.float32)
    return (loss.reshape(-1), embed_grad.reshape(-1, D), proxy_share)


def solution(mesh):
    placed = (
        P(("dp", "cls"), None),
        P("cls", None),
        P(("dp", "cls"), None),
        P(("dp", "cls")),
        P(("dp", "cls")),
    )
    return jax.shard_map(
        per_device,
        mesh=mesh,
        in_specs=placed,
        out_specs=(P(("dp", "cls")), P(("dp", "cls"), None), P("cls", "dp")),
        check_vma=False,
    )
```

```python
import functools

import jax
import jax.numpy as jnp
from jax import lax
from jax.experimental import pallas as pl
from jax.experimental.pallas import tpu as pltpu
from jax.sharding import PartitionSpec as P

D = 512
TILE = 128
BR = 128
K = 8


MESH = pl.DeviceIdType.MESH


def _a2a_kernel(n, src_ref, out_ref, send_sem, recv_sem, local_sem):
    me = lax.axis_index("cls")
    row = lax.axis_index("dp")
    barrier = pltpu.get_barrier_semaphore()

    def greet(j, carry):
        peer = lax.rem(me + j, n)
        pl.semaphore_signal(barrier, inc=1, device_id=(row, peer), device_id_type=MESH)
        return carry

    lax.fori_loop(1, n, greet, 0)
    pl.semaphore_wait(barrier, n - 1)
    local = pltpu.make_async_copy(src_ref.at[me], out_ref.at[me], local_sem)
    local.start()

    def remote(j):
        peer = lax.rem(me + j, n)
        return pltpu.make_async_remote_copy(
            src_ref=src_ref.at[peer],
            dst_ref=out_ref.at[me],
            send_sem=send_sem.at[j],
            recv_sem=recv_sem.at[j],
            device_id=(row, peer),
            device_id_type=MESH,
        )

    def launch(j, carry):
        remote(j).start()
        return carry

    def finish(j, carry):
        remote(j).wait()
        return carry

    lax.fori_loop(1, n, launch, 0)
    lax.fori_loop(1, n, finish, 0)
    local.wait()


def cls_all_to_all(x, cid):
    n = x.shape[0]
    return pl.pallas_call(
        functools.partial(_a2a_kernel, n),
        out_shape=jax.ShapeDtypeStruct(x.shape, x.dtype),
        in_specs=[pl.BlockSpec(memory_space=pl.ANY)],
        out_specs=pl.BlockSpec(memory_space=pl.ANY),
        scratch_shapes=[
            pltpu.SemaphoreType.DMA((n,)),
            pltpu.SemaphoreType.DMA((n,)),
            pltpu.SemaphoreType.DMA,
        ],
        compiler_params=pltpu.CompilerParams(collective_id=cid, has_side_effects=True),
    )(x)


logit_scale = 4.0
epsilon = 1e-06


def _block_kernel(slot_ref, count_ref, emb_ref, pos_ref, *rest):
    tiles = rest[:K]
    loss_ref, grad_ref, pair_hbm, pair_buf, pair_sem = rest[K:]
    b = pl.program_id(0)
    emb = emb_ref[0].astype(jnp.float32)
    inverse_norm = lax.rsqrt(jnp.sum(emb * emb, axis=1, keepdims=True) + epsilon)
    unit_exact = emb * inverse_norm
    unit_rows = unit_exact.astype(jnp.bfloat16)
    count = count_ref[b]
    columns = lax.broadcasted_iota(jnp.int32, (BR, TILE), 1)
    hit = columns == pos_ref[0]
    logits = []
    for k in range(K):
        cand = tiles[k][0]
        lg = logit_scale * lax.dot_general(
            unit_rows, cand, (((1,), (1,)), ((), ())), preferred_element_type=jnp.float32
        )
        logits.append(lg)
    masked = [jnp.where(k < count, logits[k], -1e30) for k in range(K)]
    peak = masked[0].max(axis=1, keepdims=True)
    for k in range(1, K):
        peak = jnp.maximum(peak, masked[k].max(axis=1, keepdims=True))
    total = jnp.zeros_like(peak)
    for k in range(K):
        total = total + jnp.sum(jnp.exp(masked[k] - peak), axis=1, keepdims=True)
    log_total = peak + jnp.log(total)
    positive = jnp.sum(jnp.where(hit, logits[0], 0.0), axis=1, keepdims=True)
    loss_ref[0] = log_total - positive
    grad_unit = jnp.zeros((BR, D), jnp.float32)
    for k in range(K):
        probabilities = jnp.exp(masked[k] - log_total)
        if k == 0:
            probabilities = probabilities - jnp.where(hit, 1.0, 0.0)
        dscore = (logit_scale * probabilities).astype(jnp.bfloat16)
        cand = tiles[k][0]
        terms = jnp.dot(dscore, cand, preferred_element_type=jnp.float32)
        grad_unit = grad_unit + terms.astype(jnp.bfloat16).astype(jnp.float32)
        pair_t = lax.dot_general(
            unit_rows, dscore, (((0,), (0,)), ((), ())), preferred_element_type=jnp.float32
        ).astype(jnp.bfloat16)
        pair_buf[:, k] = pair_t.reshape(pair_buf.shape[0], D // pair_buf.shape[0], TILE)
    copies = []
    for k in range(K):
        cp = pltpu.make_async_copy(
            pair_buf.at[:, pl.ds(k, 1)],
            pair_hbm.at[:, pl.ds(slot_ref[b * K + k], 1)],
            pair_sem.at[k],
        )
        cp.start()
        copies.append(cp)
    radial = jnp.sum(unit_exact * grad_unit, axis=1, keepdims=True)
    grad_ref[0] = ((grad_unit - unit_exact * radial) * inverse_norm).astype(grad_ref.dtype)
    for cp in copies:
        cp.wait()


def block_step(slot_of, tile_count, emb_blocks, pos_cols, fetched, parts):
    blocks = emb_blocks.shape[0]
    pairs = fetched.shape[0]

    def tile_spec(k):
        return pl.BlockSpec((1, TILE, D), lambda b, slot, cnt: (slot[b * K + k], 0, 0))

    grid_spec = pltpu.PrefetchScalarGridSpec(
        num_scalar_prefetch=2,
        grid=(blocks,),
        in_specs=[
            pl.BlockSpec((1, BR, D), lambda b, slot, cnt: (b, 0, 0)),
            pl.BlockSpec((1, BR, 1), lambda b, slot, cnt: (b, 0, 0)),
        ]
        + [tile_spec(k) for k in range(K)],
        out_specs=[
            pl.BlockSpec((1, BR, 1), lambda b, slot, cnt: (b, 0, 0)),
            pl.BlockSpec((1, BR, D), lambda b, slot, cnt: (b, 0, 0)),
            pl.BlockSpec(memory_space=pl.ANY),
        ],
        scratch_shapes=[
            pltpu.VMEM((parts, K, D // parts, TILE), jnp.bfloat16),
            pltpu.SemaphoreType.DMA((K,)),
        ],
    )
    return pl.pallas_call(
        _block_kernel,
        grid_spec=grid_spec,
        out_shape=[
            jax.ShapeDtypeStruct((blocks, BR, 1), jnp.float32),
            jax.ShapeDtypeStruct((blocks, BR, D), jnp.bfloat16),
            jax.ShapeDtypeStruct((parts, pairs, D // parts, TILE), jnp.bfloat16),
        ],
        compiler_params=pltpu.CompilerParams(vmem_limit_bytes=48 * 1024 * 1024),
    )(slot_of, tile_count, emb_blocks, pos_cols, *([fetched] * K))


def per_device(embeddings, proxies, hard_tiles, tile_count, labels):
    blocks = hard_tiles.shape[0]
    pair_count = blocks * K
    groups = lax.axis_size("cls")
    capacity = pair_count // groups
    tile_dev = proxies.shape[0] // TILE
    flat_tiles = hard_tiles.reshape(pair_count)
    owners = flat_tiles // tile_dev
    local_ids = flat_tiles % tile_dev
    counter = jnp.arange(pair_count, dtype=jnp.int32)
    same_owner = owners[:, None] == owners[None, :]
    earlier = counter[None, :] < counter[:, None]
    rank_order = jnp.sum(jnp.where(same_owner & earlier, 1, 0), axis=1).astype(jnp.int32)
    slot_of = owners * capacity + rank_order
    holder = jnp.sum(jnp.where(slot_of[None, :] == counter[:, None], counter[None, :], 0), axis=1)
    request_ids = local_ids[holder].reshape(groups, capacity)
    tile_table = proxies.reshape(tile_dev, TILE, D)
    wanted = cls_all_to_all(request_ids, 0)
    outgoing = tile_table[wanted]
    fetched = lax.all_to_all(outgoing, "cls", split_axis=0, concat_axis=0, tiled=True)
    fetched = fetched.reshape(pair_count, TILE, D)
    pos_cols = labels.reshape(blocks, BR, 1) - hard_tiles[:, 0:1, None] * TILE
    parts = lax.axis_size("dp")
    loss, embed_grad, pair_grads = block_step(
        slot_of, tile_count, embeddings.reshape(blocks, BR, D), pos_cols, fetched, parts
    )
    pair_grads = pair_grads.reshape(parts * groups, capacity, D // parts, TILE)
    returned = lax.all_to_all(pair_grads, ("dp", "cls"), split_axis=0, concat_axis=0, tiled=True)
    got_ids = lax.all_gather(wanted, "dp").reshape(parts * pair_count)
    got_terms = returned.reshape(parts * pair_count, D // parts, TILE)
    select_rows = (jnp.arange(tile_dev, dtype=jnp.int32)[:, None] == got_ids[None, :]).astype(
        jnp.bfloat16
    )
    owned = jnp.einsum("tp,pdc->tcd", select_rows, got_terms, preferred_element_type=jnp.float32)
    proxy_share = owned.reshape(tile_dev * TILE, D // parts)
    return (loss.reshape(-1), embed_grad.reshape(-1, D), proxy_share)


def solution(mesh):
    placed = (
        P(("dp", "cls"), None),
        P("cls", None),
        P(("dp", "cls"), None),
        P(("dp", "cls")),
        P(("dp", "cls")),
    )
    return jax.shard_map(
        per_device,
        mesh=mesh,
        in_specs=placed,
        out_specs=(P(("dp", "cls")), P(("dp", "cls"), None), P("cls", "dp")),
        check_vma=False,
    )
```

```python
import functools

import jax
import jax.numpy as jnp
from jax import lax
from jax.experimental import pallas as pl
from jax.experimental.pallas import tpu as pltpu
from jax.sharding import PartitionSpec as P

D = 512
TILE = 128
BR = 128
K = 8


MESH = pl.DeviceIdType.MESH


def _a2a_kernel(n, src_ref, out_ref, send_sem, recv_sem, local_sem):
    me = lax.axis_index("cls")
    row = lax.axis_index("dp")
    barrier = pltpu.get_barrier_semaphore()

    def greet(j, carry):
        peer = lax.rem(me + j, n)
        pl.semaphore_signal(barrier, inc=1, device_id=(row, peer), device_id_type=MESH)
        return carry

    lax.fori_loop(1, n, greet, 0)
    pl.semaphore_wait(barrier, n - 1)
    local = pltpu.make_async_copy(src_ref.at[me], out_ref.at[me], local_sem)
    local.start()

    def remote(j):
        peer = lax.rem(me + j, n)
        return pltpu.make_async_remote_copy(
            src_ref=src_ref.at[peer],
            dst_ref=out_ref.at[me],
            send_sem=send_sem.at[j],
            recv_sem=recv_sem.at[j],
            device_id=(row, peer),
            device_id_type=MESH,
        )

    def launch(j, carry):
        remote(j).start()
        return carry

    def finish(j, carry):
        remote(j).wait()
        return carry

    lax.fori_loop(1, n, launch, 0)
    lax.fori_loop(1, n, finish, 0)
    local.wait()


def cls_all_to_all(x, cid):
    n = x.shape[0]
    return pl.pallas_call(
        functools.partial(_a2a_kernel, n),
        out_shape=jax.ShapeDtypeStruct(x.shape, x.dtype),
        in_specs=[pl.BlockSpec(memory_space=pl.ANY)],
        out_specs=pl.BlockSpec(memory_space=pl.ANY),
        scratch_shapes=[
            pltpu.SemaphoreType.DMA((n,)),
            pltpu.SemaphoreType.DMA((n,)),
            pltpu.SemaphoreType.DMA,
        ],
        compiler_params=pltpu.CompilerParams(collective_id=cid, has_side_effects=True),
    )(x)


logit_scale = 4.0
epsilon = 1e-06


def _block_kernel(slot_ref, count_ref, emb_ref, pos_ref, *rest):
    tiles = rest[:K]
    loss_ref, grad_ref, pair_hbm, pair_buf, pair_sem = rest[K:]
    b = pl.program_id(0)
    emb = emb_ref[0].astype(jnp.float32)
    inverse_norm = lax.rsqrt(jnp.sum(emb * emb, axis=1, keepdims=True) + epsilon)
    unit_exact = emb * inverse_norm
    unit_rows = unit_exact.astype(jnp.bfloat16)
    unit_t = unit_rows.T
    count = count_ref[b]
    classes = lax.broadcasted_iota(jnp.int32, (TILE, BR), 0)
    hit = classes == pos_ref[0]
    logits = []
    for k in range(K):
        logits.append(logit_scale * jnp.dot(tiles[k][0], unit_t, preferred_element_type=jnp.float32))
    masked = [jnp.where(k < count, logits[k], -1e30) for k in range(K)]
    peak = masked[0].max(axis=0, keepdims=True)
    for k in range(1, K):
        peak = jnp.maximum(peak, masked[k].max(axis=0, keepdims=True))
    total = jnp.zeros_like(peak)
    for k in range(K):
        total = total + jnp.sum(jnp.exp(masked[k] - peak), axis=0, keepdims=True)
    log_total = peak + jnp.log(total)
    positive = jnp.sum(jnp.where(hit, logits[0], 0.0), axis=0, keepdims=True)
    loss_ref[0] = log_total - positive
    grad_unit = jnp.zeros((BR, D), jnp.float32)
    for k in range(K):
        probabilities = jnp.exp(masked[k] - log_total)
        if k == 0:
            probabilities = probabilities - jnp.where(hit, 1.0, 0.0)
        dscore = (logit_scale * probabilities).astype(jnp.bfloat16).T
        terms = jnp.dot(dscore, tiles[k][0], preferred_element_type=jnp.float32)
        grad_unit = grad_unit + terms.astype(jnp.bfloat16).astype(jnp.float32)
        pair_t = jnp.dot(unit_t, dscore, preferred_element_type=jnp.float32).astype(jnp.bfloat16)
        pair_buf[:, k] = pair_t.reshape(pair_buf.shape[0], D // pair_buf.shape[0], TILE)
    copies = []
    for k in range(K):
        cp = pltpu.make_async_copy(
            pair_buf.at[:, pl.ds(k, 1)],
            pair_hbm.at[:, pl.ds(slot_ref[b * K + k], 1)],
            pair_sem.at[k],
        )
        cp.start()
        copies.append(cp)
    radial = jnp.sum(unit_exact * grad_unit, axis=1, keepdims=True)
    grad_ref[0] = ((grad_unit - unit_exact * radial) * inverse_norm).astype(grad_ref.dtype)
    for cp in copies:
        cp.wait()


def block_step(slot_of, tile_count, emb_blocks, pos_cols, fetched, parts):
    blocks = emb_blocks.shape[0]
    pairs = fetched.shape[0]

    def tile_spec(k):
        return pl.BlockSpec((1, TILE, D), lambda b, slot, cnt: (slot[b * K + k], 0, 0))

    grid_spec = pltpu.PrefetchScalarGridSpec(
        num_scalar_prefetch=2,
        grid=(blocks,),
        in_specs=[
            pl.BlockSpec((1, BR, D), lambda b, slot, cnt: (b, 0, 0)),
            pl.BlockSpec((1, 1, BR), lambda b, slot, cnt: (b, 0, 0)),
        ]
        + [tile_spec(k) for k in range(K)],
        out_specs=[
            pl.BlockSpec((1, 1, BR), lambda b, slot, cnt: (b, 0, 0)),
            pl.BlockSpec((1, BR, D), lambda b, slot, cnt: (b, 0, 0)),
            pl.BlockSpec(memory_space=pl.ANY),
        ],
        scratch_shapes=[
            pltpu.VMEM((parts, K, D // parts, TILE), jnp.bfloat16),
            pltpu.SemaphoreType.DMA((K,)),
        ],
    )
    return pl.pallas_call(
        _block_kernel,
        grid_spec=grid_spec,
        out_shape=[
            jax.ShapeDtypeStruct((blocks, 1, BR), jnp.float32),
            jax.ShapeDtypeStruct((blocks, BR, D), jnp.bfloat16),
            jax.ShapeDtypeStruct((parts, pairs, D // parts, TILE), jnp.bfloat16),
        ],
        compiler_params=pltpu.CompilerParams(vmem_limit_bytes=48 * 1024 * 1024),
    )(slot_of, tile_count, emb_blocks, pos_cols, *([fetched] * K))


def _column_sum_kernel(ids_ref, piece_ref, out_ref):
    step = pl.program_id(0)
    chunk = piece_ref.shape[0]

    @pl.when(step == 0)
    def _():
        out_ref[...] = jnp.zeros_like(out_ref)

    def body(j, carry):
        start = pl.multiple_of(ids_ref[step * chunk + j] * TILE, TILE)
        window = pl.ds(start, TILE)
        out_ref[:, window] += piece_ref[j].astype(jnp.float32)
        return carry

    lax.fori_loop(0, chunk, body, 0, unroll=8)


def column_sum(got_ids, pieces, tile_dev, chunk=64):
    count, width, _ = pieces.shape
    grid_spec = pltpu.PrefetchScalarGridSpec(
        num_scalar_prefetch=1,
        grid=(count // chunk,),
        in_specs=[pl.BlockSpec((chunk, width, TILE), lambda s, ids: (s, 0, 0))],
        out_specs=pl.BlockSpec((width, tile_dev * TILE), lambda s, ids: (0, 0)),
    )
    return pl.pallas_call(
        _column_sum_kernel,
        grid_spec=grid_spec,
        out_shape=jax.ShapeDtypeStruct((width, tile_dev * TILE), jnp.float32),
    )(got_ids, pieces)


def per_device(embeddings, proxies, hard_tiles, tile_count, labels):
    blocks = hard_tiles.shape[0]
    pair_count = blocks * K
    groups = lax.axis_size("cls")
    capacity = pair_count // groups
    tile_dev = proxies.shape[0] // TILE
    flat_tiles = hard_tiles.reshape(pair_count)
    owners = flat_tiles // tile_dev
    local_ids = flat_tiles % tile_dev
    counter = jnp.arange(pair_count, dtype=jnp.int32)
    same_owner = owners[:, None] == owners[None, :]
    earlier = counter[None, :] < counter[:, None]
    rank_order = jnp.sum(jnp.where(same_owner & earlier, 1, 0), axis=1).astype(jnp.int32)
    slot_of = owners * capacity + rank_order
    holder = jnp.sum(jnp.where(slot_of[None, :] == counter[:, None], counter[None, :], 0), axis=1)
    request_ids = local_ids[holder].reshape(groups, capacity)
    tile_table = proxies.reshape(tile_dev, TILE, D)
    wanted = cls_all_to_all(request_ids, 0)
    outgoing = tile_table[wanted]
    fetched = lax.all_to_all(outgoing, "cls", split_axis=0, concat_axis=0, tiled=True)
    fetched = fetched.reshape(pair_count, TILE, D)
    pos_cols = labels.reshape(blocks, 1, BR) - hard_tiles[:, None, 0:1] * TILE
    parts = lax.axis_size("dp")
    loss, embed_grad, pair_grads = block_step(
        slot_of, tile_count, embeddings.reshape(blocks, BR, D), pos_cols, fetched, parts
    )
    pair_grads = pair_grads.reshape(parts * groups, capacity, D // parts, TILE)
    returned = lax.all_to_all(pair_grads, ("dp", "cls"), split_axis=0, concat_axis=0, tiled=True)
    got_ids = lax.all_gather(wanted, "dp").reshape(parts * pair_count)
    got_terms = returned.reshape(parts * pair_count, D // parts, TILE)
    proxy_share = column_sum(got_ids, got_terms, tile_dev).T
    return (loss.reshape(-1), embed_grad.reshape(-1, D), proxy_share)


def solution(mesh):
    placed = (
        P(("dp", "cls"), None),
        P("cls", None),
        P(("dp", "cls"), None),
        P(("dp", "cls")),
        P(("dp", "cls")),
    )
    return jax.shard_map(
        per_device,
        mesh=mesh,
        in_specs=placed,
        out_specs=(P(("dp", "cls")), P(("dp", "cls"), None), P("cls", "dp")),
        check_vma=False,
    )
```

```python
import functools

import jax
import jax.numpy as jnp
from jax import lax
from jax.experimental import pallas as pl
from jax.experimental.pallas import tpu as pltpu
from jax.sharding import PartitionSpec as P

D = 512
TILE = 128
BR = 128
K = 8


MESH = pl.DeviceIdType.MESH


def _a2a_kernel(n, src_ref, out_ref, send_sem, recv_sem, local_sem):
    me = lax.axis_index("cls")
    row = lax.axis_index("dp")
    barrier = pltpu.get_barrier_semaphore()

    def greet(j, carry):
        peer = lax.rem(me + j, n)
        pl.semaphore_signal(barrier, inc=1, device_id=(row, peer), device_id_type=MESH)
        return carry

    lax.fori_loop(1, n, greet, 0)
    pl.semaphore_wait(barrier, n - 1)
    local = pltpu.make_async_copy(src_ref.at[me], out_ref.at[me], local_sem)
    local.start()

    def remote(j):
        peer = lax.rem(me + j, n)
        return pltpu.make_async_remote_copy(
            src_ref=src_ref.at[peer],
            dst_ref=out_ref.at[me],
            send_sem=send_sem.at[j],
            recv_sem=recv_sem.at[j],
            device_id=(row, peer),
            device_id_type=MESH,
        )

    def launch(j, carry):
        remote(j).start()
        return carry

    def finish(j, carry):
        remote(j).wait()
        return carry

    lax.fori_loop(1, n, launch, 0)
    lax.fori_loop(1, n, finish, 0)
    local.wait()


def cls_all_to_all(x, cid):
    n = x.shape[0]
    return pl.pallas_call(
        functools.partial(_a2a_kernel, n),
        out_shape=jax.ShapeDtypeStruct(x.shape, x.dtype),
        in_specs=[pl.BlockSpec(memory_space=pl.ANY)],
        out_specs=pl.BlockSpec(memory_space=pl.ANY),
        scratch_shapes=[
            pltpu.SemaphoreType.DMA((n,)),
            pltpu.SemaphoreType.DMA((n,)),
            pltpu.SemaphoreType.DMA,
        ],
        compiler_params=pltpu.CompilerParams(collective_id=cid, has_side_effects=True),
    )(x)


logit_scale = 4.0
epsilon = 1e-06


def _score_kernel(slot_ref, count_ref, emb_ref, pos_ref, *rest):
    tiles = rest[:K]
    loss_ref, score_ref, pair_hbm, pair_buf, pair_sem = rest[K:]
    b = pl.program_id(0)
    emb = emb_ref[0].astype(jnp.float32)
    inverse_norm = lax.rsqrt(jnp.sum(emb * emb, axis=1, keepdims=True) + epsilon)
    unit_t = (emb * inverse_norm).astype(jnp.bfloat16).T
    count = count_ref[b]
    classes = lax.broadcasted_iota(jnp.int32, (TILE, BR), 0)
    hit = classes == pos_ref[0]
    logits = []
    for k in range(K):
        logits.append(logit_scale * jnp.dot(tiles[k][0], unit_t, preferred_element_type=jnp.float32))
    masked = [jnp.where(k < count, logits[k], -1e30) for k in range(K)]
    peak = masked[0].max(axis=0, keepdims=True)
    for k in range(1, K):
        peak = jnp.maximum(peak, masked[k].max(axis=0, keepdims=True))
    total = jnp.zeros_like(peak)
    for k in range(K):
        total = total + jnp.sum(jnp.exp(masked[k] - peak), axis=0, keepdims=True)
    log_total = peak + jnp.log(total)
    positive = jnp.sum(jnp.where(hit, logits[0], 0.0), axis=0, keepdims=True)
    loss_ref[0] = log_total - positive
    for k in range(K):
        probabilities = jnp.exp(masked[k] - log_total)
        if k == 0:
            probabilities = probabilities - jnp.where(hit, 1.0, 0.0)
        dscore = (logit_scale * probabilities).astype(jnp.bfloat16).T
        score_ref[0, k] = dscore
        pair_t = jnp.dot(unit_t, dscore, preferred_element_type=jnp.float32).astype(jnp.bfloat16)
        pair_buf[:, k] = pair_t.reshape(pair_buf.shape[0], D // pair_buf.shape[0], TILE)
    copies = []
    for k in range(K):
        cp = pltpu.make_async_copy(
            pair_buf.at[:, pl.ds(k, 1)],
            pair_hbm.at[:, pl.ds(slot_ref[b * K + k], 1)],
            pair_sem.at[k],
        )
        cp.start()
        copies.append(cp)
    for cp in copies:
        cp.wait()


def _embed_kernel(slot_ref, emb_ref, score_ref, *rest):
    tiles = rest[:K]
    (grad_ref,) = rest[K:]
    emb = emb_ref[0].astype(jnp.float32)
    inverse_norm = lax.rsqrt(jnp.sum(emb * emb, axis=1, keepdims=True) + epsilon)
    unit_exact = emb * inverse_norm
    grad_unit = jnp.zeros((BR, D), jnp.float32)
    for k in range(K):
        terms = jnp.dot(score_ref[0, k], tiles[k][0], preferred_element_type=jnp.float32)
        grad_unit = grad_unit + terms.astype(jnp.bfloat16).astype(jnp.float32)
    radial = jnp.sum(unit_exact * grad_unit, axis=1, keepdims=True)
    grad_ref[0] = ((grad_unit - unit_exact * radial) * inverse_norm).astype(grad_ref.dtype)


def _tile_spec(k):
    return pl.BlockSpec((1, TILE, D), lambda b, slot, *_: (slot[b * K + k], 0, 0))


def score_step(slot_of, tile_count, emb_blocks, pos_cols, fetched, parts):
    blocks = emb_blocks.shape[0]
    pairs = fetched.shape[0]
    grid_spec = pltpu.PrefetchScalarGridSpec(
        num_scalar_prefetch=2,
        grid=(blocks,),
        in_specs=[
            pl.BlockSpec((1, BR, D), lambda b, slot, cnt: (b, 0, 0)),
            pl.BlockSpec((1, 1, BR), lambda b, slot, cnt: (b, 0, 0)),
        ]
        + [_tile_spec(k) for k in range(K)],
        out_specs=[
            pl.BlockSpec((1, 1, BR), lambda b, slot, cnt: (b, 0, 0)),
            pl.BlockSpec((1, K, BR, TILE), lambda b, slot, cnt: (b, 0, 0, 0)),
            pl.BlockSpec(memory_space=pl.ANY),
        ],
        scratch_shapes=[
            pltpu.VMEM((parts, K, D // parts, TILE), jnp.bfloat16),
            pltpu.SemaphoreType.DMA((K,)),
        ],
    )
    return pl.pallas_call(
        _score_kernel,
        grid_spec=grid_spec,
        out_shape=[
            jax.ShapeDtypeStruct((blocks, 1, BR), jnp.float32),
            jax.ShapeDtypeStruct((blocks, K, BR, TILE), jnp.bfloat16),
            jax.ShapeDtypeStruct((parts, pairs, D // parts, TILE), jnp.bfloat16),
        ],
        compiler_params=pltpu.CompilerParams(vmem_limit_bytes=48 * 1024 * 1024),
    )(slot_of, tile_count, emb_blocks, pos_cols, *([fetched] * K))


def embed_step(slot_of, emb_blocks, scores, fetched):
    blocks = emb_blocks.shape[0]
    grid_spec = pltpu.PrefetchScalarGridSpec(
        num_scalar_prefetch=1,
        grid=(blocks,),
        in_specs=[
            pl.BlockSpec((1, BR, D), lambda b, slot: (b, 0, 0)),
            pl.BlockSpec((1, K, BR, TILE), lambda b, slot: (b, 0, 0, 0)),
        ]
        + [_tile_spec(k) for k in range(K)],
        out_specs=pl.BlockSpec((1, BR, D), lambda b, slot: (b, 0, 0)),
    )
    flops = blocks * K * 2 * BR * TILE * D
    return pl.pallas_call(
        _embed_kernel,
        grid_spec=grid_spec,
        out_shape=jax.ShapeDtypeStruct((blocks, BR, D), jnp.bfloat16),
        compiler_params=pltpu.CompilerParams(vmem_limit_bytes=48 * 1024 * 1024),
        cost_estimate=pl.CostEstimate(
            flops=flops, transcendentals=0, bytes_accessed=blocks * (K + 3) * TILE * D * 2
        ),
    )(slot_of, emb_blocks, scores, *([fetched] * K))


def _column_sum_kernel(ids_ref, piece_ref, out_ref):
    step = pl.program_id(0)
    chunk = piece_ref.shape[0]

    @pl.when(step == 0)
    def _():
        out_ref[...] = jnp.zeros_like(out_ref)

    def body(j, carry):
        start = pl.multiple_of(ids_ref[step * chunk + j] * TILE, TILE)
        window = pl.ds(start, TILE)
        out_ref[:, window] += piece_ref[j].astype(jnp.float32)
        return carry

    lax.fori_loop(0, chunk, body, 0, unroll=8)


def column_sum(got_ids, pieces, tile_dev, chunk=64):
    count, width, _ = pieces.shape
    grid_spec = pltpu.PrefetchScalarGridSpec(
        num_scalar_prefetch=1,
        grid=(count // chunk,),
        in_specs=[pl.BlockSpec((chunk, width, TILE), lambda s, ids: (s, 0, 0))],
        out_specs=pl.BlockSpec((width, tile_dev * TILE), lambda s, ids: (0, 0)),
    )
    return pl.pallas_call(
        _column_sum_kernel,
        grid_spec=grid_spec,
        out_shape=jax.ShapeDtypeStruct((width, tile_dev * TILE), jnp.float32),
    )(got_ids, pieces)


def per_device(embeddings, proxies, hard_tiles, tile_count, labels):
    blocks = hard_tiles.shape[0]
    pair_count = blocks * K
    groups = lax.axis_size("cls")
    capacity = pair_count // groups
    tile_dev = proxies.shape[0] // TILE
    flat_tiles = hard_tiles.reshape(pair_count)
    owners = flat_tiles // tile_dev
    local_ids = flat_tiles % tile_dev
    counter = jnp.arange(pair_count, dtype=jnp.int32)
    same_owner = owners[:, None] == owners[None, :]
    earlier = counter[None, :] < counter[:, None]
    rank_order = jnp.sum(jnp.where(same_owner & earlier, 1, 0), axis=1).astype(jnp.int32)
    slot_of = owners * capacity + rank_order
    holder = jnp.sum(jnp.where(slot_of[None, :] == counter[:, None], counter[None, :], 0), axis=1)
    request_ids = local_ids[holder].reshape(groups, capacity)
    tile_table = proxies.reshape(tile_dev, TILE, D)
    wanted = cls_all_to_all(request_ids, 0)
    outgoing = tile_table[wanted]
    fetched = lax.all_to_all(outgoing, "cls", split_axis=0, concat_axis=0, tiled=True)
    fetched = fetched.reshape(pair_count, TILE, D)
    pos_cols = labels.reshape(blocks, 1, BR) - hard_tiles[:, None, 0:1] * TILE
    parts = lax.axis_size("dp")
    emb_blocks = embeddings.reshape(blocks, BR, D)
    loss, scores, pair_grads = score_step(slot_of, tile_count, emb_blocks, pos_cols, fetched, parts)
    embed_grad = embed_step(slot_of, emb_blocks, scores, fetched)
    pair_grads = pair_grads.reshape(parts * groups, capacity, D // parts, TILE)
    returned = lax.all_to_all(pair_grads, ("dp", "cls"), split_axis=0, concat_axis=0, tiled=True)
    got_ids = lax.all_gather(wanted, "dp").reshape(parts * pair_count)
    got_terms = returned.reshape(parts * pair_count, D // parts, TILE)
    proxy_share = column_sum(got_ids, got_terms, tile_dev).T
    return (loss.reshape(-1), embed_grad.reshape(-1, D), proxy_share)


def solution(mesh):
    placed = (
        P(("dp", "cls"), None),
        P("cls", None),
        P(("dp", "cls"), None),
        P(("dp", "cls")),
        P(("dp", "cls")),
    )
    return jax.shard_map(
        per_device,
        mesh=mesh,
        in_specs=placed,
        out_specs=(P(("dp", "cls")), P(("dp", "cls"), None), P("cls", "dp")),
        check_vma=False,
    )
```

```python
import functools

import jax
import jax.numpy as jnp
from jax import lax
from jax.experimental import pallas as pl
from jax.experimental.pallas import tpu as pltpu
from jax.sharding import PartitionSpec as P

D = 512
TILE = 128
BR = 128
K = 8


MESH = pl.DeviceIdType.MESH


def _a2a_kernel(n, src_ref, out_ref, send_sem, recv_sem, local_sem):
    me = lax.axis_index("cls")
    row = lax.axis_index("dp")
    barrier = pltpu.get_barrier_semaphore()

    def greet(j, carry):
        peer = lax.rem(me + j, n)
        pl.semaphore_signal(barrier, inc=1, device_id=(row, peer), device_id_type=MESH)
        return carry

    lax.fori_loop(1, n, greet, 0)
    pl.semaphore_wait(barrier, n - 1)
    local = pltpu.make_async_copy(src_ref.at[me], out_ref.at[me], local_sem)
    local.start()

    def remote(j):
        peer = lax.rem(me + j, n)
        return pltpu.make_async_remote_copy(
            src_ref=src_ref.at[peer],
            dst_ref=out_ref.at[me],
            send_sem=send_sem.at[j],
            recv_sem=recv_sem.at[j],
            device_id=(row, peer),
            device_id_type=MESH,
        )

    def launch(j, carry):
        remote(j).start()
        return carry

    def finish(j, carry):
        remote(j).wait()
        return carry

    lax.fori_loop(1, n, launch, 0)
    lax.fori_loop(1, n, finish, 0)
    local.wait()


def cls_all_to_all(x, cid):
    n = x.shape[0]
    return pl.pallas_call(
        functools.partial(_a2a_kernel, n),
        out_shape=jax.ShapeDtypeStruct(x.shape, x.dtype),
        in_specs=[pl.BlockSpec(memory_space=pl.ANY)],
        out_specs=pl.BlockSpec(memory_space=pl.ANY),
        scratch_shapes=[
            pltpu.SemaphoreType.DMA((n,)),
            pltpu.SemaphoreType.DMA((n,)),
            pltpu.SemaphoreType.DMA,
        ],
        compiler_params=pltpu.CompilerParams(collective_id=cid, has_side_effects=True),
    )(x)


logit_scale = 4.0
epsilon = 1e-06


def _score_kernel(slot_ref, count_ref, emb_ref, pos_ref, *rest):
    tiles = rest[:K]
    loss_ref, score_ref, pair_hbm, pair_buf, pair_sem = rest[K:]
    b = pl.program_id(0)
    last = pl.num_programs(0) - 1

    def pending(par, k, slot):
        return pltpu.make_async_copy(
            pair_buf.at[par, :, pl.ds(k, 1)],
            pair_hbm.at[:, pl.ds(slot, 1)],
            pair_sem.at[par, k],
        )
    emb = emb_ref[0].astype(jnp.float32)
    inverse_norm = lax.rsqrt(jnp.sum(emb * emb, axis=1, keepdims=True) + epsilon)
    unit_t = (emb * inverse_norm).astype(jnp.bfloat16).T
    count = count_ref[b]
    classes = lax.broadcasted_iota(jnp.int32, (TILE, BR), 0)
    hit = classes == pos_ref[0]
    logits = []
    for k in range(K):
        logits.append(logit_scale * jnp.dot(tiles[k][0], unit_t, preferred_element_type=jnp.float32))
    masked = [jnp.where(k < count, logits[k], -1e30) for k in range(K)]
    peak = masked[0].max(axis=0, keepdims=True)
    for k in range(1, K):
        peak = jnp.maximum(peak, masked[k].max(axis=0, keepdims=True))
    shifted = [jnp.exp(masked[k] - peak) for k in range(K)]
    total = jnp.zeros_like(peak)
    for k in range(K):
        total = total + jnp.sum(shifted[k], axis=0, keepdims=True)
    log_total = peak + jnp.log(total)
    positive = jnp.sum(jnp.where(hit, logits[0], 0.0), axis=0, keepdims=True)
    loss_ref[0] = log_total - positive
    inverse_total = 1.0 / total
    parity = b % 2

    @pl.when(b >= 2)
    def _():
        for k in range(K):
            pending(parity, k, 0).wait()

    for k in range(K):
        probabilities = shifted[k] * inverse_total
        if k == 0:
            probabilities = probabilities - jnp.where(hit, 1.0, 0.0)
        dscore = (logit_scale * probabilities).astype(jnp.bfloat16).T
        score_ref[0, k] = dscore
        pair_t = jnp.dot(unit_t, dscore, preferred_element_type=jnp.float32).astype(jnp.bfloat16)
        pair_buf[parity, :, k] = pair_t.reshape(pair_buf.shape[1], D // pair_buf.shape[1], TILE)
    for k in range(K):
        pending(parity, k, slot_ref[b * K + k]).start()

    @pl.when(b == last)
    def _():
        for k in range(K):
            pending(parity, k, 0).wait()

    @pl.when((b == last) & (b >= 1))
    def _():
        for k in range(K):
            pending(1 - parity, k, 0).wait()


def _embed_kernel(slot_ref, emb_ref, score_ref, *rest):
    tiles = rest[:K]
    (grad_ref,) = rest[K:]
    emb = emb_ref[0].astype(jnp.float32)
    inverse_norm = lax.rsqrt(jnp.sum(emb * emb, axis=1, keepdims=True) + epsilon)
    unit_exact = emb * inverse_norm
    grad_unit = jnp.zeros((BR, D), jnp.float32)
    for k in range(K):
        terms = jnp.dot(score_ref[0, k], tiles[k][0], preferred_element_type=jnp.float32)
        grad_unit = grad_unit + terms.astype(jnp.bfloat16).astype(jnp.float32)
    radial = jnp.sum(unit_exact * grad_unit, axis=1, keepdims=True)
    grad_ref[0] = ((grad_unit - unit_exact * radial) * inverse_norm).astype(grad_ref.dtype)


def _tile_spec(k):
    return pl.BlockSpec((1, TILE, D), lambda b, slot, *_: (slot[b * K + k], 0, 0))


def score_step(slot_of, tile_count, emb_blocks, pos_cols, fetched, parts):
    blocks = emb_blocks.shape[0]
    pairs = fetched.shape[0]
    grid_spec = pltpu.PrefetchScalarGridSpec(
        num_scalar_prefetch=2,
        grid=(blocks,),
        in_specs=[
            pl.BlockSpec((1, BR, D), lambda b, slot, cnt: (b, 0, 0)),
            pl.BlockSpec((1, 1, BR), lambda b, slot, cnt: (b, 0, 0)),
        ]
        + [_tile_spec(k) for k in range(K)],
        out_specs=[
            pl.BlockSpec((1, 1, BR), lambda b, slot, cnt: (b, 0, 0)),
            pl.BlockSpec((1, K, BR, TILE), lambda b, slot, cnt: (b, 0, 0, 0)),
            pl.BlockSpec(memory_space=pl.ANY),
        ],
        scratch_shapes=[
            pltpu.VMEM((2, parts, K, D // parts, TILE), jnp.bfloat16),
            pltpu.SemaphoreType.DMA((2, K)),
        ],
    )
    return pl.pallas_call(
        _score_kernel,
        grid_spec=grid_spec,
        out_shape=[
            jax.ShapeDtypeStruct((blocks, 1, BR), jnp.float32),
            jax.ShapeDtypeStruct((blocks, K, BR, TILE), jnp.bfloat16),
            jax.ShapeDtypeStruct((parts, pairs, D // parts, TILE), jnp.bfloat16),
        ],
        compiler_params=pltpu.CompilerParams(vmem_limit_bytes=48 * 1024 * 1024),
    )(slot_of, tile_count, emb_blocks, pos_cols, *([fetched] * K))


def embed_step(slot_of, emb_blocks, scores, fetched):
    blocks = emb_blocks.shape[0]
    grid_spec = pltpu.PrefetchScalarGridSpec(
        num_scalar_prefetch=1,
        grid=(blocks,),
        in_specs=[
            pl.BlockSpec((1, BR, D), lambda b, slot: (b, 0, 0)),
            pl.BlockSpec((1, K, BR, TILE), lambda b, slot: (b, 0, 0, 0)),
        ]
        + [_tile_spec(k) for k in range(K)],
        out_specs=pl.BlockSpec((1, BR, D), lambda b, slot: (b, 0, 0)),
    )
    flops = blocks * K * 2 * BR * TILE * D
    return pl.pallas_call(
        _embed_kernel,
        grid_spec=grid_spec,
        out_shape=jax.ShapeDtypeStruct((blocks, BR, D), jnp.bfloat16),
        compiler_params=pltpu.CompilerParams(vmem_limit_bytes=48 * 1024 * 1024),
        cost_estimate=pl.CostEstimate(
            flops=flops, transcendentals=0, bytes_accessed=blocks * (K + 3) * TILE * D * 2
        ),
    )(slot_of, emb_blocks, scores, *([fetched] * K))


def _column_sum_kernel(ids_ref, piece_ref, out_ref):
    step = pl.program_id(0)
    chunk = piece_ref.shape[0]

    @pl.when(step == 0)
    def _():
        out_ref[...] = jnp.zeros_like(out_ref)

    def body(j, carry):
        start = pl.multiple_of(ids_ref[step * chunk + j] * TILE, TILE)
        window = pl.ds(start, TILE)
        out_ref[:, window] += piece_ref[j].astype(jnp.float32)
        return carry

    lax.fori_loop(0, chunk, body, 0, unroll=8)


def column_sum(got_ids, pieces, tile_dev, chunk=64):
    count, width, _ = pieces.shape
    grid_spec = pltpu.PrefetchScalarGridSpec(
        num_scalar_prefetch=1,
        grid=(count // chunk,),
        in_specs=[pl.BlockSpec((chunk, width, TILE), lambda s, ids: (s, 0, 0))],
        out_specs=pl.BlockSpec((width, tile_dev * TILE), lambda s, ids: (0, 0)),
    )
    return pl.pallas_call(
        _column_sum_kernel,
        grid_spec=grid_spec,
        out_shape=jax.ShapeDtypeStruct((width, tile_dev * TILE), jnp.float32),
    )(got_ids, pieces)


def per_device(embeddings, proxies, hard_tiles, tile_count, labels):
    blocks = hard_tiles.shape[0]
    pair_count = blocks * K
    groups = lax.axis_size("cls")
    capacity = pair_count // groups
    tile_dev = proxies.shape[0] // TILE
    flat_tiles = hard_tiles.reshape(pair_count)
    owners = flat_tiles // tile_dev
    local_ids = flat_tiles % tile_dev
    counter = jnp.arange(pair_count, dtype=jnp.int32)
    same_owner = owners[:, None] == owners[None, :]
    earlier = counter[None, :] < counter[:, None]
    rank_order = jnp.sum(jnp.where(same_owner & earlier, 1, 0), axis=1).astype(jnp.int32)
    slot_of = owners * capacity + rank_order
    holder = jnp.sum(jnp.where(slot_of[None, :] == counter[:, None], counter[None, :], 0), axis=1)
    request_ids = local_ids[holder].reshape(groups, capacity)
    tile_table = proxies.reshape(tile_dev, TILE, D)
    wanted = cls_all_to_all(request_ids, 0)
    outgoing = tile_table[wanted]
    fetched = lax.all_to_all(outgoing, "cls", split_axis=0, concat_axis=0, tiled=True)
    fetched = fetched.reshape(pair_count, TILE, D)
    pos_cols = labels.reshape(blocks, 1, BR) - hard_tiles[:, None, 0:1] * TILE
    parts = lax.axis_size("dp")
    emb_blocks = embeddings.reshape(blocks, BR, D)
    loss, scores, pair_grads = score_step(slot_of, tile_count, emb_blocks, pos_cols, fetched, parts)
    embed_grad = embed_step(slot_of, emb_blocks, scores, fetched)
    pair_grads = pair_grads.reshape(parts * groups, capacity, D // parts, TILE)
    returned = lax.all_to_all(pair_grads, ("dp", "cls"), split_axis=0, concat_axis=0, tiled=True)
    got_ids = lax.all_gather(wanted, "dp").reshape(parts * pair_count)
    got_terms = returned.reshape(parts * pair_count, D // parts, TILE)
    proxy_share = column_sum(got_ids, got_terms, tile_dev).T
    return (loss.reshape(-1), embed_grad.reshape(-1, D), proxy_share)


def solution(mesh):
    placed = (
        P(("dp", "cls"), None),
        P("cls", None),
        P(("dp", "cls"), None),
        P(("dp", "cls")),
        P(("dp", "cls")),
    )
    return jax.shard_map(
        per_device,
        mesh=mesh,
        in_specs=placed,
        out_specs=(P(("dp", "cls")), P(("dp", "cls"), None), P("cls", "dp")),
        check_vma=False,
    )
```

```python
import functools

import jax
import jax.numpy as jnp
from jax import lax
from jax.experimental import pallas as pl
from jax.experimental.pallas import tpu as pltpu
from jax.sharding import PartitionSpec as P

D = 512
TILE = 128
BR = 128
K = 8


MESH = pl.DeviceIdType.MESH


def _a2a_kernel(n, src_ref, out_ref, send_sem, recv_sem, local_sem):
    me = lax.axis_index("cls")
    row = lax.axis_index("dp")
    barrier = pltpu.get_barrier_semaphore()

    def greet(j, carry):
        peer = lax.rem(me + j, n)
        pl.semaphore_signal(barrier, inc=1, device_id=(row, peer), device_id_type=MESH)
        return carry

    lax.fori_loop(1, n, greet, 0)
    pl.semaphore_wait(barrier, n - 1)
    local = pltpu.make_async_copy(src_ref.at[me], out_ref.at[me], local_sem)
    local.start()

    def remote(j):
        peer = lax.rem(me + j, n)
        return pltpu.make_async_remote_copy(
            src_ref=src_ref.at[peer],
            dst_ref=out_ref.at[me],
            send_sem=send_sem.at[j],
            recv_sem=recv_sem.at[j],
            device_id=(row, peer),
            device_id_type=MESH,
        )

    def launch(j, carry):
        remote(j).start()
        return carry

    def finish(j, carry):
        remote(j).wait()
        return carry

    lax.fori_loop(1, n, launch, 0)
    lax.fori_loop(1, n, finish, 0)
    local.wait()


def cls_all_to_all(x, cid):
    n = x.shape[0]
    return pl.pallas_call(
        functools.partial(_a2a_kernel, n),
        out_shape=jax.ShapeDtypeStruct(x.shape, x.dtype),
        in_specs=[pl.BlockSpec(memory_space=pl.ANY)],
        out_specs=pl.BlockSpec(memory_space=pl.ANY),
        scratch_shapes=[
            pltpu.SemaphoreType.DMA((n,)),
            pltpu.SemaphoreType.DMA((n,)),
            pltpu.SemaphoreType.DMA,
        ],
        compiler_params=pltpu.CompilerParams(collective_id=cid, has_side_effects=True),
    )(x)


logit_scale = 4.0
epsilon = 1e-06


def _score_kernel(slot_ref, count_ref, emb_ref, pos_ref, *rest):
    tiles = rest[:K]
    loss_ref, score_ref, pair_hbm, pair_buf, pair_sem = rest[K:]
    b = pl.program_id(0)
    last = pl.num_programs(0) - 1

    def pending(par, k, slot):
        return pltpu.make_async_copy(
            pair_buf.at[par, :, pl.ds(k, 1)],
            pair_hbm.at[:, pl.ds(slot, 1)],
            pair_sem.at[par, k],
        )
    emb = emb_ref[0].astype(jnp.float32)
    inverse_norm = lax.rsqrt(jnp.sum(emb * emb, axis=1, keepdims=True) + epsilon)
    unit_t = (emb * inverse_norm).astype(jnp.bfloat16).T
    count = count_ref[b]
    classes = lax.broadcasted_iota(jnp.int32, (TILE, BR), 0)
    hit = classes == pos_ref[0]
    logits = []
    for k in range(K):
        logits.append(logit_scale * jnp.dot(tiles[k][0], unit_t, preferred_element_type=jnp.float32))
    masked = [jnp.where(k < count, logits[k], -1e30) for k in range(K)]
    peak = masked[0].max(axis=0, keepdims=True)
    for k in range(1, K):
        peak = jnp.maximum(peak, masked[k].max(axis=0, keepdims=True))
    shifted = [jnp.exp(masked[k] - peak) for k in range(K)]
    total = jnp.zeros_like(peak)
    for k in range(K):
        total = total + jnp.sum(shifted[k], axis=0, keepdims=True)
    log_total = peak + jnp.log(total)
    positive = jnp.sum(jnp.where(hit, logits[0], 0.0), axis=0, keepdims=True)
    loss_ref[0] = log_total - positive
    inverse_total = 1.0 / total
    parity = b % 2

    @pl.when(b >= 2)
    def _():
        for k in range(K):
            pending(parity, k, 0).wait()

    for k in range(K):
        probabilities = shifted[k] * inverse_total
        if k == 0:
            probabilities = probabilities - jnp.where(hit, 1.0, 0.0)
        dscore = (logit_scale * probabilities).astype(jnp.bfloat16).T
        score_ref[0, k] = dscore
        pair_t = jnp.dot(unit_t, dscore, preferred_element_type=jnp.float32).astype(jnp.bfloat16)
        pair_buf[parity, :, k] = pair_t.reshape(pair_buf.shape[1], D // pair_buf.shape[1], TILE)
    for k in range(K):
        pending(parity, k, slot_ref[b * K + k]).start()

    @pl.when(b == last)
    def _():
        for k in range(K):
            pending(parity, k, 0).wait()

    @pl.when((b == last) & (b >= 1))
    def _():
        for k in range(K):
            pending(1 - parity, k, 0).wait()


def _embed_kernel(slot_ref, emb_ref, score_ref, *rest):
    tiles = rest[:K]
    (grad_ref,) = rest[K:]
    emb = emb_ref[0].astype(jnp.float32)
    inverse_norm = lax.rsqrt(jnp.sum(emb * emb, axis=1, keepdims=True) + epsilon)
    unit_exact = emb * inverse_norm
    grad_unit = jnp.zeros((BR, D), jnp.float32)
    for k in range(K):
        terms = jnp.dot(score_ref[0, k], tiles[k][0], preferred_element_type=jnp.float32)
        grad_unit = grad_unit + terms.astype(jnp.bfloat16).astype(jnp.float32)
    radial = jnp.sum(unit_exact * grad_unit, axis=1, keepdims=True)
    grad_ref[0] = ((grad_unit - unit_exact * radial) * inverse_norm).astype(grad_ref.dtype)


def _tile_spec(k):
    return pl.BlockSpec((1, TILE, D), lambda b, slot, *_: (slot[b * K + k], 0, 0))


def score_step(slot_of, tile_count, emb_blocks, pos_cols, fetched, parts):
    blocks = emb_blocks.shape[0]
    pairs = fetched.shape[0]
    grid_spec = pltpu.PrefetchScalarGridSpec(
        num_scalar_prefetch=2,
        grid=(blocks,),
        in_specs=[
            pl.BlockSpec((1, BR, D), lambda b, slot, cnt: (b, 0, 0)),
            pl.BlockSpec((1, 1, BR), lambda b, slot, cnt: (b, 0, 0)),
        ]
        + [_tile_spec(k) for k in range(K)],
        out_specs=[
            pl.BlockSpec((1, 1, BR), lambda b, slot, cnt: (b, 0, 0)),
            pl.BlockSpec((1, K, BR, TILE), lambda b, slot, cnt: (b, 0, 0, 0)),
            pl.BlockSpec(memory_space=pl.ANY),
        ],
        scratch_shapes=[
            pltpu.VMEM((2, parts, K, D // parts, TILE), jnp.bfloat16),
            pltpu.SemaphoreType.DMA((2, K)),
        ],
    )
    return pl.pallas_call(
        _score_kernel,
        grid_spec=grid_spec,
        out_shape=[
            jax.ShapeDtypeStruct((blocks, 1, BR), jnp.float32),
            jax.ShapeDtypeStruct((blocks, K, BR, TILE), jnp.bfloat16),
            jax.ShapeDtypeStruct((parts, pairs, D // parts, TILE), jnp.bfloat16),
        ],
        compiler_params=pltpu.CompilerParams(vmem_limit_bytes=48 * 1024 * 1024),
    )(slot_of, tile_count, emb_blocks, pos_cols, *([fetched] * K))


def embed_step(slot_of, emb_blocks, scores, fetched):
    blocks = emb_blocks.shape[0]
    grid_spec = pltpu.PrefetchScalarGridSpec(
        num_scalar_prefetch=1,
        grid=(blocks,),
        in_specs=[
            pl.BlockSpec((1, BR, D), lambda b, slot: (b, 0, 0)),
            pl.BlockSpec((1, K, BR, TILE), lambda b, slot: (b, 0, 0, 0)),
        ]
        + [_tile_spec(k) for k in range(K)],
        out_specs=pl.BlockSpec((1, BR, D), lambda b, slot: (b, 0, 0)),
    )
    flops = blocks * K * 2 * BR * TILE * D
    return pl.pallas_call(
        _embed_kernel,
        grid_spec=grid_spec,
        out_shape=jax.ShapeDtypeStruct((blocks, BR, D), jnp.bfloat16),
        compiler_params=pltpu.CompilerParams(vmem_limit_bytes=48 * 1024 * 1024),
        cost_estimate=pl.CostEstimate(
            flops=flops, transcendentals=0, bytes_accessed=blocks * (K + 3) * TILE * D * 2
        ),
    )(slot_of, emb_blocks, scores, *([fetched] * K))


def _column_sum_kernel(ids_ref, piece_ref, out_ref):
    step = pl.program_id(0)
    chunk = piece_ref.shape[0]

    @pl.when(step == 0)
    def _():
        out_ref[...] = jnp.zeros_like(out_ref)

    def body(j, carry):
        start = pl.multiple_of(ids_ref[step * chunk + j] * TILE, TILE)
        window = pl.ds(start, TILE)
        out_ref[:, window] += piece_ref[j].astype(jnp.float32)
        return carry

    lax.fori_loop(0, chunk, body, 0, unroll=8)


def column_sum(got_ids, pieces, tile_dev, chunk=64):
    count, width, _ = pieces.shape
    grid_spec = pltpu.PrefetchScalarGridSpec(
        num_scalar_prefetch=1,
        grid=(count // chunk,),
        in_specs=[pl.BlockSpec((chunk, width, TILE), lambda s, ids: (s, 0, 0))],
        out_specs=pl.BlockSpec((width, tile_dev * TILE), lambda s, ids: (0, 0)),
    )
    return pl.pallas_call(
        _column_sum_kernel,
        grid_spec=grid_spec,
        out_shape=jax.ShapeDtypeStruct((width, tile_dev * TILE), jnp.float32),
    )(got_ids, pieces)


def per_device(embeddings, proxies, hard_tiles, tile_count, labels):
    blocks = hard_tiles.shape[0]
    pair_count = blocks * K
    groups = lax.axis_size("cls")
    capacity = pair_count // groups
    tile_dev = proxies.shape[0] // TILE
    flat_tiles = hard_tiles.reshape(pair_count)
    owners = flat_tiles // tile_dev
    local_ids = flat_tiles % tile_dev
    counter = jnp.arange(pair_count, dtype=jnp.int32)
    same_owner = owners[:, None] == owners[None, :]
    earlier = counter[None, :] < counter[:, None]
    rank_order = jnp.sum(jnp.where(same_owner & earlier, 1, 0), axis=1).astype(jnp.int32)
    slot_of = owners * capacity + rank_order
    holder = jnp.sum(jnp.where(slot_of[None, :] == counter[:, None], counter[None, :], 0), axis=1)
    request_ids = local_ids[holder].reshape(groups, capacity)
    tile_table = proxies.reshape(tile_dev, TILE, D)
    wanted = cls_all_to_all(request_ids, 0)
    outgoing = tile_table[wanted]
    got_ids = lax.all_gather(wanted, "dp").reshape(-1)
    fetched = lax.all_to_all(outgoing, "cls", split_axis=0, concat_axis=0, tiled=True)
    fetched, got_ids = lax.optimization_barrier((fetched, got_ids))
    fetched = fetched.reshape(pair_count, TILE, D)
    pos_cols = labels.reshape(blocks, 1, BR) - hard_tiles[:, None, 0:1] * TILE
    parts = lax.axis_size("dp")
    emb_blocks = embeddings.reshape(blocks, BR, D)
    loss, scores, pair_grads = score_step(slot_of, tile_count, emb_blocks, pos_cols, fetched, parts)
    embed_grad = embed_step(slot_of, emb_blocks, scores, fetched)
    pair_grads = pair_grads.reshape(parts * groups, capacity, D // parts, TILE)
    returned = lax.all_to_all(pair_grads, ("dp", "cls"), split_axis=0, concat_axis=0, tiled=True)
    got_terms = returned.reshape(parts * pair_count, D // parts, TILE)
    proxy_share = column_sum(got_ids, got_terms, tile_dev).T
    return (loss.reshape(-1), embed_grad.reshape(-1, D), proxy_share)


def solution(mesh):
    placed = (
        P(("dp", "cls"), None),
        P("cls", None),
        P(("dp", "cls"), None),
        P(("dp", "cls")),
        P(("dp", "cls")),
    )
    return jax.shard_map(
        per_device,
        mesh=mesh,
        in_specs=placed,
        out_specs=(P(("dp", "cls")), P(("dp", "cls"), None), P("cls", "dp")),
        check_vma=False,
    )
```

```python
import functools

import jax
import jax.numpy as jnp
from jax import lax
from jax.experimental import pallas as pl
from jax.experimental.pallas import tpu as pltpu
from jax.sharding import PartitionSpec as P

D = 512
TILE = 128
BR = 128
K = 8


MESH = pl.DeviceIdType.MESH


def _a2a_kernel(n, src_ref, out_ref, send_sem, recv_sem, local_sem):
    me = lax.axis_index("cls")
    row = lax.axis_index("dp")
    local = pltpu.make_async_copy(src_ref.at[me], out_ref.at[me], local_sem)
    local.start()

    def remote(j):
        peer = lax.rem(me + j, n)
        return pltpu.make_async_remote_copy(
            src_ref=src_ref.at[peer],
            dst_ref=out_ref.at[me],
            send_sem=send_sem.at[j],
            recv_sem=recv_sem.at[j],
            device_id=(row, peer),
            device_id_type=MESH,
        )

    def launch(j, carry):
        remote(j).start()
        return carry

    def finish(j, carry):
        remote(j).wait()
        return carry

    lax.fori_loop(1, n, launch, 0)
    lax.fori_loop(1, n, finish, 0)
    local.wait()


def cls_all_to_all(x):
    n = x.shape[0]
    return pl.pallas_call(
        functools.partial(_a2a_kernel, n),
        out_shape=jax.ShapeDtypeStruct(x.shape, x.dtype),
        in_specs=[pl.BlockSpec(memory_space=pl.ANY)],
        out_specs=pl.BlockSpec(memory_space=pl.ANY),
        scratch_shapes=[
            pltpu.SemaphoreType.DMA((n,)),
            pltpu.SemaphoreType.DMA((n,)),
            pltpu.SemaphoreType.DMA,
        ],
        compiler_params=pltpu.CompilerParams(has_side_effects=True),
    )(x)


logit_scale = 4.0
epsilon = 1e-06


def _score_kernel(slot_ref, count_ref, emb_ref, pos_ref, *rest):
    tiles = rest[:K]
    loss_ref, score_ref, pair_hbm, pair_buf, pair_sem = rest[K:]
    b = pl.program_id(0)
    last = pl.num_programs(0) - 1

    def pending(par, k, slot):
        return pltpu.make_async_copy(
            pair_buf.at[par, :, pl.ds(k, 1)],
            pair_hbm.at[:, pl.ds(slot, 1)],
            pair_sem.at[par, k],
        )
    emb = emb_ref[0].astype(jnp.float32)
    inverse_norm = lax.rsqrt(jnp.sum(emb * emb, axis=1, keepdims=True) + epsilon)
    unit_t = (emb * inverse_norm).astype(jnp.bfloat16).T
    count = count_ref[b]
    classes = lax.broadcasted_iota(jnp.int32, (TILE, BR), 0)
    hit = classes == pos_ref[0]
    logits = []
    for k in range(K):
        logits.append(logit_scale * jnp.dot(tiles[k][0], unit_t, preferred_element_type=jnp.float32))
    masked = [jnp.where(k < count, logits[k], -1e30) for k in range(K)]
    peak = masked[0].max(axis=0, keepdims=True)
    for k in range(1, K):
        peak = jnp.maximum(peak, masked[k].max(axis=0, keepdims=True))
    shifted = [jnp.exp(masked[k] - peak) for k in range(K)]
    total = jnp.zeros_like(peak)
    for k in range(K):
        total = total + jnp.sum(shifted[k], axis=0, keepdims=True)
    log_total = peak + jnp.log(total)
    positive = jnp.sum(jnp.where(hit, logits[0], 0.0), axis=0, keepdims=True)
    loss_ref[0] = log_total - positive
    inverse_total = 1.0 / total
    parity = b % 2

    @pl.when(b >= 2)
    def _():
        for k in range(K):
            pending(parity, k, 0).wait()

    for k in range(K):
        probabilities = shifted[k] * inverse_total
        if k == 0:
            probabilities = probabilities - jnp.where(hit, 1.0, 0.0)
        dscore = (logit_scale * probabilities).astype(jnp.bfloat16).T
        score_ref[0, k] = dscore
        pair_t = jnp.dot(unit_t, dscore, preferred_element_type=jnp.float32).astype(jnp.bfloat16)
        pair_buf[parity, :, k] = pair_t.reshape(pair_buf.shape[1], D // pair_buf.shape[1], TILE)
    for k in range(K):
        pending(parity, k, slot_ref[b * K + k]).start()

    @pl.when(b == last)
    def _():
        for k in range(K):
            pending(parity, k, 0).wait()

    @pl.when((b == last) & (b >= 1))
    def _():
        for k in range(K):
            pending(1 - parity, k, 0).wait()


def _embed_kernel(slot_ref, emb_ref, score_ref, *rest):
    tiles = rest[:K]
    (grad_ref,) = rest[K:]
    emb = emb_ref[0].astype(jnp.float32)
    inverse_norm = lax.rsqrt(jnp.sum(emb * emb, axis=1, keepdims=True) + epsilon)
    unit_exact = emb * inverse_norm
    grad_unit = jnp.zeros((BR, D), jnp.float32)
    for k in range(K):
        terms = jnp.dot(score_ref[0, k], tiles[k][0], preferred_element_type=jnp.float32)
        grad_unit = grad_unit + terms.astype(jnp.bfloat16).astype(jnp.float32)
    radial = jnp.sum(unit_exact * grad_unit, axis=1, keepdims=True)
    grad_ref[0] = ((grad_unit - unit_exact * radial) * inverse_norm).astype(grad_ref.dtype)


def _tile_spec(k):
    return pl.BlockSpec((1, TILE, D), lambda b, slot, *_: (slot[b * K + k], 0, 0))


def score_step(slot_of, tile_count, emb_blocks, pos_cols, fetched, parts):
    blocks = emb_blocks.shape[0]
    pairs = fetched.shape[0]
    grid_spec = pltpu.PrefetchScalarGridSpec(
        num_scalar_prefetch=2,
        grid=(blocks,),
        in_specs=[
            pl.BlockSpec((1, BR, D), lambda b, slot, cnt: (b, 0, 0)),
            pl.BlockSpec((1, 1, BR), lambda b, slot, cnt: (b, 0, 0)),
        ]
        + [_tile_spec(k) for k in range(K)],
        out_specs=[
            pl.BlockSpec((1, 1, BR), lambda b, slot, cnt: (b, 0, 0)),
            pl.BlockSpec((1, K, BR, TILE), lambda b, slot, cnt: (b, 0, 0, 0)),
            pl.BlockSpec(memory_space=pl.ANY),
        ],
        scratch_shapes=[
            pltpu.VMEM((2, parts, K, D // parts, TILE), jnp.bfloat16),
            pltpu.SemaphoreType.DMA((2, K)),
        ],
    )
    return pl.pallas_call(
        _score_kernel,
        grid_spec=grid_spec,
        out_shape=[
            jax.ShapeDtypeStruct((blocks, 1, BR), jnp.float32),
            jax.ShapeDtypeStruct((blocks, K, BR, TILE), jnp.bfloat16),
            jax.ShapeDtypeStruct((parts, pairs, D // parts, TILE), jnp.bfloat16),
        ],
        compiler_params=pltpu.CompilerParams(vmem_limit_bytes=48 * 1024 * 1024),
    )(slot_of, tile_count, emb_blocks, pos_cols, *([fetched] * K))


def embed_step(slot_of, emb_blocks, scores, fetched):
    blocks = emb_blocks.shape[0]
    grid_spec = pltpu.PrefetchScalarGridSpec(
        num_scalar_prefetch=1,
        grid=(blocks,),
        in_specs=[
            pl.BlockSpec((1, BR, D), lambda b, slot: (b, 0, 0)),
            pl.BlockSpec((1, K, BR, TILE), lambda b, slot: (b, 0, 0, 0)),
        ]
        + [_tile_spec(k) for k in range(K)],
        out_specs=pl.BlockSpec((1, BR, D), lambda b, slot: (b, 0, 0)),
    )
    flops = blocks * K * 2 * BR * TILE * D
    return pl.pallas_call(
        _embed_kernel,
        grid_spec=grid_spec,
        out_shape=jax.ShapeDtypeStruct((blocks, BR, D), jnp.bfloat16),
        compiler_params=pltpu.CompilerParams(vmem_limit_bytes=48 * 1024 * 1024),
        cost_estimate=pl.CostEstimate(
            flops=flops, transcendentals=0, bytes_accessed=blocks * (K + 3) * TILE * D * 2
        ),
    )(slot_of, emb_blocks, scores, *([fetched] * K))


def _column_sum_kernel(ids_ref, piece_ref, out_ref):
    step = pl.program_id(0)
    chunk = piece_ref.shape[0]

    @pl.when(step == 0)
    def _():
        out_ref[...] = jnp.zeros_like(out_ref)

    def body(j, carry):
        start = pl.multiple_of(ids_ref[step * chunk + j] * TILE, TILE)
        window = pl.ds(start, TILE)
        out_ref[:, window] += piece_ref[j].astype(jnp.float32)
        return carry

    lax.fori_loop(0, chunk, body, 0, unroll=8)


def column_sum(got_ids, pieces, tile_dev, chunk=64):
    count, width, _ = pieces.shape
    grid_spec = pltpu.PrefetchScalarGridSpec(
        num_scalar_prefetch=1,
        grid=(count // chunk,),
        in_specs=[pl.BlockSpec((chunk, width, TILE), lambda s, ids: (s, 0, 0))],
        out_specs=pl.BlockSpec((width, tile_dev * TILE), lambda s, ids: (0, 0)),
    )
    return pl.pallas_call(
        _column_sum_kernel,
        grid_spec=grid_spec,
        out_shape=jax.ShapeDtypeStruct((width, tile_dev * TILE), jnp.float32),
    )(got_ids, pieces)


def per_device(embeddings, proxies, hard_tiles, tile_count, labels):
    blocks = hard_tiles.shape[0]
    pair_count = blocks * K
    groups = lax.axis_size("cls")
    capacity = pair_count // groups
    tile_dev = proxies.shape[0] // TILE
    flat_tiles = hard_tiles.reshape(pair_count)
    owners = flat_tiles // tile_dev
    local_ids = flat_tiles % tile_dev
    counter = jnp.arange(pair_count, dtype=jnp.int32)
    same_owner = owners[:, None] == owners[None, :]
    earlier = counter[None, :] < counter[:, None]
    rank_order = jnp.sum(jnp.where(same_owner & earlier, 1, 0), axis=1).astype(jnp.int32)
    slot_of = owners * capacity + rank_order
    holder = jnp.sum(jnp.where(slot_of[None, :] == counter[:, None], counter[None, :], 0), axis=1)
    request_ids = local_ids[holder].reshape(groups, capacity)
    tile_table = proxies.reshape(tile_dev, TILE, D)
    wanted = cls_all_to_all(request_ids)
    outgoing = tile_table[wanted]
    fetched = lax.all_to_all(outgoing, "cls", split_axis=0, concat_axis=0, tiled=True)
    fetched = fetched.reshape(pair_count, TILE, D)
    pos_cols = labels.reshape(blocks, 1, BR) - hard_tiles[:, None, 0:1] * TILE
    parts = lax.axis_size("dp")
    emb_blocks = embeddings.reshape(blocks, BR, D)
    loss, scores, pair_grads = score_step(slot_of, tile_count, emb_blocks, pos_cols, fetched, parts)
    embed_grad = embed_step(slot_of, emb_blocks, scores, fetched)
    pair_grads = pair_grads.reshape(parts * groups, capacity, D // parts, TILE)
    returned = lax.all_to_all(pair_grads, ("dp", "cls"), split_axis=0, concat_axis=0, tiled=True)
    got_ids = lax.all_gather(wanted, "dp").reshape(parts * pair_count)
    got_terms = returned.reshape(parts * pair_count, D // parts, TILE)
    proxy_share = column_sum(got_ids, got_terms, tile_dev).T
    return (loss.reshape(-1), embed_grad.reshape(-1, D), proxy_share)


def solution(mesh):
    placed = (
        P(("dp", "cls"), None),
        P("cls", None),
        P(("dp", "cls"), None),
        P(("dp", "cls")),
        P(("dp", "cls")),
    )
    return jax.shard_map(
        per_device,
        mesh=mesh,
        in_specs=placed,
        out_specs=(P(("dp", "cls")), P(("dp", "cls"), None), P("cls", "dp")),
        check_vma=False,
    )
```

```python
import functools

import jax
import jax.numpy as jnp
from jax import lax
from jax.experimental import pallas as pl
from jax.experimental.pallas import tpu as pltpu
from jax.sharding import PartitionSpec as P

D = 512
TILE = 128
BR = 128
K = 8


MESH = pl.DeviceIdType.MESH


def _a2a_kernel(n, src_ref, out_ref, send_sem, recv_sem, local_sem):
    me = lax.axis_index("cls")
    row = lax.axis_index("dp")
    barrier = pltpu.get_barrier_semaphore()

    def greet(j, carry):
        peer = lax.rem(me + j, n)
        pl.semaphore_signal(barrier, inc=1, device_id=(row, peer), device_id_type=MESH)
        return carry

    lax.fori_loop(1, n, greet, 0)
    pl.semaphore_wait(barrier, n - 1)
    local = pltpu.make_async_copy(src_ref.at[me], out_ref.at[me], local_sem)
    local.start()

    def remote(j):
        peer = lax.rem(me + j, n)
        return pltpu.make_async_remote_copy(
            src_ref=src_ref.at[peer],
            dst_ref=out_ref.at[me],
            send_sem=send_sem.at[j],
            recv_sem=recv_sem.at[j],
            device_id=(row, peer),
            device_id_type=MESH,
        )

    def launch(j, carry):
        remote(j).start()
        return carry

    def finish(j, carry):
        remote(j).wait()
        return carry

    lax.fori_loop(1, n, launch, 0)
    lax.fori_loop(1, n, finish, 0)
    local.wait()


def cls_all_to_all(x, cid):
    n = x.shape[0]
    return pl.pallas_call(
        functools.partial(_a2a_kernel, n),
        out_shape=jax.ShapeDtypeStruct(x.shape, x.dtype),
        in_specs=[pl.BlockSpec(memory_space=pl.ANY)],
        out_specs=pl.BlockSpec(memory_space=pl.ANY),
        scratch_shapes=[
            pltpu.SemaphoreType.DMA((n,)),
            pltpu.SemaphoreType.DMA((n,)),
            pltpu.SemaphoreType.DMA,
        ],
        compiler_params=pltpu.CompilerParams(collective_id=cid, has_side_effects=True),
    )(x)


logit_scale = 4.0
epsilon = 1e-06


def _block_scores(emb_ref, pos_ref, count, tiles):
    emb = emb_ref[0].astype(jnp.float32)
    inverse_norm = lax.rsqrt(jnp.sum(emb * emb, axis=1, keepdims=True) + epsilon)
    unit_exact = emb * inverse_norm
    unit_t = unit_exact.astype(jnp.bfloat16).T
    classes = lax.broadcasted_iota(jnp.int32, (TILE, BR), 0)
    hit = classes == pos_ref[0]
    logits = []
    for k in range(K):
        logits.append(logit_scale * jnp.dot(tiles[k][0], unit_t, preferred_element_type=jnp.float32))
    masked = [jnp.where(k < count, logits[k], -1e30) for k in range(K)]
    peak = masked[0].max(axis=0, keepdims=True)
    for k in range(1, K):
        peak = jnp.maximum(peak, masked[k].max(axis=0, keepdims=True))
    shifted = [jnp.exp(masked[k] - peak) for k in range(K)]
    total = jnp.zeros_like(peak)
    for k in range(K):
        total = total + jnp.sum(shifted[k], axis=0, keepdims=True)
    log_total = peak + jnp.log(total)
    positive = jnp.sum(jnp.where(hit, logits[0], 0.0), axis=0, keepdims=True)
    inverse_total = 1.0 / total
    scores = []
    for k in range(K):
        probabilities = shifted[k] * inverse_total
        if k == 0:
            probabilities = probabilities - jnp.where(hit, 1.0, 0.0)
        scores.append((logit_scale * probabilities).astype(jnp.bfloat16).T)
    return unit_exact, inverse_norm, unit_t, log_total - positive, scores


def _score_kernel(slot_ref, count_ref, emb_ref, pos_ref, *rest):
    tiles = rest[:K]
    loss_ref, pair_hbm, pair_buf, pair_sem = rest[K:]
    b = pl.program_id(0)
    last = pl.num_programs(0) - 1

    def pending(par, k, slot):
        return pltpu.make_async_copy(
            pair_buf.at[par, :, pl.ds(k, 1)],
            pair_hbm.at[:, pl.ds(slot, 1)],
            pair_sem.at[par, k],
        )

    _, _, unit_t, loss, scores = _block_scores(emb_ref, pos_ref, count_ref[b], tiles)
    loss_ref[0] = loss
    parity = b % 2

    @pl.when(b >= 2)
    def _():
        for k in range(K):
            pending(parity, k, 0).wait()

    for k in range(K):
        pair_t = jnp.dot(unit_t, scores[k], preferred_element_type=jnp.float32).astype(jnp.bfloat16)
        pair_buf[parity, :, k] = pair_t.reshape(pair_buf.shape[1], D // pair_buf.shape[1], TILE)
    for k in range(K):
        pending(parity, k, slot_ref[b * K + k]).start()

    @pl.when(b == last)
    def _():
        for k in range(K):
            pending(parity, k, 0).wait()

    @pl.when((b == last) & (b >= 1))
    def _():
        for k in range(K):
            pending(1 - parity, k, 0).wait()


def _embed_kernel(slot_ref, count_ref, emb_ref, pos_ref, *rest):
    tiles = rest[:K]
    (grad_ref,) = rest[K:]
    b = pl.program_id(0)
    unit_exact, inverse_norm, _, _, scores = _block_scores(emb_ref, pos_ref, count_ref[b], tiles)
    grad_unit = jnp.zeros((BR, D), jnp.float32)
    for k in range(K):
        terms = jnp.dot(scores[k], tiles[k][0], preferred_element_type=jnp.float32)
        grad_unit = grad_unit + terms.astype(jnp.bfloat16).astype(jnp.float32)
    radial = jnp.sum(unit_exact * grad_unit, axis=1, keepdims=True)
    grad_ref[0] = ((grad_unit - unit_exact * radial) * inverse_norm).astype(grad_ref.dtype)


def _tile_spec(k):
    return pl.BlockSpec((1, TILE, D), lambda b, slot, *_: (slot[b * K + k], 0, 0))


def score_step(slot_of, tile_count, emb_blocks, pos_cols, fetched, parts):
    blocks = emb_blocks.shape[0]
    pairs = fetched.shape[0]
    grid_spec = pltpu.PrefetchScalarGridSpec(
        num_scalar_prefetch=2,
        grid=(blocks,),
        in_specs=[
            pl.BlockSpec((1, BR, D), lambda b, slot, cnt: (b, 0, 0)),
            pl.BlockSpec((1, 1, BR), lambda b, slot, cnt: (b, 0, 0)),
        ]
        + [_tile_spec(k) for k in range(K)],
        out_specs=[
            pl.BlockSpec((1, 1, BR), lambda b, slot, cnt: (b, 0, 0)),
            pl.BlockSpec(memory_space=pl.ANY),
        ],
        scratch_shapes=[
            pltpu.VMEM((2, parts, K, D // parts, TILE), jnp.bfloat16),
            pltpu.SemaphoreType.DMA((2, K)),
        ],
    )
    return pl.pallas_call(
        _score_kernel,
        grid_spec=grid_spec,
        out_shape=[
            jax.ShapeDtypeStruct((blocks, 1, BR), jnp.float32),
            jax.ShapeDtypeStruct((parts, pairs, D // parts, TILE), jnp.bfloat16),
        ],
        compiler_params=pltpu.CompilerParams(vmem_limit_bytes=48 * 1024 * 1024),
    )(slot_of, tile_count, emb_blocks, pos_cols, *([fetched] * K))


def embed_step(slot_of, tile_count, emb_blocks, pos_cols, fetched):
    blocks = emb_blocks.shape[0]
    grid_spec = pltpu.PrefetchScalarGridSpec(
        num_scalar_prefetch=2,
        grid=(blocks,),
        in_specs=[
            pl.BlockSpec((1, BR, D), lambda b, slot, cnt: (b, 0, 0)),
            pl.BlockSpec((1, 1, BR), lambda b, slot, cnt: (b, 0, 0)),
        ]
        + [_tile_spec(k) for k in range(K)],
        out_specs=pl.BlockSpec((1, BR, D), lambda b, slot, cnt: (b, 0, 0)),
    )
    flops = blocks * K * 4 * BR * TILE * D
    return pl.pallas_call(
        _embed_kernel,
        grid_spec=grid_spec,
        out_shape=jax.ShapeDtypeStruct((blocks, BR, D), jnp.bfloat16),
        compiler_params=pltpu.CompilerParams(vmem_limit_bytes=48 * 1024 * 1024),
        cost_estimate=pl.CostEstimate(
            flops=flops, transcendentals=blocks * K * BR * TILE, bytes_accessed=blocks * (K + 2) * TILE * D * 2
        ),
    )(slot_of, tile_count, emb_blocks, pos_cols, *([fetched] * K))


def _column_sum_kernel(ids_ref, piece_ref, out_ref):
    step = pl.program_id(0)
    chunk = piece_ref.shape[0]

    @pl.when(step == 0)
    def _():
        out_ref[...] = jnp.zeros_like(out_ref)

    def body(j, carry):
        start = pl.multiple_of(ids_ref[step * chunk + j] * TILE, TILE)
        window = pl.ds(start, TILE)
        out_ref[:, window] += piece_ref[j].astype(jnp.float32)
        return carry

    lax.fori_loop(0, chunk, body, 0, unroll=8)


def column_sum(got_ids, pieces, tile_dev, chunk=64):
    count, width, _ = pieces.shape
    grid_spec = pltpu.PrefetchScalarGridSpec(
        num_scalar_prefetch=1,
        grid=(count // chunk,),
        in_specs=[pl.BlockSpec((chunk, width, TILE), lambda s, ids: (s, 0, 0))],
        out_specs=pl.BlockSpec((width, tile_dev * TILE), lambda s, ids: (0, 0)),
    )
    return pl.pallas_call(
        _column_sum_kernel,
        grid_spec=grid_spec,
        out_shape=jax.ShapeDtypeStruct((width, tile_dev * TILE), jnp.float32),
    )(got_ids, pieces)


def per_device(embeddings, proxies, hard_tiles, tile_count, labels):
    blocks = hard_tiles.shape[0]
    pair_count = blocks * K
    groups = lax.axis_size("cls")
    capacity = pair_count // groups
    tile_dev = proxies.shape[0] // TILE
    flat_tiles = hard_tiles.reshape(pair_count)
    owners = flat_tiles // tile_dev
    local_ids = flat_tiles % tile_dev
    counter = jnp.arange(pair_count, dtype=jnp.int32)
    same_owner = owners[:, None] == owners[None, :]
    earlier = counter[None, :] < counter[:, None]
    rank_order = jnp.sum(jnp.where(same_owner & earlier, 1, 0), axis=1).astype(jnp.int32)
    slot_of = owners * capacity + rank_order
    holder = jnp.sum(jnp.where(slot_of[None, :] == counter[:, None], counter[None, :], 0), axis=1)
    request_ids = local_ids[holder].reshape(groups, capacity)
    tile_table = proxies.reshape(tile_dev, TILE, D)
    wanted = cls_all_to_all(request_ids, 0)
    outgoing = tile_table[wanted]
    fetched = lax.all_to_all(outgoing, "cls", split_axis=0, concat_axis=0, tiled=True)
    fetched = fetched.reshape(pair_count, TILE, D)
    pos_cols = labels.reshape(blocks, 1, BR) - hard_tiles[:, None, 0:1] * TILE
    parts = lax.axis_size("dp")
    emb_blocks = embeddings.reshape(blocks, BR, D)
    loss, pair_grads = score_step(slot_of, tile_count, emb_blocks, pos_cols, fetched, parts)
    embed_grad = embed_step(slot_of, tile_count, emb_blocks, pos_cols, fetched)
    pair_grads = pair_grads.reshape(parts * groups, capacity, D // parts, TILE)
    returned = lax.all_to_all(pair_grads, ("dp", "cls"), split_axis=0, concat_axis=0, tiled=True)
    got_ids = lax.all_gather(wanted, "dp").reshape(parts * pair_count)
    got_terms = returned.reshape(parts * pair_count, D // parts, TILE)
    proxy_share = column_sum(got_ids, got_terms, tile_dev).T
    return (loss.reshape(-1), embed_grad.reshape(-1, D), proxy_share)


def solution(mesh):
    placed = (
        P(("dp", "cls"), None),
        P("cls", None),
        P(("dp", "cls"), None),
        P(("dp", "cls")),
        P(("dp", "cls")),
    )
    return jax.shard_map(
        per_device,
        mesh=mesh,
        in_specs=placed,
        out_specs=(P(("dp", "cls")), P(("dp", "cls"), None), P("cls", "dp")),
        check_vma=False,
    )
```

```python
import functools

import jax
import jax.numpy as jnp
from jax import lax
from jax.experimental import pallas as pl
from jax.experimental.pallas import tpu as pltpu
from jax.sharding import PartitionSpec as P

D = 512
TILE = 128
BR = 128
K = 8


MESH = pl.DeviceIdType.MESH


def _a2a_kernel(n, src_ref, out_ref, send_sem, recv_sem, local_sem):
    me = lax.axis_index("cls")
    row = lax.axis_index("dp")
    barrier = pltpu.get_barrier_semaphore()

    def greet(j, carry):
        peer = lax.rem(me + j, n)
        pl.semaphore_signal(barrier, inc=1, device_id=(row, peer), device_id_type=MESH)
        return carry

    lax.fori_loop(1, n, greet, 0)
    pl.semaphore_wait(barrier, n - 1)
    local = pltpu.make_async_copy(src_ref.at[me], out_ref.at[me], local_sem)
    local.start()

    def remote(j):
        peer = lax.rem(me + j, n)
        return pltpu.make_async_remote_copy(
            src_ref=src_ref.at[peer],
            dst_ref=out_ref.at[me],
            send_sem=send_sem.at[j],
            recv_sem=recv_sem.at[j],
            device_id=(row, peer),
            device_id_type=MESH,
        )

    def launch(j, carry):
        remote(j).start()
        return carry

    def finish(j, carry):
        remote(j).wait()
        return carry

    lax.fori_loop(1, n, launch, 0)
    lax.fori_loop(1, n, finish, 0)
    local.wait()


def cls_all_to_all(x, cid):
    n = x.shape[0]
    return pl.pallas_call(
        functools.partial(_a2a_kernel, n),
        out_shape=jax.ShapeDtypeStruct(x.shape, x.dtype),
        in_specs=[pl.BlockSpec(memory_space=pl.ANY)],
        out_specs=pl.BlockSpec(memory_space=pl.ANY),
        scratch_shapes=[
            pltpu.SemaphoreType.DMA((n,)),
            pltpu.SemaphoreType.DMA((n,)),
            pltpu.SemaphoreType.DMA,
        ],
        compiler_params=pltpu.CompilerParams(collective_id=cid, has_side_effects=True),
    )(x)


logit_scale = 4.0
epsilon = 1e-06


def _block_scores(emb_ref, pos_ref, count, tiles):
    emb = emb_ref[0].astype(jnp.float32)
    inverse_norm = lax.rsqrt(jnp.sum(emb * emb, axis=1, keepdims=True) + epsilon)
    unit_exact = emb * inverse_norm
    unit_t = unit_exact.astype(jnp.bfloat16).T
    classes = lax.broadcasted_iota(jnp.int32, (TILE, BR), 0)
    hit = classes == pos_ref[0]
    logits = []
    for k in range(K):
        logits.append(logit_scale * jnp.dot(tiles[k][0], unit_t, preferred_element_type=jnp.float32))
    masked = [jnp.where(k < count, logits[k], -1e30) for k in range(K)]
    peak = masked[0].max(axis=0, keepdims=True)
    for k in range(1, K):
        peak = jnp.maximum(peak, masked[k].max(axis=0, keepdims=True))
    shifted = [jnp.exp(masked[k] - peak) for k in range(K)]
    total = jnp.zeros_like(peak)
    for k in range(K):
        total = total + jnp.sum(shifted[k], axis=0, keepdims=True)
    log_total = peak + jnp.log(total)
    positive = jnp.sum(jnp.where(hit, logits[0], 0.0), axis=0, keepdims=True)
    inverse_total = 1.0 / total
    scores = []
    for k in range(K):
        probabilities = shifted[k] * inverse_total
        if k == 0:
            probabilities = probabilities - jnp.where(hit, 1.0, 0.0)
        scores.append((logit_scale * probabilities).astype(jnp.bfloat16).T)
    return unit_exact, inverse_norm, unit_t, log_total - positive, scores


def _score_kernel(slot_ref, count_ref, emb_ref, pos_ref, *rest):
    per_step = emb_ref.shape[0]
    tiles = rest[: per_step * K]
    loss_ref, pair_hbm, pair_buf, pair_sem = rest[per_step * K:]
    g = pl.program_id(0)
    last = pl.num_programs(0) - 1
    width = per_step * K

    def pending(par, i, slot):
        return pltpu.make_async_copy(
            pair_buf.at[par, :, pl.ds(i, 1)],
            pair_hbm.at[:, pl.ds(slot, 1)],
            pair_sem.at[par, i],
        )

    parity = g % 2

    @pl.when(g >= 2)
    def _():
        for i in range(width):
            pending(parity, i, 0).wait()

    for j in range(per_step):
        b = g * per_step + j
        block_tiles = tiles[j * K:(j + 1) * K]
        _, _, unit_t, loss, scores = _block_scores(
            emb_ref.at[pl.ds(j, 1)], pos_ref.at[pl.ds(j, 1)], count_ref[b], block_tiles
        )
        loss_ref[j] = loss
        for k in range(K):
            pair_t = jnp.dot(unit_t, scores[k], preferred_element_type=jnp.float32).astype(jnp.bfloat16)
            pair_buf[parity, :, j * K + k] = pair_t.reshape(pair_buf.shape[1], D // pair_buf.shape[1], TILE)
        for k in range(K):
            pending(parity, j * K + k, slot_ref[b * K + k]).start()

    @pl.when(g == last)
    def _():
        for i in range(width):
            pending(parity, i, 0).wait()

    @pl.when((g == last) & (g >= 1))
    def _():
        for i in range(width):
            pending(1 - parity, i, 0).wait()


def _embed_kernel(slot_ref, count_ref, emb_ref, pos_ref, *rest):
    tiles = rest[:K]
    (grad_ref,) = rest[K:]
    b = pl.program_id(0)
    unit_exact, inverse_norm, _, _, scores = _block_scores(emb_ref, pos_ref, count_ref[b], tiles)
    grad_unit = jnp.zeros((BR, D), jnp.float32)
    for k in range(K):
        terms = jnp.dot(scores[k], tiles[k][0], preferred_element_type=jnp.float32)
        grad_unit = grad_unit + terms.astype(jnp.bfloat16).astype(jnp.float32)
    radial = jnp.sum(unit_exact * grad_unit, axis=1, keepdims=True)
    grad_ref[0] = ((grad_unit - unit_exact * radial) * inverse_norm).astype(grad_ref.dtype)


def _tile_spec(k):
    return pl.BlockSpec((1, TILE, D), lambda b, slot, *_: (slot[b * K + k], 0, 0))


def score_step(slot_of, tile_count, emb_blocks, pos_cols, fetched, parts, per_step=2):
    blocks = emb_blocks.shape[0]
    pairs = fetched.shape[0]

    def step_tile_spec(i):
        j, k = divmod(i, K)
        return pl.BlockSpec(
            (1, TILE, D), lambda g, slot, cnt: (slot[(g * per_step + j) * K + k], 0, 0)
        )

    grid_spec = pltpu.PrefetchScalarGridSpec(
        num_scalar_prefetch=2,
        grid=(blocks // per_step,),
        in_specs=[
            pl.BlockSpec((per_step, BR, D), lambda g, slot, cnt: (g, 0, 0)),
            pl.BlockSpec((per_step, 1, BR), lambda g, slot, cnt: (g, 0, 0)),
        ]
        + [step_tile_spec(i) for i in range(per_step * K)],
        out_specs=[
            pl.BlockSpec((per_step, 1, BR), lambda g, slot, cnt: (g, 0, 0)),
            pl.BlockSpec(memory_space=pl.ANY),
        ],
        scratch_shapes=[
            pltpu.VMEM((2, parts, per_step * K, D // parts, TILE), jnp.bfloat16),
            pltpu.SemaphoreType.DMA((2, per_step * K)),
        ],
    )
    return pl.pallas_call(
        _score_kernel,
        grid_spec=grid_spec,
        out_shape=[
            jax.ShapeDtypeStruct((blocks, 1, BR), jnp.float32),
            jax.ShapeDtypeStruct((parts, pairs, D // parts, TILE), jnp.bfloat16),
        ],
        compiler_params=pltpu.CompilerParams(vmem_limit_bytes=48 * 1024 * 1024),
    )(slot_of, tile_count, emb_blocks, pos_cols, *([fetched] * (per_step * K)))


def embed_step(slot_of, tile_count, emb_blocks, pos_cols, fetched):
    blocks = emb_blocks.shape[0]
    grid_spec = pltpu.PrefetchScalarGridSpec(
        num_scalar_prefetch=2,
        grid=(blocks,),
        in_specs=[
            pl.BlockSpec((1, BR, D), lambda b, slot, cnt: (b, 0, 0)),
            pl.BlockSpec((1, 1, BR), lambda b, slot, cnt: (b, 0, 0)),
        ]
        + [_tile_spec(k) for k in range(K)],
        out_specs=pl.BlockSpec((1, BR, D), lambda b, slot, cnt: (b, 0, 0)),
    )
    flops = blocks * K * 4 * BR * TILE * D
    return pl.pallas_call(
        _embed_kernel,
        grid_spec=grid_spec,
        out_shape=jax.ShapeDtypeStruct((blocks, BR, D), jnp.bfloat16),
        compiler_params=pltpu.CompilerParams(vmem_limit_bytes=48 * 1024 * 1024),
        cost_estimate=pl.CostEstimate(
            flops=flops, transcendentals=blocks * K * BR * TILE, bytes_accessed=blocks * (K + 2) * TILE * D * 2
        ),
    )(slot_of, tile_count, emb_blocks, pos_cols, *([fetched] * K))


def _column_sum_kernel(ids_ref, piece_ref, out_ref):
    step = pl.program_id(0)
    chunk = piece_ref.shape[0]

    @pl.when(step == 0)
    def _():
        out_ref[...] = jnp.zeros_like(out_ref)

    def body(j, carry):
        start = pl.multiple_of(ids_ref[step * chunk + j] * TILE, TILE)
        window = pl.ds(start, TILE)
        out_ref[:, window] += piece_ref[j].astype(jnp.float32)
        return carry

    lax.fori_loop(0, chunk, body, 0, unroll=8)


def column_sum(got_ids, pieces, tile_dev, chunk=64):
    count, width, _ = pieces.shape
    grid_spec = pltpu.PrefetchScalarGridSpec(
        num_scalar_prefetch=1,
        grid=(count // chunk,),
        in_specs=[pl.BlockSpec((chunk, width, TILE), lambda s, ids: (s, 0, 0))],
        out_specs=pl.BlockSpec((width, tile_dev * TILE), lambda s, ids: (0, 0)),
    )
    return pl.pallas_call(
        _column_sum_kernel,
        grid_spec=grid_spec,
        out_shape=jax.ShapeDtypeStruct((width, tile_dev * TILE), jnp.float32),
    )(got_ids, pieces)


def per_device(embeddings, proxies, hard_tiles, tile_count, labels):
    blocks = hard_tiles.shape[0]
    pair_count = blocks * K
    groups = lax.axis_size("cls")
    capacity = pair_count // groups
    tile_dev = proxies.shape[0] // TILE
    flat_tiles = hard_tiles.reshape(pair_count)
    owners = flat_tiles // tile_dev
    local_ids = flat_tiles % tile_dev
    counter = jnp.arange(pair_count, dtype=jnp.int32)
    same_owner = owners[:, None] == owners[None, :]
    earlier = counter[None, :] < counter[:, None]
    rank_order = jnp.sum(jnp.where(same_owner & earlier, 1, 0), axis=1).astype(jnp.int32)
    slot_of = owners * capacity + rank_order
    holder = jnp.sum(jnp.where(slot_of[None, :] == counter[:, None], counter[None, :], 0), axis=1)
    request_ids = local_ids[holder].reshape(groups, capacity)
    tile_table = proxies.reshape(tile_dev, TILE, D)
    wanted = cls_all_to_all(request_ids, 0)
    outgoing = tile_table[wanted]
    fetched = lax.all_to_all(outgoing, "cls", split_axis=0, concat_axis=0, tiled=True)
    fetched = fetched.reshape(pair_count, TILE, D)
    pos_cols = labels.reshape(blocks, 1, BR) - hard_tiles[:, None, 0:1] * TILE
    parts = lax.axis_size("dp")
    emb_blocks = embeddings.reshape(blocks, BR, D)
    loss, pair_grads = score_step(slot_of, tile_count, emb_blocks, pos_cols, fetched, parts)
    embed_grad = embed_step(slot_of, tile_count, emb_blocks, pos_cols, fetched)
    pair_grads = pair_grads.reshape(parts * groups, capacity, D // parts, TILE)
    returned = lax.all_to_all(pair_grads, ("dp", "cls"), split_axis=0, concat_axis=0, tiled=True)
    got_ids = lax.all_gather(wanted, "dp").reshape(parts * pair_count)
    got_terms = returned.reshape(parts * pair_count, D // parts, TILE)
    proxy_share = column_sum(got_ids, got_terms, tile_dev).T
    return (loss.reshape(-1), embed_grad.reshape(-1, D), proxy_share)


def solution(mesh):
    placed = (
        P(("dp", "cls"), None),
        P("cls", None),
        P(("dp", "cls"), None),
        P(("dp", "cls")),
        P(("dp", "cls")),
    )
    return jax.shard_map(
        per_device,
        mesh=mesh,
        in_specs=placed,
        out_specs=(P(("dp", "cls")), P(("dp", "cls"), None), P("cls", "dp")),
        check_vma=False,
    )
```

```python
import functools

import jax
import jax.numpy as jnp
from jax import lax
from jax.experimental import pallas as pl
from jax.experimental.pallas import tpu as pltpu
from jax.sharding import PartitionSpec as P

D = 512
TILE = 128
BR = 128
K = 8


MESH = pl.DeviceIdType.MESH


def _a2a_kernel(n, src_ref, out_ref, send_sem, recv_sem, local_sem):
    me = lax.axis_index("cls")
    row = lax.axis_index("dp")
    barrier = pltpu.get_barrier_semaphore()

    def greet(j, carry):
        peer = lax.rem(me + j, n)
        pl.semaphore_signal(barrier, inc=1, device_id=(row, peer), device_id_type=MESH)
        return carry

    lax.fori_loop(1, n, greet, 0)
    pl.semaphore_wait(barrier, n - 1)
    local = pltpu.make_async_copy(src_ref.at[me], out_ref.at[me], local_sem)
    local.start()

    def remote(j):
        peer = lax.rem(me + j, n)
        return pltpu.make_async_remote_copy(
            src_ref=src_ref.at[peer],
            dst_ref=out_ref.at[me],
            send_sem=send_sem.at[j],
            recv_sem=recv_sem.at[j],
            device_id=(row, peer),
            device_id_type=MESH,
        )

    def launch(j, carry):
        remote(j).start()
        return carry

    def finish(j, carry):
        remote(j).wait()
        return carry

    lax.fori_loop(1, n, launch, 0)
    lax.fori_loop(1, n, finish, 0)
    local.wait()


def cls_all_to_all(x, cid):
    n = x.shape[0]
    return pl.pallas_call(
        functools.partial(_a2a_kernel, n),
        out_shape=jax.ShapeDtypeStruct(x.shape, x.dtype),
        in_specs=[pl.BlockSpec(memory_space=pl.ANY)],
        out_specs=pl.BlockSpec(memory_space=pl.ANY),
        scratch_shapes=[
            pltpu.SemaphoreType.DMA((n,)),
            pltpu.SemaphoreType.DMA((n,)),
            pltpu.SemaphoreType.DMA,
        ],
        compiler_params=pltpu.CompilerParams(collective_id=cid, has_side_effects=True),
    )(x)


logit_scale = 4.0
epsilon = 1e-06


def _block_scores(emb_ref, pos_ref, count, tiles):
    emb = emb_ref[0].astype(jnp.float32)
    inverse_norm = lax.rsqrt(jnp.sum(emb * emb, axis=1, keepdims=True) + epsilon)
    unit_exact = emb * inverse_norm
    unit_t = unit_exact.astype(jnp.bfloat16).T
    classes = lax.broadcasted_iota(jnp.int32, (TILE, BR), 0)
    hit = classes == pos_ref[0]
    logits = []
    for k in range(K):
        logits.append(logit_scale * jnp.dot(tiles[k][0], unit_t, preferred_element_type=jnp.float32))
    masked = [jnp.where(k < count, logits[k], -1e30) for k in range(K)]
    peak = masked[0].max(axis=0, keepdims=True)
    for k in range(1, K):
        peak = jnp.maximum(peak, masked[k].max(axis=0, keepdims=True))
    shifted = [jnp.exp(masked[k] - peak) for k in range(K)]
    total = jnp.zeros_like(peak)
    for k in range(K):
        total = total + jnp.sum(shifted[k], axis=0, keepdims=True)
    log_total = peak + jnp.log(total)
    positive = jnp.sum(jnp.where(hit, logits[0], 0.0), axis=0, keepdims=True)
    inverse_total = 1.0 / total
    scores = []
    for k in range(K):
        probabilities = shifted[k] * inverse_total
        if k == 0:
            probabilities = probabilities - jnp.where(hit, 1.0, 0.0)
        scores.append((logit_scale * probabilities).astype(jnp.bfloat16).T)
    return unit_exact, inverse_norm, unit_t, log_total - positive, scores


def _score_kernel(slot_ref, count_ref, emb_ref, pos_ref, *rest):
    per_step = emb_ref.shape[0]
    tiles = rest[: per_step * K]
    loss_ref, pair_hbm, pair_buf, pair_sem = rest[per_step * K:]
    g = pl.program_id(0)
    last = pl.num_programs(0) - 1
    width = per_step * K

    def pending(par, i, slot):
        return pltpu.make_async_copy(
            pair_buf.at[par, :, pl.ds(i, 1)],
            pair_hbm.at[:, pl.ds(slot, 1)],
            pair_sem.at[par, i],
        )

    parity = g % 2

    @pl.when(g >= 2)
    def _():
        for i in range(width):
            pending(parity, i, 0).wait()

    for j in range(per_step):
        b = g * per_step + j
        block_tiles = tiles[j * K:(j + 1) * K]
        _, _, unit_t, loss, scores = _block_scores(
            emb_ref.at[pl.ds(j, 1)], pos_ref.at[pl.ds(j, 1)], count_ref[b], block_tiles
        )
        loss_ref[j] = loss
        for k in range(K):
            pair_t = jnp.dot(unit_t, scores[k], preferred_element_type=jnp.float32).astype(jnp.bfloat16)
            pair_buf[parity, :, j * K + k] = pair_t.reshape(pair_buf.shape[1], D // pair_buf.shape[1], TILE)
        for k in range(K):
            pending(parity, j * K + k, slot_ref[b * K + k]).start()

    @pl.when(g == last)
    def _():
        for i in range(width):
            pending(parity, i, 0).wait()

    @pl.when((g == last) & (g >= 1))
    def _():
        for i in range(width):
            pending(1 - parity, i, 0).wait()


def _embed_kernel(slot_ref, count_ref, emb_ref, pos_ref, *rest):
    tiles = rest[:K]
    (grad_ref,) = rest[K:]
    b = pl.program_id(0)
    unit_exact, inverse_norm, _, _, scores = _block_scores(emb_ref, pos_ref, count_ref[b], tiles)
    grad_unit = jnp.zeros((BR, D), jnp.float32)
    for k in range(K):
        terms = jnp.dot(scores[k], tiles[k][0], preferred_element_type=jnp.float32)
        grad_unit = grad_unit + terms.astype(jnp.bfloat16).astype(jnp.float32)
    radial = jnp.sum(unit_exact * grad_unit, axis=1, keepdims=True)
    grad_ref[0] = ((grad_unit - unit_exact * radial) * inverse_norm).astype(grad_ref.dtype)


def _tile_spec(k):
    return pl.BlockSpec((1, TILE, D), lambda b, slot, *_: (slot[b * K + k], 0, 0))


def score_step(slot_of, tile_count, emb_blocks, pos_cols, fetched, parts, per_step=4):
    blocks = emb_blocks.shape[0]
    pairs = fetched.shape[0]

    def step_tile_spec(i):
        j, k = divmod(i, K)
        return pl.BlockSpec(
            (1, TILE, D), lambda g, slot, cnt: (slot[(g * per_step + j) * K + k], 0, 0)
        )

    grid_spec = pltpu.PrefetchScalarGridSpec(
        num_scalar_prefetch=2,
        grid=(blocks // per_step,),
        in_specs=[
            pl.BlockSpec((per_step, BR, D), lambda g, slot, cnt: (g, 0, 0)),
            pl.BlockSpec((per_step, 1, BR), lambda g, slot, cnt: (g, 0, 0)),
        ]
        + [step_tile_spec(i) for i in range(per_step * K)],
        out_specs=[
            pl.BlockSpec((per_step, 1, BR), lambda g, slot, cnt: (g, 0, 0)),
            pl.BlockSpec(memory_space=pl.ANY),
        ],
        scratch_shapes=[
            pltpu.VMEM((2, parts, per_step * K, D // parts, TILE), jnp.bfloat16),
            pltpu.SemaphoreType.DMA((2, per_step * K)),
        ],
    )
    return pl.pallas_call(
        _score_kernel,
        grid_spec=grid_spec,
        out_shape=[
            jax.ShapeDtypeStruct((blocks, 1, BR), jnp.float32),
            jax.ShapeDtypeStruct((parts, pairs, D // parts, TILE), jnp.bfloat16),
        ],
        compiler_params=pltpu.CompilerParams(vmem_limit_bytes=48 * 1024 * 1024),
    )(slot_of, tile_count, emb_blocks, pos_cols, *([fetched] * (per_step * K)))


def embed_step(slot_of, tile_count, emb_blocks, pos_cols, fetched):
    blocks = emb_blocks.shape[0]
    grid_spec = pltpu.PrefetchScalarGridSpec(
        num_scalar_prefetch=2,
        grid=(blocks,),
        in_specs=[
            pl.BlockSpec((1, BR, D), lambda b, slot, cnt: (b, 0, 0)),
            pl.BlockSpec((1, 1, BR), lambda b, slot, cnt: (b, 0, 0)),
        ]
        + [_tile_spec(k) for k in range(K)],
        out_specs=pl.BlockSpec((1, BR, D), lambda b, slot, cnt: (b, 0, 0)),
    )
    flops = blocks * K * 4 * BR * TILE * D
    return pl.pallas_call(
        _embed_kernel,
        grid_spec=grid_spec,
        out_shape=jax.ShapeDtypeStruct((blocks, BR, D), jnp.bfloat16),
        compiler_params=pltpu.CompilerParams(vmem_limit_bytes=48 * 1024 * 1024),
        cost_estimate=pl.CostEstimate(
            flops=flops, transcendentals=blocks * K * BR * TILE, bytes_accessed=blocks * (K + 2) * TILE * D * 2
        ),
    )(slot_of, tile_count, emb_blocks, pos_cols, *([fetched] * K))


def _column_sum_kernel(ids_ref, piece_ref, out_ref):
    step = pl.program_id(0)
    chunk = piece_ref.shape[0]

    @pl.when(step == 0)
    def _():
        out_ref[...] = jnp.zeros_like(out_ref)

    def body(j, carry):
        start = pl.multiple_of(ids_ref[step * chunk + j] * TILE, TILE)
        window = pl.ds(start, TILE)
        out_ref[:, window] += piece_ref[j].astype(jnp.float32)
        return carry

    lax.fori_loop(0, chunk, body, 0, unroll=8)


def column_sum(got_ids, pieces, tile_dev, chunk=64):
    count, width, _ = pieces.shape
    grid_spec = pltpu.PrefetchScalarGridSpec(
        num_scalar_prefetch=1,
        grid=(count // chunk,),
        in_specs=[pl.BlockSpec((chunk, width, TILE), lambda s, ids: (s, 0, 0))],
        out_specs=pl.BlockSpec((width, tile_dev * TILE), lambda s, ids: (0, 0)),
    )
    return pl.pallas_call(
        _column_sum_kernel,
        grid_spec=grid_spec,
        out_shape=jax.ShapeDtypeStruct((width, tile_dev * TILE), jnp.float32),
    )(got_ids, pieces)


def per_device(embeddings, proxies, hard_tiles, tile_count, labels):
    blocks = hard_tiles.shape[0]
    pair_count = blocks * K
    groups = lax.axis_size("cls")
    capacity = pair_count // groups
    tile_dev = proxies.shape[0] // TILE
    flat_tiles = hard_tiles.reshape(pair_count)
    owners = flat_tiles // tile_dev
    local_ids = flat_tiles % tile_dev
    counter = jnp.arange(pair_count, dtype=jnp.int32)
    same_owner = owners[:, None] == owners[None, :]
    earlier = counter[None, :] < counter[:, None]
    rank_order = jnp.sum(jnp.where(same_owner & earlier, 1, 0), axis=1).astype(jnp.int32)
    slot_of = owners * capacity + rank_order
    holder = jnp.sum(jnp.where(slot_of[None, :] == counter[:, None], counter[None, :], 0), axis=1)
    request_ids = local_ids[holder].reshape(groups, capacity)
    tile_table = proxies.reshape(tile_dev, TILE, D)
    wanted = cls_all_to_all(request_ids, 0)
    outgoing = tile_table[wanted]
    fetched = lax.all_to_all(outgoing, "cls", split_axis=0, concat_axis=0, tiled=True)
    fetched = fetched.reshape(pair_count, TILE, D)
    pos_cols = labels.reshape(blocks, 1, BR) - hard_tiles[:, None, 0:1] * TILE
    parts = lax.axis_size("dp")
    emb_blocks = embeddings.reshape(blocks, BR, D)
    loss, pair_grads = score_step(slot_of, tile_count, emb_blocks, pos_cols, fetched, parts)
    embed_grad = embed_step(slot_of, tile_count, emb_blocks, pos_cols, fetched)
    pair_grads = pair_grads.reshape(parts * groups, capacity, D // parts, TILE)
    returned = lax.all_to_all(pair_grads, ("dp", "cls"), split_axis=0, concat_axis=0, tiled=True)
    got_ids = lax.all_gather(wanted, "dp").reshape(parts * pair_count)
    got_terms = returned.reshape(parts * pair_count, D // parts, TILE)
    proxy_share = column_sum(got_ids, got_terms, tile_dev).T
    return (loss.reshape(-1), embed_grad.reshape(-1, D), proxy_share)


def solution(mesh):
    placed = (
        P(("dp", "cls"), None),
        P("cls", None),
        P(("dp", "cls"), None),
        P(("dp", "cls")),
        P(("dp", "cls")),
    )
    return jax.shard_map(
        per_device,
        mesh=mesh,
        in_specs=placed,
        out_specs=(P(("dp", "cls")), P(("dp", "cls"), None), P("cls", "dp")),
        check_vma=False,
    )
```

```python
import functools

import jax
import jax.numpy as jnp
from jax import lax
from jax.experimental import pallas as pl
from jax.experimental.pallas import tpu as pltpu
from jax.sharding import PartitionSpec as P

D = 512
TILE = 128
BR = 128
K = 8


MESH = pl.DeviceIdType.MESH


def _a2a_kernel(n, src_ref, out_ref, send_sem, recv_sem, local_sem):
    me = lax.axis_index("cls")
    row = lax.axis_index("dp")
    barrier = pltpu.get_barrier_semaphore()

    def greet(j, carry):
        peer = lax.rem(me + j, n)
        pl.semaphore_signal(barrier, inc=1, device_id=(row, peer), device_id_type=MESH)
        return carry

    lax.fori_loop(1, n, greet, 0)
    pl.semaphore_wait(barrier, n - 1)
    local = pltpu.make_async_copy(src_ref.at[me], out_ref.at[me], local_sem)
    local.start()

    def remote(j):
        peer = lax.rem(me + j, n)
        return pltpu.make_async_remote_copy(
            src_ref=src_ref.at[peer],
            dst_ref=out_ref.at[me],
            send_sem=send_sem.at[j],
            recv_sem=recv_sem.at[j],
            device_id=(row, peer),
            device_id_type=MESH,
        )

    def launch(j, carry):
        remote(j).start()
        return carry

    def finish(j, carry):
        remote(j).wait()
        return carry

    lax.fori_loop(1, n, launch, 0)
    lax.fori_loop(1, n, finish, 0)
    local.wait()


def cls_all_to_all(x, cid):
    n = x.shape[0]
    return pl.pallas_call(
        functools.partial(_a2a_kernel, n),
        out_shape=jax.ShapeDtypeStruct(x.shape, x.dtype),
        in_specs=[pl.BlockSpec(memory_space=pl.ANY)],
        out_specs=pl.BlockSpec(memory_space=pl.ANY),
        scratch_shapes=[
            pltpu.SemaphoreType.DMA((n,)),
            pltpu.SemaphoreType.DMA((n,)),
            pltpu.SemaphoreType.DMA,
        ],
        compiler_params=pltpu.CompilerParams(collective_id=cid, has_side_effects=True),
    )(x)


logit_scale = 4.0
epsilon = 1e-06


def _block_scores(emb_ref, pos_ref, count, tiles):
    emb = emb_ref[0].astype(jnp.float32)
    inverse_norm = lax.rsqrt(jnp.sum(emb * emb, axis=1, keepdims=True) + epsilon)
    unit_exact = emb * inverse_norm
    unit_t = unit_exact.astype(jnp.bfloat16).T
    classes = lax.broadcasted_iota(jnp.int32, (TILE, BR), 0)
    hit = classes == pos_ref[0]
    logits = []
    for k in range(K):
        logits.append(logit_scale * jnp.dot(tiles[k][0], unit_t, preferred_element_type=jnp.float32))
    masked = [jnp.where(k < count, logits[k], -1e30) for k in range(K)]
    peak = masked[0].max(axis=0, keepdims=True)
    for k in range(1, K):
        peak = jnp.maximum(peak, masked[k].max(axis=0, keepdims=True))
    shifted = [jnp.exp(masked[k] - peak) for k in range(K)]
    total = jnp.zeros_like(peak)
    for k in range(K):
        total = total + jnp.sum(shifted[k], axis=0, keepdims=True)
    log_total = peak + jnp.log(total)
    positive = jnp.sum(jnp.where(hit, logits[0], 0.0), axis=0, keepdims=True)
    inverse_total = 1.0 / total
    scores = []
    for k in range(K):
        probabilities = shifted[k] * inverse_total
        if k == 0:
            probabilities = probabilities - jnp.where(hit, 1.0, 0.0)
        scores.append((logit_scale * probabilities).astype(jnp.bfloat16).T)
    return unit_exact, inverse_norm, unit_t, log_total - positive, scores


def _score_kernel(slot_ref, count_ref, emb_ref, pos_ref, *rest):
    per_step = emb_ref.shape[0]
    tiles = rest[: per_step * K]
    loss_ref, pair_hbm, pair_buf, pair_sem = rest[per_step * K:]
    g = pl.program_id(0)
    last = pl.num_programs(0) - 1
    width = per_step * K

    def pending(par, i, slot):
        return pltpu.make_async_copy(
            pair_buf.at[par, :, pl.ds(i, 1)],
            pair_hbm.at[:, pl.ds(slot, 1)],
            pair_sem.at[par, i],
        )

    parity = g % 2

    @pl.when(g >= 2)
    def _():
        for i in range(width):
            pending(parity, i, 0).wait()

    for j in range(per_step):
        b = g * per_step + j
        block_tiles = tiles[j * K:(j + 1) * K]
        _, _, unit_t, loss, scores = _block_scores(
            emb_ref.at[pl.ds(j, 1)], pos_ref.at[pl.ds(j, 1)], count_ref[b], block_tiles
        )
        loss_ref[j] = loss
        for k in range(K):
            pair_t = jnp.dot(unit_t, scores[k], preferred_element_type=jnp.float32).astype(jnp.bfloat16)
            pair_buf[parity, :, j * K + k] = pair_t.reshape(pair_buf.shape[1], D // pair_buf.shape[1], TILE)
        for k in range(K):
            pending(parity, j * K + k, slot_ref[b * K + k]).start()

    @pl.when(g == last)
    def _():
        for i in range(width):
            pending(parity, i, 0).wait()

    @pl.when((g == last) & (g >= 1))
    def _():
        for i in range(width):
            pending(1 - parity, i, 0).wait()


def _embed_kernel(slot_ref, count_ref, emb_ref, pos_ref, *rest):
    tiles = rest[:K]
    (grad_ref,) = rest[K:]
    b = pl.program_id(0)
    unit_exact, inverse_norm, _, _, scores = _block_scores(emb_ref, pos_ref, count_ref[b], tiles)
    grad_unit = jnp.zeros((BR, D), jnp.float32)
    for k in range(K):
        terms = jnp.dot(scores[k], tiles[k][0], preferred_element_type=jnp.float32)
        grad_unit = grad_unit + terms.astype(jnp.bfloat16).astype(jnp.float32)
    radial = jnp.sum(unit_exact * grad_unit, axis=1, keepdims=True)
    grad_ref[0] = ((grad_unit - unit_exact * radial) * inverse_norm).astype(grad_ref.dtype)


def _tile_spec(k):
    return pl.BlockSpec((1, TILE, D), lambda b, slot, *_: (slot[b * K + k], 0, 0))


def score_step(slot_of, tile_count, emb_blocks, pos_cols, fetched, parts, per_step=4):
    blocks = emb_blocks.shape[0]
    pairs = fetched.shape[0]

    def step_tile_spec(i):
        j, k = divmod(i, K)
        return pl.BlockSpec(
            (1, TILE, D), lambda g, slot, cnt: (slot[(g * per_step + j) * K + k], 0, 0)
        )

    grid_spec = pltpu.PrefetchScalarGridSpec(
        num_scalar_prefetch=2,
        grid=(blocks // per_step,),
        in_specs=[
            pl.BlockSpec((per_step, BR, D), lambda g, slot, cnt: (g, 0, 0)),
            pl.BlockSpec((per_step, 1, BR), lambda g, slot, cnt: (g, 0, 0)),
        ]
        + [step_tile_spec(i) for i in range(per_step * K)],
        out_specs=[
            pl.BlockSpec((per_step, 1, BR), lambda g, slot, cnt: (g, 0, 0)),
            pl.BlockSpec(memory_space=pl.ANY),
        ],
        scratch_shapes=[
            pltpu.VMEM((2, parts, per_step * K, D // parts, TILE), jnp.bfloat16),
            pltpu.SemaphoreType.DMA((2, per_step * K)),
        ],
    )
    return pl.pallas_call(
        _score_kernel,
        grid_spec=grid_spec,
        out_shape=[
            jax.ShapeDtypeStruct((blocks, 1, BR), jnp.float32),
            jax.ShapeDtypeStruct((parts, pairs, D // parts, TILE), jnp.bfloat16),
        ],
        compiler_params=pltpu.CompilerParams(vmem_limit_bytes=48 * 1024 * 1024),
    )(slot_of, tile_count, emb_blocks, pos_cols, *([fetched] * (per_step * K)))


def embed_step(slot_of, tile_count, emb_blocks, pos_cols, fetched):
    blocks = emb_blocks.shape[0]
    grid_spec = pltpu.PrefetchScalarGridSpec(
        num_scalar_prefetch=2,
        grid=(blocks,),
        in_specs=[
            pl.BlockSpec((1, BR, D), lambda b, slot, cnt: (b, 0, 0)),
            pl.BlockSpec((1, 1, BR), lambda b, slot, cnt: (b, 0, 0)),
        ]
        + [_tile_spec(k) for k in range(K)],
        out_specs=pl.BlockSpec((1, BR, D), lambda b, slot, cnt: (b, 0, 0)),
    )
    flops = blocks * K * 4 * BR * TILE * D
    return pl.pallas_call(
        _embed_kernel,
        grid_spec=grid_spec,
        out_shape=jax.ShapeDtypeStruct((blocks, BR, D), jnp.bfloat16),
        compiler_params=pltpu.CompilerParams(vmem_limit_bytes=48 * 1024 * 1024),
        cost_estimate=pl.CostEstimate(
            flops=flops, transcendentals=blocks * K * BR * TILE, bytes_accessed=blocks * (K + 2) * TILE * D * 2
        ),
    )(slot_of, tile_count, emb_blocks, pos_cols, *([fetched] * K))


def _column_sum_kernel(ids_ref, piece_ref, out_ref):
    step = pl.program_id(0)
    chunk = piece_ref.shape[0]

    @pl.when(step == 0)
    def _():
        out_ref[...] = jnp.zeros_like(out_ref)

    def body(j, carry):
        start = pl.multiple_of(ids_ref[step * chunk + j] * TILE, TILE)
        window = pl.ds(start, TILE)
        out_ref[:, window] += piece_ref[j].astype(jnp.float32)
        return carry

    lax.fori_loop(0, chunk, body, 0, unroll=8)


def column_sum(got_ids, pieces, tile_dev, chunk=128):
    count, width, _ = pieces.shape
    grid_spec = pltpu.PrefetchScalarGridSpec(
        num_scalar_prefetch=1,
        grid=(count // chunk,),
        in_specs=[pl.BlockSpec((chunk, width, TILE), lambda s, ids: (s, 0, 0))],
        out_specs=pl.BlockSpec((width, tile_dev * TILE), lambda s, ids: (0, 0)),
    )
    return pl.pallas_call(
        _column_sum_kernel,
        grid_spec=grid_spec,
        out_shape=jax.ShapeDtypeStruct((width, tile_dev * TILE), jnp.float32),
    )(got_ids, pieces)


def per_device(embeddings, proxies, hard_tiles, tile_count, labels):
    blocks = hard_tiles.shape[0]
    pair_count = blocks * K
    groups = lax.axis_size("cls")
    capacity = pair_count // groups
    tile_dev = proxies.shape[0] // TILE
    flat_tiles = hard_tiles.reshape(pair_count)
    owners = flat_tiles // tile_dev
    local_ids = flat_tiles % tile_dev
    counter = jnp.arange(pair_count, dtype=jnp.int32)
    same_owner = owners[:, None] == owners[None, :]
    earlier = counter[None, :] < counter[:, None]
    rank_order = jnp.sum(jnp.where(same_owner & earlier, 1, 0), axis=1).astype(jnp.int32)
    slot_of = owners * capacity + rank_order
    holder = jnp.sum(jnp.where(slot_of[None, :] == counter[:, None], counter[None, :], 0), axis=1)
    request_ids = local_ids[holder].reshape(groups, capacity)
    tile_table = proxies.reshape(tile_dev, TILE, D)
    wanted = cls_all_to_all(request_ids, 0)
    outgoing = tile_table[wanted]
    fetched = lax.all_to_all(outgoing, "cls", split_axis=0, concat_axis=0, tiled=True)
    fetched = fetched.reshape(pair_count, TILE, D)
    pos_cols = labels.reshape(blocks, 1, BR) - hard_tiles[:, None, 0:1] * TILE
    parts = lax.axis_size("dp")
    emb_blocks = embeddings.reshape(blocks, BR, D)
    loss, pair_grads = score_step(slot_of, tile_count, emb_blocks, pos_cols, fetched, parts)
    embed_grad = embed_step(slot_of, tile_count, emb_blocks, pos_cols, fetched)
    pair_grads = pair_grads.reshape(parts * groups, capacity, D // parts, TILE)
    returned = lax.all_to_all(pair_grads, ("dp", "cls"), split_axis=0, concat_axis=0, tiled=True)
    got_ids = lax.all_gather(wanted, "dp").reshape(parts * pair_count)
    got_terms = returned.reshape(parts * pair_count, D // parts, TILE)
    proxy_share = column_sum(got_ids, got_terms, tile_dev).T
    return (loss.reshape(-1), embed_grad.reshape(-1, D), proxy_share)


def solution(mesh):
    placed = (
        P(("dp", "cls"), None),
        P("cls", None),
        P(("dp", "cls"), None),
        P(("dp", "cls")),
        P(("dp", "cls")),
    )
    return jax.shard_map(
        per_device,
        mesh=mesh,
        in_specs=placed,
        out_specs=(P(("dp", "cls")), P(("dp", "cls"), None), P("cls", "dp")),
        check_vma=False,
    )
```

```python
import functools

import jax
import jax.numpy as jnp
from jax import lax
from jax.experimental import pallas as pl
from jax.experimental.pallas import tpu as pltpu
from jax.sharding import PartitionSpec as P

D = 512
TILE = 128
BR = 128
K = 8


MESH = pl.DeviceIdType.MESH


def _a2a_kernel(n, src_ref, out_ref, send_sem, recv_sem, local_sem):
    me = lax.axis_index("cls")
    row = lax.axis_index("dp")
    barrier = pltpu.get_barrier_semaphore()

    def greet(j, carry):
        peer = lax.rem(me + j, n)
        pl.semaphore_signal(barrier, inc=1, device_id=(row, peer), device_id_type=MESH)
        return carry

    lax.fori_loop(1, n, greet, 0)
    pl.semaphore_wait(barrier, n - 1)
    local = pltpu.make_async_copy(src_ref.at[me], out_ref.at[me], local_sem)
    local.start()

    def remote(j):
        peer = lax.rem(me + j, n)
        return pltpu.make_async_remote_copy(
            src_ref=src_ref.at[peer],
            dst_ref=out_ref.at[me],
            send_sem=send_sem.at[j],
            recv_sem=recv_sem.at[j],
            device_id=(row, peer),
            device_id_type=MESH,
        )

    def launch(j, carry):
        remote(j).start()
        return carry

    def finish(j, carry):
        remote(j).wait()
        return carry

    lax.fori_loop(1, n, launch, 0)
    lax.fori_loop(1, n, finish, 0)
    local.wait()


def cls_all_to_all(x, cid):
    n = x.shape[0]
    return pl.pallas_call(
        functools.partial(_a2a_kernel, n),
        out_shape=jax.ShapeDtypeStruct(x.shape, x.dtype),
        in_specs=[pl.BlockSpec(memory_space=pl.ANY)],
        out_specs=pl.BlockSpec(memory_space=pl.ANY),
        scratch_shapes=[
            pltpu.SemaphoreType.DMA((n,)),
            pltpu.SemaphoreType.DMA((n,)),
            pltpu.SemaphoreType.DMA,
        ],
        compiler_params=pltpu.CompilerParams(collective_id=cid, has_side_effects=True),
    )(x)


logit_scale = 4.0
epsilon = 1e-06


def _block_scores(emb_ref, pos_ref, count, tiles):
    emb = emb_ref[0].astype(jnp.float32)
    inverse_norm = lax.rsqrt(jnp.sum(emb * emb, axis=1, keepdims=True) + epsilon)
    unit_exact = emb * inverse_norm
    unit_t = unit_exact.astype(jnp.bfloat16).T
    classes = lax.broadcasted_iota(jnp.int32, (TILE, BR), 0)
    hit = classes == pos_ref[0]
    logits = []
    for k in range(K):
        logits.append(logit_scale * jnp.dot(tiles[k][0], unit_t, preferred_element_type=jnp.float32))
    masked = [jnp.where(k < count, logits[k], -1e30) for k in range(K)]
    peak = masked[0].max(axis=0, keepdims=True)
    for k in range(1, K):
        peak = jnp.maximum(peak, masked[k].max(axis=0, keepdims=True))
    shifted = [jnp.exp(masked[k] - peak) for k in range(K)]
    total = jnp.zeros_like(peak)
    for k in range(K):
        total = total + jnp.sum(shifted[k], axis=0, keepdims=True)
    log_total = peak + jnp.log(total)
    positive = jnp.sum(jnp.where(hit, logits[0], 0.0), axis=0, keepdims=True)
    inverse_total = 1.0 / total
    scores = []
    for k in range(K):
        probabilities = shifted[k] * inverse_total
        if k == 0:
            probabilities = probabilities - jnp.where(hit, 1.0, 0.0)
        scores.append((logit_scale * probabilities).astype(jnp.bfloat16).T)
    return unit_exact, inverse_norm, unit_t, log_total - positive, scores


def _score_kernel(slot_ref, count_ref, emb_ref, pos_ref, *rest):
    per_step = emb_ref.shape[0]
    tiles = rest[: per_step * K]
    loss_ref, pair_hbm, pair_buf, pair_sem = rest[per_step * K:]
    g = pl.program_id(0)
    last = pl.num_programs(0) - 1
    width = per_step * K

    def pending(par, i, slot):
        return pltpu.make_async_copy(
            pair_buf.at[par, :, pl.ds(i, 1)],
            pair_hbm.at[:, pl.ds(slot, 1)],
            pair_sem.at[par, i],
        )

    parity = g % 2

    @pl.when(g >= 2)
    def _():
        for i in range(width):
            pending(parity, i, 0).wait()

    for j in range(per_step):
        b = g * per_step + j
        block_tiles = tiles[j * K:(j + 1) * K]
        _, _, unit_t, loss, scores = _block_scores(
            emb_ref.at[pl.ds(j, 1)], pos_ref.at[pl.ds(j, 1)], count_ref[b], block_tiles
        )
        loss_ref[j] = loss
        for k in range(K):
            pair_t = jnp.dot(unit_t, scores[k], preferred_element_type=jnp.float32).astype(jnp.bfloat16)
            pair_buf[parity, :, j * K + k] = pair_t.reshape(pair_buf.shape[1], D // pair_buf.shape[1], TILE)
        for k in range(K):
            pending(parity, j * K + k, slot_ref[b * K + k]).start()

    @pl.when(g == last)
    def _():
        for i in range(width):
            pending(parity, i, 0).wait()

    @pl.when((g == last) & (g >= 1))
    def _():
        for i in range(width):
            pending(1 - parity, i, 0).wait()


def _embed_kernel(slot_ref, count_ref, emb_ref, pos_ref, *rest):
    tiles = rest[:K]
    (grad_ref,) = rest[K:]
    b = pl.program_id(0)
    unit_exact, inverse_norm, _, _, scores = _block_scores(emb_ref, pos_ref, count_ref[b], tiles)
    grad_unit = jnp.zeros((BR, D), jnp.float32)
    for k in range(K):
        terms = jnp.dot(scores[k], tiles[k][0], preferred_element_type=jnp.float32)
        grad_unit = grad_unit + terms.astype(jnp.bfloat16).astype(jnp.float32)
    radial = jnp.sum(unit_exact * grad_unit, axis=1, keepdims=True)
    grad_ref[0] = ((grad_unit - unit_exact * radial) * inverse_norm).astype(grad_ref.dtype)


def _tile_spec(k):
    return pl.BlockSpec((1, TILE, D), lambda b, slot, *_: (slot[b * K + k], 0, 0))


def score_step(slot_of, tile_count, emb_blocks, pos_cols, fetched, parts, per_step=4):
    blocks = emb_blocks.shape[0]
    pairs = fetched.shape[0]

    def step_tile_spec(i):
        j, k = divmod(i, K)
        return pl.BlockSpec(
            (1, TILE, D), lambda g, slot, cnt: (slot[(g * per_step + j) * K + k], 0, 0)
        )

    grid_spec = pltpu.PrefetchScalarGridSpec(
        num_scalar_prefetch=2,
        grid=(blocks // per_step,),
        in_specs=[
            pl.BlockSpec((per_step, BR, D), lambda g, slot, cnt: (g, 0, 0)),
            pl.BlockSpec((per_step, 1, BR), lambda g, slot, cnt: (g, 0, 0)),
        ]
        + [step_tile_spec(i) for i in range(per_step * K)],
        out_specs=[
            pl.BlockSpec((per_step, 1, BR), lambda g, slot, cnt: (g, 0, 0)),
            pl.BlockSpec(memory_space=pl.ANY),
        ],
        scratch_shapes=[
            pltpu.VMEM((2, parts, per_step * K, D // parts, TILE), jnp.bfloat16),
            pltpu.SemaphoreType.DMA((2, per_step * K)),
        ],
    )
    return pl.pallas_call(
        _score_kernel,
        grid_spec=grid_spec,
        out_shape=[
            jax.ShapeDtypeStruct((blocks, 1, BR), jnp.float32),
            jax.ShapeDtypeStruct((parts, pairs, D // parts, TILE), jnp.bfloat16),
        ],
        compiler_params=pltpu.CompilerParams(vmem_limit_bytes=48 * 1024 * 1024),
    )(slot_of, tile_count, emb_blocks, pos_cols, *([fetched] * (per_step * K)))


def embed_step(slot_of, tile_count, emb_blocks, pos_cols, fetched):
    blocks = emb_blocks.shape[0]
    grid_spec = pltpu.PrefetchScalarGridSpec(
        num_scalar_prefetch=2,
        grid=(blocks,),
        in_specs=[
            pl.BlockSpec((1, BR, D), lambda b, slot, cnt: (b, 0, 0)),
            pl.BlockSpec((1, 1, BR), lambda b, slot, cnt: (b, 0, 0)),
        ]
        + [_tile_spec(k) for k in range(K)],
        out_specs=pl.BlockSpec((1, BR, D), lambda b, slot, cnt: (b, 0, 0)),
    )
    flops = blocks * K * 4 * BR * TILE * D
    return pl.pallas_call(
        _embed_kernel,
        grid_spec=grid_spec,
        out_shape=jax.ShapeDtypeStruct((blocks, BR, D), jnp.bfloat16),
        compiler_params=pltpu.CompilerParams(vmem_limit_bytes=48 * 1024 * 1024),
        cost_estimate=pl.CostEstimate(
            flops=flops, transcendentals=blocks * K * BR * TILE, bytes_accessed=blocks * (K + 2) * TILE * D * 2
        ),
    )(slot_of, tile_count, emb_blocks, pos_cols, *([fetched] * K))


def _column_sum_kernel(ids_ref, piece_ref, out_ref):
    step = pl.program_id(0)
    chunk = piece_ref.shape[0]

    @pl.when(step == 0)
    def _():
        out_ref[...] = jnp.zeros_like(out_ref)

    def body(j, carry):
        start = pl.multiple_of(ids_ref[step * chunk + j] * TILE, TILE)
        window = pl.ds(start, TILE)
        out_ref[:, window] += piece_ref[j].astype(jnp.float32)
        return carry

    lax.fori_loop(0, chunk, body, 0, unroll=16)


def column_sum(got_ids, pieces, tile_dev, chunk=128):
    count, width, _ = pieces.shape
    grid_spec = pltpu.PrefetchScalarGridSpec(
        num_scalar_prefetch=1,
        grid=(count // chunk,),
        in_specs=[pl.BlockSpec((chunk, width, TILE), lambda s, ids: (s, 0, 0))],
        out_specs=pl.BlockSpec((width, tile_dev * TILE), lambda s, ids: (0, 0)),
    )
    return pl.pallas_call(
        _column_sum_kernel,
        grid_spec=grid_spec,
        out_shape=jax.ShapeDtypeStruct((width, tile_dev * TILE), jnp.float32),
    )(got_ids, pieces)


def per_device(embeddings, proxies, hard_tiles, tile_count, labels):
    blocks = hard_tiles.shape[0]
    pair_count = blocks * K
    groups = lax.axis_size("cls")
    capacity = pair_count // groups
    tile_dev = proxies.shape[0] // TILE
    flat_tiles = hard_tiles.reshape(pair_count)
    owners = flat_tiles // tile_dev
    local_ids = flat_tiles % tile_dev
    counter = jnp.arange(pair_count, dtype=jnp.int32)
    same_owner = owners[:, None] == owners[None, :]
    earlier = counter[None, :] < counter[:, None]
    rank_order = jnp.sum(jnp.where(same_owner & earlier, 1, 0), axis=1).astype(jnp.int32)
    slot_of = owners * capacity + rank_order
    holder = jnp.sum(jnp.where(slot_of[None, :] == counter[:, None], counter[None, :], 0), axis=1)
    request_ids = local_ids[holder].reshape(groups, capacity)
    tile_table = proxies.reshape(tile_dev, TILE, D)
    wanted = cls_all_to_all(request_ids, 0)
    outgoing = tile_table[wanted]
    fetched = lax.all_to_all(outgoing, "cls", split_axis=0, concat_axis=0, tiled=True)
    fetched = fetched.reshape(pair_count, TILE, D)
    pos_cols = labels.reshape(blocks, 1, BR) - hard_tiles[:, None, 0:1] * TILE
    parts = lax.axis_size("dp")
    emb_blocks = embeddings.reshape(blocks, BR, D)
    loss, pair_grads = score_step(slot_of, tile_count, emb_blocks, pos_cols, fetched, parts)
    embed_grad = embed_step(slot_of, tile_count, emb_blocks, pos_cols, fetched)
    pair_grads = pair_grads.reshape(parts * groups, capacity, D // parts, TILE)
    returned = lax.all_to_all(pair_grads, ("dp", "cls"), split_axis=0, concat_axis=0, tiled=True)
    got_ids = lax.all_gather(wanted, "dp").reshape(parts * pair_count)
    got_terms = returned.reshape(parts * pair_count, D // parts, TILE)
    proxy_share = column_sum(got_ids, got_terms, tile_dev).T
    return (loss.reshape(-1), embed_grad.reshape(-1, D), proxy_share)


def solution(mesh):
    placed = (
        P(("dp", "cls"), None),
        P("cls", None),
        P(("dp", "cls"), None),
        P(("dp", "cls")),
        P(("dp", "cls")),
    )
    return jax.shard_map(
        per_device,
        mesh=mesh,
        in_specs=placed,
        out_specs=(P(("dp", "cls")), P(("dp", "cls"), None), P("cls", "dp")),
        check_vma=False,
    )
```

```python
import functools

import jax
import jax.numpy as jnp
from jax import lax
from jax.experimental import pallas as pl
from jax.experimental.pallas import tpu as pltpu
from jax.sharding import PartitionSpec as P

D = 512
TILE = 128
BR = 128
K = 8


MESH = pl.DeviceIdType.MESH


def _a2a_kernel(n, src_ref, out_ref, send_sem, recv_sem, local_sem):
    me = lax.axis_index("cls")
    row = lax.axis_index("dp")
    barrier = pltpu.get_barrier_semaphore()

    def greet(j, carry):
        peer = lax.rem(me + j, n)
        pl.semaphore_signal(barrier, inc=1, device_id=(row, peer), device_id_type=MESH)
        return carry

    lax.fori_loop(1, n, greet, 0)
    pl.semaphore_wait(barrier, n - 1)
    local = pltpu.make_async_copy(src_ref.at[me], out_ref.at[me], local_sem)
    local.start()

    def remote(j):
        peer = lax.rem(me + j, n)
        return pltpu.make_async_remote_copy(
            src_ref=src_ref.at[peer],
            dst_ref=out_ref.at[me],
            send_sem=send_sem.at[j],
            recv_sem=recv_sem.at[j],
            device_id=(row, peer),
            device_id_type=MESH,
        )

    def launch(j, carry):
        remote(j).start()
        return carry

    def finish(j, carry):
        remote(j).wait()
        return carry

    lax.fori_loop(1, n, launch, 0)
    lax.fori_loop(1, n, finish, 0)
    local.wait()


def cls_all_to_all(x, cid):
    n = x.shape[0]
    return pl.pallas_call(
        functools.partial(_a2a_kernel, n),
        out_shape=jax.ShapeDtypeStruct(x.shape, x.dtype),
        in_specs=[pl.BlockSpec(memory_space=pl.ANY)],
        out_specs=pl.BlockSpec(memory_space=pl.ANY),
        scratch_shapes=[
            pltpu.SemaphoreType.DMA((n,)),
            pltpu.SemaphoreType.DMA((n,)),
            pltpu.SemaphoreType.DMA,
        ],
        compiler_params=pltpu.CompilerParams(collective_id=cid, has_side_effects=True),
    )(x)


logit_scale = 4.0
epsilon = 1e-06


def _block_scores(emb_ref, pos_ref, count, tiles):
    emb = emb_ref[0].astype(jnp.float32)
    inverse_norm = lax.rsqrt(jnp.sum(emb * emb, axis=1, keepdims=True) + epsilon)
    unit_exact = emb * inverse_norm
    unit_t = unit_exact.astype(jnp.bfloat16).T
    classes = lax.broadcasted_iota(jnp.int32, (TILE, BR), 0)
    hit = classes == pos_ref[0]
    logits = []
    for k in range(K):
        logits.append(logit_scale * jnp.dot(tiles[k][0], unit_t, preferred_element_type=jnp.float32))
    masked = [jnp.where(k < count, logits[k], -1e30) for k in range(K)]
    peak = masked[0].max(axis=0, keepdims=True)
    for k in range(1, K):
        peak = jnp.maximum(peak, masked[k].max(axis=0, keepdims=True))
    shifted = [jnp.exp(masked[k] - peak) for k in range(K)]
    total = jnp.zeros_like(peak)
    for k in range(K):
        total = total + jnp.sum(shifted[k], axis=0, keepdims=True)
    log_total = peak + jnp.log(total)
    positive = jnp.sum(jnp.where(hit, logits[0], 0.0), axis=0, keepdims=True)
    inverse_total = 1.0 / total
    scores = []
    for k in range(K):
        probabilities = shifted[k] * inverse_total
        if k == 0:
            probabilities = probabilities - jnp.where(hit, 1.0, 0.0)
        scores.append((logit_scale * probabilities).astype(jnp.bfloat16).T)
    return unit_exact, inverse_norm, unit_t, log_total - positive, scores


def _score_kernel(slot_ref, count_ref, emb_ref, pos_ref, *rest):
    per_step = emb_ref.shape[0]
    tiles = rest[: per_step * K]
    loss_ref, pair_hbm, pair_buf, pair_sem = rest[per_step * K:]
    g = pl.program_id(0)
    last = pl.num_programs(0) - 1
    width = per_step * K

    def pending(par, i, slot):
        return pltpu.make_async_copy(
            pair_buf.at[par, :, pl.ds(i, 1)],
            pair_hbm.at[:, pl.ds(slot, 1)],
            pair_sem.at[par, i],
        )

    parity = g % 2

    @pl.when(g >= 2)
    def _():
        for i in range(width):
            pending(parity, i, 0).wait()

    for j in range(per_step):
        b = g * per_step + j
        block_tiles = tiles[j * K:(j + 1) * K]
        _, _, unit_t, loss, scores = _block_scores(
            emb_ref.at[pl.ds(j, 1)], pos_ref.at[pl.ds(j, 1)], count_ref[b], block_tiles
        )
        loss_ref[j] = loss
        for k in range(K):
            pair_t = jnp.dot(unit_t, scores[k], preferred_element_type=jnp.float32).astype(jnp.bfloat16)
            pair_buf[parity, :, j * K + k] = pair_t.reshape(pair_buf.shape[1], D // pair_buf.shape[1], TILE)
        for k in range(K):
            pending(parity, j * K + k, slot_ref[b * K + k]).start()

    @pl.when(g == last)
    def _():
        for i in range(width):
            pending(parity, i, 0).wait()

    @pl.when((g == last) & (g >= 1))
    def _():
        for i in range(width):
            pending(1 - parity, i, 0).wait()


def _embed_kernel(slot_ref, count_ref, emb_ref, pos_ref, *rest):
    tiles = rest[:K]
    (grad_ref,) = rest[K:]
    b = pl.program_id(0)
    unit_exact, inverse_norm, _, _, scores = _block_scores(emb_ref, pos_ref, count_ref[b], tiles)
    grad_unit = jnp.zeros((BR, D), jnp.float32)
    for k in range(K):
        terms = jnp.dot(scores[k], tiles[k][0], preferred_element_type=jnp.float32)
        grad_unit = grad_unit + terms.astype(jnp.bfloat16).astype(jnp.float32)
    radial = jnp.sum(unit_exact * grad_unit, axis=1, keepdims=True)
    grad_ref[0] = ((grad_unit - unit_exact * radial) * inverse_norm).astype(grad_ref.dtype)


def _tile_spec(k):
    return pl.BlockSpec((1, TILE, D), lambda b, slot, *_: (slot[b * K + k], 0, 0))


def score_step(slot_of, tile_count, emb_blocks, pos_cols, fetched, parts, per_step=4):
    blocks = emb_blocks.shape[0]
    pairs = fetched.shape[0]

    def step_tile_spec(i):
        j, k = divmod(i, K)
        return pl.BlockSpec(
            (1, TILE, D), lambda g, slot, cnt: (slot[(g * per_step + j) * K + k], 0, 0)
        )

    grid_spec = pltpu.PrefetchScalarGridSpec(
        num_scalar_prefetch=2,
        grid=(blocks // per_step,),
        in_specs=[
            pl.BlockSpec((per_step, BR, D), lambda g, slot, cnt: (g, 0, 0)),
            pl.BlockSpec((per_step, 1, BR), lambda g, slot, cnt: (g, 0, 0)),
        ]
        + [step_tile_spec(i) for i in range(per_step * K)],
        out_specs=[
            pl.BlockSpec((per_step, 1, BR), lambda g, slot, cnt: (g, 0, 0)),
            pl.BlockSpec(memory_space=pl.ANY),
        ],
        scratch_shapes=[
            pltpu.VMEM((2, parts, per_step * K, D // parts, TILE), jnp.bfloat16),
            pltpu.SemaphoreType.DMA((2, per_step * K)),
        ],
    )
    return pl.pallas_call(
        _score_kernel,
        grid_spec=grid_spec,
        out_shape=[
            jax.ShapeDtypeStruct((blocks, 1, BR), jnp.float32),
            jax.ShapeDtypeStruct((parts, pairs, D // parts, TILE), jnp.bfloat16),
        ],
        compiler_params=pltpu.CompilerParams(vmem_limit_bytes=48 * 1024 * 1024),
    )(slot_of, tile_count, emb_blocks, pos_cols, *([fetched] * (per_step * K)))


def embed_step(slot_of, tile_count, emb_blocks, pos_cols, fetched):
    blocks = emb_blocks.shape[0]
    grid_spec = pltpu.PrefetchScalarGridSpec(
        num_scalar_prefetch=2,
        grid=(blocks,),
        in_specs=[
            pl.BlockSpec((1, BR, D), lambda b, slot, cnt: (b, 0, 0)),
            pl.BlockSpec((1, 1, BR), lambda b, slot, cnt: (b, 0, 0)),
        ]
        + [_tile_spec(k) for k in range(K)],
        out_specs=pl.BlockSpec((1, BR, D), lambda b, slot, cnt: (b, 0, 0)),
    )
    flops = blocks * K * 4 * BR * TILE * D
    return pl.pallas_call(
        _embed_kernel,
        grid_spec=grid_spec,
        out_shape=jax.ShapeDtypeStruct((blocks, BR, D), jnp.bfloat16),
        compiler_params=pltpu.CompilerParams(vmem_limit_bytes=48 * 1024 * 1024),
        cost_estimate=pl.CostEstimate(
            flops=flops, transcendentals=blocks * K * BR * TILE, bytes_accessed=blocks * (K + 2) * TILE * D * 2
        ),
    )(slot_of, tile_count, emb_blocks, pos_cols, *([fetched] * K))


def _column_sum_kernel(ids_ref, piece_ref, out_ref):
    step = pl.program_id(0)
    chunk = piece_ref.shape[0]

    @pl.when(step == 0)
    def _():
        out_ref[...] = jnp.zeros_like(out_ref)

    def body(j, carry):
        start = pl.multiple_of(ids_ref[step * chunk + j] * TILE, TILE)
        window = pl.ds(start, TILE)
        out_ref[:, window] += piece_ref[j].astype(jnp.float32)
        return carry

    lax.fori_loop(0, chunk, body, 0, unroll=16)


def column_sum(got_ids, pieces, tile_dev, chunk=256):
    count, width, _ = pieces.shape
    grid_spec = pltpu.PrefetchScalarGridSpec(
        num_scalar_prefetch=1,
        grid=(count // chunk,),
        in_specs=[pl.BlockSpec((chunk, width, TILE), lambda s, ids: (s, 0, 0))],
        out_specs=pl.BlockSpec((width, tile_dev * TILE), lambda s, ids: (0, 0)),
    )
    return pl.pallas_call(
        _column_sum_kernel,
        grid_spec=grid_spec,
        out_shape=jax.ShapeDtypeStruct((width, tile_dev * TILE), jnp.float32),
    )(got_ids, pieces)


def per_device(embeddings, proxies, hard_tiles, tile_count, labels):
    blocks = hard_tiles.shape[0]
    pair_count = blocks * K
    groups = lax.axis_size("cls")
    capacity = pair_count // groups
    tile_dev = proxies.shape[0] // TILE
    flat_tiles = hard_tiles.reshape(pair_count)
    owners = flat_tiles // tile_dev
    local_ids = flat_tiles % tile_dev
    counter = jnp.arange(pair_count, dtype=jnp.int32)
    same_owner = owners[:, None] == owners[None, :]
    earlier = counter[None, :] < counter[:, None]
    rank_order = jnp.sum(jnp.where(same_owner & earlier, 1, 0), axis=1).astype(jnp.int32)
    slot_of = owners * capacity + rank_order
    holder = jnp.sum(jnp.where(slot_of[None, :] == counter[:, None], counter[None, :], 0), axis=1)
    request_ids = local_ids[holder].reshape(groups, capacity)
    tile_table = proxies.reshape(tile_dev, TILE, D)
    wanted = cls_all_to_all(request_ids, 0)
    outgoing = tile_table[wanted]
    fetched = lax.all_to_all(outgoing, "cls", split_axis=0, concat_axis=0, tiled=True)
    fetched = fetched.reshape(pair_count, TILE, D)
    pos_cols = labels.reshape(blocks, 1, BR) - hard_tiles[:, None, 0:1] * TILE
    parts = lax.axis_size("dp")
    emb_blocks = embeddings.reshape(blocks, BR, D)
    loss, pair_grads = score_step(slot_of, tile_count, emb_blocks, pos_cols, fetched, parts)
    embed_grad = embed_step(slot_of, tile_count, emb_blocks, pos_cols, fetched)
    pair_grads = pair_grads.reshape(parts * groups, capacity, D // parts, TILE)
    returned = lax.all_to_all(pair_grads, ("dp", "cls"), split_axis=0, concat_axis=0, tiled=True)
    got_ids = lax.all_gather(wanted, "dp").reshape(parts * pair_count)
    got_terms = returned.reshape(parts * pair_count, D // parts, TILE)
    proxy_share = column_sum(got_ids, got_terms, tile_dev).T
    return (loss.reshape(-1), embed_grad.reshape(-1, D), proxy_share)


def solution(mesh):
    placed = (
        P(("dp", "cls"), None),
        P("cls", None),
        P(("dp", "cls"), None),
        P(("dp", "cls")),
        P(("dp", "cls")),
    )
    return jax.shard_map(
        per_device,
        mesh=mesh,
        in_specs=placed,
        out_specs=(P(("dp", "cls")), P(("dp", "cls"), None), P("cls", "dp")),
        check_vma=False,
    )
```
